32 devices in a mesh: gx: 4 (over z), gy: 4 (over y, x), gz: 2 (over core).
Axes of the slice: x: 2, y: 2, z: 4, core: 2. Of those that a mesh axis runs over, the one named last changes fastest.
Arguments:
- rock_ids: int32 [16, 512, 512], P('gz', 'gx', 'gy'), may hold values from 0 to 7
- log_perm: float32 [16, 512, 512], P('gz', 'gx', 'gy'), may hold values from -3 to 3
- rock_diagonal: float32 [8, 3], replicated, may hold values from 0.2 to 5
- rock_shear: float32 [8, 3], replicated, may hold values from -0.8 to 0.8
- rock_storage: float32 [8], replicated, may hold values from 0.05 to 0.5
- source: float32 [16, 512, 512], P('gz', 'gx', 'gy'), may hold values from -6 to 6
- pressure_start: float32 [16, 512, 512], P('gz', 'gx', 'gy'), may hold values from -6 to 6
Outputs:
- pressure: float32 [16, 512, 512], P('gz', 'gx', 'gy')
- residual: float32 [16, 512, 512], P('gz', 'gx', 'gy')
The draws below stay inside these ranges and needn't reach their ends.
All inputs are finite; a program needn't handle non-finite values.
Results may differ from the reference program's by a relative error of at most 0.0003.
Values sent between devices are 32-bit elements; how exact they have to be, the bound alone decides.
A program may use at most 128 MiB of HBM per device.

```python
import math
import jax
import jax.numpy as jnp
from jax import lax

CZ = 8
CX = 128
CY = 128
CLASSES = 8
ITERS = 2
SWEEPS = 2
NZ = 16
NX = 512
NY = 512
N_GX = 4
N_GY = 4
N_GZ = 2


def place_ends(result, key, smallest, largest):
    index_at = [jax.random.randint(jax.random.fold_in(key, axis), (), 0, length) for axis, length in enumerate(result.shape)]
    widest = result.shape.index(max(result.shape))
    next_to = index_at[:widest] + [(index_at[widest] + 1) % result.shape[widest]] + index_at[widest + 1:]
    return result.at[tuple(index_at)].set(smallest).at[tuple(next_to)].set(largest)


def block_scale(rng, shape, pieces, low, top_value):
    factor_of = 1.0
    for dim, shards_of in pieces:
        steps = jax.random.uniform(jax.random.fold_in(jax.random.fold_in(rng, 6), dim), (shards_of,), jnp.float32, low / len(pieces), top_value / len(pieces))
        factor_of = factor_of * jnp.repeat(jnp.exp(steps), shape[dim] // shards_of).reshape((-1,) + (1,) * (len(shape) - 1 - dim))
    return factor_of


def centred(stream_key, extent, width, most, shards=(), held_as=jnp.bfloat16):
    gain = block_scale(stream_key, extent, shards, -0.22, 0.18) if shards else 1.0
    array = jax.random.normal(stream_key, extent, jnp.float32) * width * gain
    return jnp.minimum(jnp.maximum(array, -most), most).astype(held_as)


def setup_inputs(seed: int = 0) -> dict:
    streams_of = jax.random.split(jax.random.key(seed), 8)
    rock_ids = place_ends(jax.random.randint(streams_of[0], (NZ, NX, NY), 0, CLASSES), jax.random.fold_in(streams_of[0], 1), 0, CLASSES - 1).astype(jnp.int32)
    log_perm = centred(streams_of[1], (NZ, NX, NY), 1.0, 3.0, ((0, 2), (1, 4), (2, 4)), jnp.float32)
    rock_diagonal = jnp.clip(jnp.exp(jax.random.uniform(streams_of[2], (CLASSES, 3), jnp.float32, math.log(0.2), math.log(5.0))), 0.2, 5.0)
    rock_shear = jnp.clip(jax.random.uniform(streams_of[3], (CLASSES, 3), jnp.float32, -0.8, 0.8), -0.8, 0.8)
    rock_storage = jnp.clip(jnp.exp(jax.random.uniform(streams_of[4], (CLASSES,), jnp.float32, math.log(0.05), math.log(0.5))), 0.05, 0.5)
    source = centred(streams_of[5], (NZ, NX, NY), 1.0, 6.0, ((0, 2), (1, 4), (2, 4)), jnp.float32)
    pressure_start = centred(streams_of[6], (NZ, NX, NY), 1.0, 6.0, ((0, 2), (1, 4), (2, 4)), jnp.float32)
    return dict(rock_ids=rock_ids, log_perm=log_perm, rock_diagonal=rock_diagonal, rock_shear=rock_shear, rock_storage=rock_storage, source=source, pressure_start=pressure_start)


ROBIN = 0.5

def build_offsets():
    found = []
    for axis in range(3):
        for sign in (1, -1):
            vector = [0, 0, 0]
            vector[axis] = sign
            found.append((tuple(vector), axis, 1))
    for first, second, comp in ((0, 1, 3), (0, 2, 4), (1, 2, 5)):
        for sign_a in (1, -1):
            for sign_b in (1, -1):
                vector = [0, 0, 0]
                vector[first] = sign_a
                vector[second] = sign_b
                found.append((tuple(vector), comp, sign_a * sign_b))
    return found

def class_tables(rock_diagonal, rock_shear):
    col_z = rock_diagonal[:, 0]
    col_x = rock_diagonal[:, 1]
    col_y = rock_diagonal[:, 2]
    cross = jnp.sqrt(jnp.stack([col_z * col_x, col_z * col_y, col_x * col_y], axis=1))
    return jnp.concatenate([rock_diagonal, rock_shear * cross], axis=1)

def tensor_parts(ids, log_perm, table):
    parts = jnp.zeros((6,) + ids.shape, jnp.float32)
    zero = jnp.zeros((), jnp.float32)
    for klass in range(table.shape[0]):
        hit = (ids == klass)[None]
        parts = parts + jnp.where(hit, table[klass][:, None, None, None], zero)
    return parts * jnp.exp(log_perm)[None]

def class_value(ids, values):
    found = jnp.zeros(ids.shape, jnp.float32)
    for klass in range(values.shape[0]):
        found = jnp.where(ids == klass, values[klass], found)
    return found

def shifted(padded, vector):
    depth = padded.shape[-3] - 2
    rows = padded.shape[-2] - 2
    cols = padded.shape[-1] - 2
    return padded[..., 1 + vector[0]:1 + vector[0] + depth, 1 + vector[1]:1 + vector[1] + rows, 1 + vector[2]:1 + vector[2] + cols]

def border_masks(shape):
    masks = []
    for vector, comp, sign in build_offsets():
        mask = jnp.zeros(shape, bool)
        for axis in range(3):
            count = shape[axis]
            dims = [1, 1, 1]
            dims[axis] = count
            index = jnp.arange(count, dtype=jnp.int32).reshape(dims)
            if vector[axis] == 1:
                mask = mask | (index == count - 1)
            elif vector[axis] == -1:
                mask = mask | (index == 0)
        masks.append(mask)
    return masks

def prepare(kpad, storage):
    center = kpad[:, 1:-1, 1:-1, 1:-1]
    coefs = []
    for vector, comp, sign in build_offsets():
        near = shifted(kpad[comp], vector)
        if comp < 3:
            coef = 2.0 * center[comp] * near / (center[comp] + near)
        else:
            coef = 0.125 * sign * (center[comp] + near)
        coefs.append(coef)
    masks = border_masks(storage.shape)
    diag = storage
    robin = jnp.zeros(storage.shape, jnp.float32)
    for coef, mask in zip(coefs, masks):
        size = jnp.abs(coef)
        diag = diag + size
        robin = robin + jnp.where(mask, size, jnp.zeros((), jnp.float32))
    return (coefs, diag, ROBIN * robin)

def block_solve(coefs, diag, robin, source, ppad):
    old = ppad[1:-1, 1:-1, 1:-1]
    solution = old
    for sweep in range(SWEEPS):
        full = ppad.at[1:-1, 1:-1, 1:-1].set(solution)
        total = source + robin * old
        for coef, (vector, comp, sign) in zip(coefs, build_offsets()):
            total = total + coef * shifted(full, vector)
        solution = total / (diag + robin)
    return solution

def block_residual(coefs, diag, source, ppad):
    applied = diag * ppad[1:-1, 1:-1, 1:-1]
    for coef, (vector, comp, sign) in zip(coefs, build_offsets()):
        applied = applied - coef * shifted(ppad, vector)
    return source - applied

def reference(rock_ids, log_perm, rock_diagonal, rock_shear, rock_storage, source, pressure_start):
    table = class_tables(rock_diagonal, rock_shear)
    ids_pad = jnp.pad(rock_ids, 1, constant_values=-1)
    perm_pad = jnp.pad(log_perm, 1)
    nblocks = N_GZ * N_GX * N_GY

    def corner(block):
        zero_z = block // (N_GX * N_GY) * CZ
        zero_x = block // N_GY % N_GX * CX
        zero_y = block % N_GY * CY
        return (zero_z.astype(jnp.int32), zero_x.astype(jnp.int32), zero_y.astype(jnp.int32))

    def sweep_all(current, final):
        ppad = jnp.pad(current, 1)

        def one(block):
            starts = corner(block)
            ids_block = lax.dynamic_slice(ids_pad, starts, (CZ + 2, CX + 2, CY + 2))
            perm_block = lax.dynamic_slice(perm_pad, starts, (CZ + 2, CX + 2, CY + 2))
            kpad = tensor_parts(ids_block, perm_block, table)
            storage = class_value(ids_block[1:-1, 1:-1, 1:-1], rock_storage)
            coefs, diag, robin = prepare(kpad, storage)
            src = lax.dynamic_slice(source, starts, (CZ, CX, CY))
            pblock = lax.dynamic_slice(ppad, starts, (CZ + 2, CX + 2, CY + 2))
            if final:
                return block_residual(coefs, diag, src, pblock)
            return block_solve(coefs, diag, robin, src, pblock)
        blocks = lax.map(one, jnp.arange(nblocks, dtype=jnp.int32))
        blocks = blocks.reshape(N_GZ, N_GX, N_GY, CZ, CX, CY).transpose(0, 3, 1, 4, 2, 5)
        return blocks.reshape(N_GZ * CZ, N_GX * CX, N_GY * CY)
    pressure = pressure_start
    for step in range(ITERS):
        pressure = sweep_all(pressure, False)
    residual = sweep_all(pressure, True)
    return (pressure, residual)
```

```python
import itertools

import jax
import jax.numpy as jnp
from jax import lax
from jax.experimental import pallas as pl
from jax.experimental.pallas import tpu as pltpu
from jax.sharding import PartitionSpec as P

ITERS = 2
SWEEPS = 2
ROBIN = 0.5
AXES = ("gz", "gx", "gy")
LANES = 128


def build_offsets():
    found = []
    for axis in range(3):
        for sign in (1, -1):
            vector = [0, 0, 0]
            vector[axis] = sign
            found.append((tuple(vector), axis, 1))
    for first, second, comp in ((0, 1, 3), (0, 2, 4), (1, 2, 5)):
        for sign_a in (1, -1):
            for sign_b in (1, -1):
                vector = [0, 0, 0]
                vector[first] = sign_a
                vector[second] = sign_b
                found.append((tuple(vector), comp, sign_a * sign_b))
    return found


OFFSETS = build_offsets()
DIRS = [vector for vector, comp, sign in OFFSETS]
SLOT = {vector: index for index, vector in enumerate(DIRS)}
X_DIRS = [d for d in DIRS if d[1] != 0]
Y_DIRS = [d for d in DIRS if d[1] == 0 and d[2] != 0]
Z_DIRS = [d for d in DIRS if d[1] == 0 and d[2] == 0]
X_SLOT = {d: i for i, d in enumerate(X_DIRS)}
Y_SLOT = {d: i for i, d in enumerate(Y_DIRS)}
Z_SLOT = {d: i for i, d in enumerate(Z_DIRS)}
X_FIRST = sorted(X_DIRS, key=lambda d: -abs(d[2]))
YZ_DIRS = Y_DIRS + Z_DIRS


def make_kernel(sizes, shape, classes):
    cz, cx, cy = shape
    tiles = cx // 8
    top = cx + 8
    last = cz - 1

    def kernel(
        ids_hbm, lp_hbm, dia_ref, she_ref, sto_ref, src_hbm, p_hbm,
        out_hbm, res_hbm,
        tab, ten, ten_p, ten_m,
        va, vap, vam, vb, vbp, vbm,
        coef, diag, robin, inv, base, part, pack, zpad,
        rcx, rcy, rcz,
        zs1, xs1, ys1, zl1, xl1, yl1,
        zs2, xs2, ys2, zl2, xl2, yl2,
        zs3, xs3, ys3, zl3, xl3, yl3,
        ids_ref, lp_ref, src_ref, p_ref, res_ref, load_sem,
        send_sem, recv_sem,
    ):
        loads = [
            pltpu.make_async_copy(a, b, load_sem.at[i])
            for i, (a, b) in enumerate(
                ((ids_hbm, ids_ref), (lp_hbm, lp_ref), (p_hbm, p_ref), (src_hbm, src_ref))
            )
        ]
        for load in loads:
            load.start()
        here = [lax.axis_index(a) for a in AXES]

        def exists(d):
            ok = None
            for axis in range(3):
                if d[axis] == 1:
                    term = here[axis] < sizes[axis] - 1
                elif d[axis] == -1:
                    term = here[axis] > 0
                else:
                    continue
                ok = term if ok is None else jnp.logical_and(ok, term)
            return ok

        def target(d):
            return {a: here[i] + d[i] for i, a in enumerate(AXES) if d[i] != 0}

        there = {d: exists(d) for d in DIRS}
        barrier = pltpu.get_barrier_semaphore()

        for ref in (zl1, xl1, yl1, zl2, xl2, yl2, zl3, xl3, yl3):
            ref[...] = jnp.zeros_like(ref)

        expected = jnp.int32(0)
        for d in DIRS:
            @pl.when(there[d])
            def _(d=d):
                pl.semaphore_signal(
                    barrier, inc=1, device_id=target(d),
                    device_id_type=pl.DeviceIdType.MESH,
                )
            expected = expected + there[d].astype(jnp.int32)

        stages = (
            (zs1, xs1, ys1, zl1, xl1, yl1),
            (zs2, xs2, ys2, zl2, xl2, yl2),
            (zs3, xs3, ys3, zl3, xl3, yl3),
        )

        lane = lax.broadcasted_iota(jnp.int32, (cx, LANES), 1)

        def pack_faces(stage, q, plane, row):
            zs, xs, ys = stages[stage][:3]
            for side, z in ((0, 0), (1, last)):
                zs[side, q] = plane(z)
            if row is not None:
                for side, x in ((0, 0), (1, cx - 1)):
                    xs[side, q] = row(x)
            mixed = jnp.zeros((cx, LANES), jnp.float32)
            for z in range(cz):
                moved = pltpu.roll(plane(z), 2 * z + 1, 1)
                mixed = jnp.where((lane // 2) == z, moved, mixed)
            ys[q] = mixed.T[: 2 * cz]

        def copy_of(stage, d):
            zs, xs, ys, zl, xl, yl = stages[stage]
            if d[1] != 0:
                src, dst = xs.at[(d[1] + 1) // 2], xl.at[X_SLOT[d]]
            elif d[2] != 0:
                src, dst = ys, yl.at[Y_SLOT[d]]
            else:
                src, dst = zs.at[(d[0] + 1) // 2], zl.at[Z_SLOT[d]]
            return pltpu.make_async_remote_copy(
                src_ref=src, dst_ref=dst,
                send_sem=send_sem.at[stage, SLOT[d]],
                recv_sem=recv_sem.at[stage, SLOT[d]],
                device_id=target(d), device_id_type=pl.DeviceIdType.MESH,
            )

        def opposite(d):
            return tuple(-c for c in d)

        def start(stage, dirs):
            for d in dirs:
                @pl.when(there[d])
                def _(d=d):
                    copy_of(stage, d).start()

        def arrive(stage):
            for d in DIRS:
                @pl.when(there[opposite(d)])
                def _(d=d):
                    copy_of(stage, d).wait_recv()

        def getters(stage, q):
            zl, xl, yl = stages[stage][3:]

            def get_z(sz):
                return zl[Z_SLOT[(-sz, 0, 0)], q]

            def get_x(sx, sz, sy):
                return xl[X_SLOT[(-sz, -sx, -sy)], q]

            def get_y(sy, sz):
                return yl[Y_SLOT[(-sz, 0, -sy)], q]

            return get_z, get_x, get_y

        lane_x = lax.broadcasted_iota(jnp.int32, (cz, LANES), 1)
        sub_x = lax.broadcasted_iota(jnp.int32, (cz, LANES), 0)
        lane_y = lax.broadcasted_iota(jnp.int32, (2 * cz, LANES), 1)
        sub_y = lax.broadcasted_iota(jnp.int32, (2 * cz, LANES), 0)
        even = sub_y % 2 == 0
        zero = jnp.float32(0)

        def turn(value):
            axis = value.ndim - 1
            return pltpu.roll(value, LANES - 1, axis), pltpu.roll(value, 1, axis)

        def near_x(get, sx, kinds):
            get_x = get[1]
            plain = get_x(sx, 0, 0)
            out = [plain]
            if "z" in kinds:
                out.append(jnp.where(sub_x < last, pltpu.roll(plain, cz - 1, 0), zero))
                out.append(jnp.where(sub_x > 0, pltpu.roll(plain, 1, 0), zero))
            if "y" in kinds:
                side = jnp.where(lane_x >= LANES // 2, get_x(sx, 0, -1), get_x(sx, 0, 1))
                out.append(pltpu.roll(jnp.where(lane_x == 0, side, plain), LANES - 1, 1))
                out.append(pltpu.roll(jnp.where(lane_x == LANES - 1, side, plain), 1, 1))
            return out

        def near_y(get, kinds):
            get_y = get[2]
            plain = jnp.where(
                even,
                pltpu.roll(get_y(1, 0), 2 * cz - 1, 0),
                pltpu.roll(get_y(-1, 0), 1, 0),
            )
            out = [plain]
            if "z" in kinds:
                out.append(jnp.where(sub_y < 2 * last, pltpu.roll(plain, 2 * cz - 2, 0), zero))
                out.append(jnp.where(sub_y >= 2, pltpu.roll(plain, 2, 0), zero))
            if "x" in kinds:
                ahead, behind = turn(plain)
                out.append(jnp.where(lane_y < LANES - 1, ahead, zero))
                out.append(jnp.where(lane_y > 0, behind, zero))
            return out

        def pack_sides(get):
            get_y = get[2]
            pack[2 * cz : 4 * cz, :] = jnp.where(even, get_y(-1, -1), get_y(1, -1))
            pack[4 * cz : 6 * cz, :] = jnp.where(even, get_y(-1, 1), get_y(1, 1))

        def near_z(get, sz, kinds, turned):
            get_z, get_x, get_y = get
            plain = get_z(sz)
            out = [plain]
            row = last if sz == -1 else 0
            if "x" in kinds:
                zpad[8:top, :] = plain
                zpad[7:8, :] = get_x(-1, sz, 0)[row : row + 1]
                zpad[top : top + 1, :] = get_x(1, sz, 0)[row : row + 1]
                out.append(zpad[9 : top + 1, :])
                out.append(zpad[7 : top - 1, :])
            if "y" in kinds:
                first = 4 * cz - 2 if sz == -1 else 4 * cz
                side = pltpu.roll(turned, LANES - 1 - first, 1)
                out.append(pltpu.roll(jnp.where(lane == 0, side, plain), LANES - 1, 1))
                out.append(pltpu.roll(jnp.where(lane == LANES - 1, side, plain), 1, 1))
            return out

        def harmonic(own, near):
            return 2.0 * own * near / (own + near)

        ends = jnp.logical_or(lane == 0, lane == LANES - 1)

        def spread(dest, add, turned, of_x, of_z):
            for z in range(cz):
                got = jnp.where(ends, pltpu.roll(turned, LANES - 1 - 2 * z, 1), zero)
                if z == 0:
                    got = got + of_z(-1)
                if z == last:
                    got = got + of_z(1)
                if add:
                    dest[z] += got
                else:
                    dest[z] = got
            for sx, row in ((-1, 0), (1, cx - 1)):
                dest[:, row, :] += of_x(sx)

        for load in loads[:3]:
            load.wait()

        pack_faces(
            0, 0,
            lambda z: (ids_ref[z] + 1).astype(jnp.float32),
            lambda x: (ids_ref[:, x, :] + 1).astype(jnp.float32),
        )
        pack_faces(0, 1, lambda z: lp_ref[z], lambda x: lp_ref[:, x, :])
        pack_faces(0, 2, lambda z: p_ref[z], lambda x: p_ref[:, x, :])

        for c in range(classes):
            cols = [jnp.full((8, LANES), dia_ref[k, c], jnp.float32) for k in range(3)]
            for k in range(3):
                tab[k, c] = cols[k]
            for k, (a, b) in enumerate(((0, 1), (0, 2), (1, 2))):
                tab[3 + k, c] = she_ref[k, c] * jnp.sqrt(cols[a] * cols[b])
            tab[6, c] = jnp.full((8, LANES), sto_ref[c], jnp.float32)

        pack[...] = jnp.zeros_like(pack)
        for ref in (va, vap, vam, vb, vbp, vbm):
            for z in (0, cz + 1):
                ref[z] = jnp.zeros_like(ref[z])
            for lo in (0, top):
                ref[:, lo : lo + 8, :] = jnp.zeros((cz + 2, 8, LANES), jnp.float32)

        def rows_of(t):
            return pl.ds(pl.multiple_of(t * 8, 8), 8)

        def lookup(code, comps):
            found = [jnp.zeros(code.shape, jnp.float32) for _ in comps]
            for c in range(classes):
                hit = code == jnp.float32(c + 1)
                found = [
                    jnp.where(hit, jnp.broadcast_to(tab[k, c, 0:1, :], code.shape), f)
                    for k, f in zip(comps, found)
                ]
            return found

        def tensor_tile(t, carry):
            r = rows_of(t)
            out = rows_of(t + 1)
            code = (ids_ref[:, r, :] + 1).astype(jnp.float32)
            gain = jnp.exp(lp_ref[:, r, :])
            found = lookup(code, range(7))
            for k in range(6):
                value = found[k] * gain
                ten[k, 1 : cz + 1, out, :] = value
                if k in (2, 4, 5):
                    slot = (2, 4, 5).index(k)
                    ahead, behind = turn(value)
                    ten_p[slot, 1 : cz + 1, out, :] = ahead
                    ten_m[slot, 1 : cz + 1, out, :] = behind
            diag[:, r, :] = found[6]
            value = p_ref[:, r, :]
            ahead, behind = turn(value)
            va[1 : cz + 1, out, :] = value
            vap[1 : cz + 1, out, :] = ahead
            vam[1 : cz + 1, out, :] = behind
            return carry

        lax.fori_loop(0, tiles, tensor_tile, 0, unroll=2)

        pl.semaphore_wait(barrier, expected)
        start(0, X_FIRST + YZ_DIRS)

        def near_of(refs, t):
            plain, plus, minus = refs
            by_y = {0: plain, 1: plus, -1: minus}
            cache = {}

            def near(vector):
                dz, dx, dy = vector
                if (dx, dy) not in cache:
                    ref = by_y[dy]
                    r = pl.ds(t * 8 + 8 + dx, 8) if dx else rows_of(t + 1)
                    if dx and dy:
                        cache[(dx, dy)] = ref[1 : cz + 1, r, :]
                    else:
                        cache[(dx, dy)] = ref[:, r, :]
                got = cache[(dx, dy)]
                if dx and dy:
                    return got
                return got[1 + dz : 1 + dz + cz]

            return near

        zi = lax.broadcasted_iota(jnp.int32, (cz, 8, LANES), 0)
        xi = lax.broadcasted_iota(jnp.int32, (cz, 8, LANES), 1)
        yi = lax.broadcasted_iota(jnp.int32, (cz, 8, LANES), 2)

        def coef_tile(t, carry):
            r = rows_of(t)
            mid = rows_of(t + 1)
            at = (zi, xi + t * 8, yi)
            total = diag[:, r, :]
            nears = {
                0: near_of((ten.at[0], None, None), t),
                1: near_of((ten.at[1], None, None), t),
                2: near_of((ten.at[2], ten_p.at[0], ten_m.at[0]), t),
                3: near_of((ten.at[3], None, None), t),
                4: near_of((ten.at[4], ten_p.at[1], ten_m.at[1]), t),
                5: near_of((ten.at[5], ten_p.at[2], ten_m.at[2]), t),
            }
            for e, (vector, comp, sign) in enumerate(OFFSETS):
                own = ten[comp, 1 : cz + 1, mid, :]
                near = nears[comp](vector)
                if comp < 3:
                    value = harmonic(own, near)
                else:
                    value = 0.125 * sign * (own + near)
                out = None
                for axis in range(3):
                    if vector[axis] == 0:
                        continue
                    edge = shape[axis] - 1 if vector[axis] == 1 else 0
                    hit = at[axis] == edge
                    out = hit if out is None else jnp.logical_or(out, hit)
                value = jnp.where(out, zero, value)
                coef[e, :, r, :] = value
                total = total + jnp.abs(value)
            diag[:, r, :] = total
            return carry

        lax.fori_loop(0, tiles, coef_tile, 0)

        def gather(refs, t, acc):
            near = near_of(refs, t)
            r = rows_of(t)
            for e, (vector, comp, sign) in enumerate(OFFSETS):
                acc = acc + coef[e, :, r, :] * near(vector)
            return acc

        a_refs = (va, vap, vam)
        b_refs = (vb, vbp, vbm)

        loads[3].wait()

        def inside_tile(t, carry):
            r = rows_of(t)
            part[:, r, :] = gather(a_refs, t, src_ref[:, r, :])
            return carry

        lax.fori_loop(0, tiles, inside_tile, 0, unroll=4)

        arrive(0)

        gid = getters(0, 0)
        glp = getters(0, 1)

        def tensor_get(k):
            def of(which):
                def get(*args):
                    code = gid[which](*args)
                    return lookup(code, [k])[0] * jnp.exp(glp[which](*args))
                return get
            return of(0), of(1), of(2)

        gets = {k: tensor_get(k) for k in range(6)}
        rim_x = {}
        for side, sx in ((0, -1), (1, 1)):
            row = 8 if sx == -1 else top - 1
            own = {k: ten[k, 1 : cz + 1, row, :] for k in (1, 3, 5)}
            values = [harmonic(own[1], near_x(gets[1], sx, "")[0])]
            near = near_x(gets[3], sx, "z")
            for dz, got, ok in ((1, near[1], sub_x < last), (-1, near[2], sub_x > 0)):
                values.append(jnp.where(ok, 0.125 * (dz * sx) * (own[3] + got), zero))
            near = near_x(gets[5], sx, "y")
            for dy, got in ((1, near[1]), (-1, near[2])):
                values.append(0.125 * (sx * dy) * (own[5] + got))
            size = None
            for j, value in enumerate(values):
                rcx[side, j] = value
                size = jnp.abs(value) if size is None else size + jnp.abs(value)
            rim_x[sx] = size

        code = ys1[0]
        gain = jnp.exp(ys1[1])
        own = {k: f * gain for k, f in zip((2, 4, 5), lookup(code, (2, 4, 5)))}
        sy = jnp.where(even, jnp.float32(0.125), jnp.float32(-0.125))
        values = [harmonic(own[2], near_y(gets[2], "")[0])]
        near = near_y(gets[4], "z")
        for dz, got, ok in ((1, near[1], sub_y < 2 * last), (-1, near[2], sub_y >= 2)):
            values.append(jnp.where(ok, dz * sy * (own[4] + got), zero))
        near = near_y(gets[5], "x")
        for dx, got, ok in ((1, near[1], lane_y < LANES - 1), (-1, near[2], lane_y > 0)):
            values.append(jnp.where(ok, dx * sy * (own[5] + got), zero))
        size = None
        for j, value in enumerate(values):
            rcy[j] = value
            size = jnp.abs(value) if size is None else size + jnp.abs(value)
        pack[0 : 2 * cz, :] = size
        pack_sides(gets[4])
        turned = pack[...].T
        rim_z = {}
        for side, sz in ((0, -1), (1, 1)):
            z = 1 if sz == -1 else cz
            own = {k: ten[k, z, 8:top, :] for k in (0, 3, 4)}
            values = [harmonic(own[0], near_z(gets[0], sz, "", None)[0])]
            near = near_z(gets[3], sz, "x", None)
            for dx, got in ((1, near[1]), (-1, near[2])):
                values.append(0.125 * (sz * dx) * (own[3] + got))
            near = near_z(gets[4], sz, "y", turned)
            for dy, got in ((1, near[1]), (-1, near[2])):
                values.append(0.125 * (sz * dy) * (own[4] + got))
            size = None
            for j, value in enumerate(values):
                rcz[side, j] = value
                size = jnp.abs(value) if size is None else size + jnp.abs(value)
            rim_z[sz] = size
        spread(robin, False, turned, lambda sx: rim_x[sx], lambda sz: rim_z[sz])

        def scale_tile(t, carry):
            r = rows_of(t)
            rim = robin[:, r, :]
            total = diag[:, r, :] + rim
            rim = ROBIN * rim
            diag[:, r, :] = total
            robin[:, r, :] = rim
            inv[:, r, :] = 1.0 / (total + rim)
            return carry

        lax.fori_loop(0, tiles, scale_tile, 0, unroll=4)

        def weigh(weights, values):
            out = None
            for j, value in enumerate(values):
                term = weights(j) * value
                out = term if out is None else out + term
            return out

        def spread_pressure(dest, add, stage, q):
            get = getters(stage, q)
            pack[0 : 2 * cz, :] = weigh(lambda j: rcy[j], near_y(get, "zx"))
            pack_sides(get)
            turned = pack[...].T
            spread(
                dest, add, turned,
                lambda sx: weigh(lambda j: rcx[(sx + 1) // 2, j], near_x(get, sx, "zy")),
                lambda sz: weigh(lambda j: rcz[(sz + 1) // 2, j], near_z(get, sz, "xy", turned)),
            )

        def first_tile(t, carry):
            r = rows_of(t)
            mid = rows_of(t + 1)
            fixed = base[:, r, :] + robin[:, r, :] * va[1 : cz + 1, mid, :]
            u = (fixed + part[:, r, :]) * inv[:, r, :]
            base[:, r, :] = fixed + src_ref[:, r, :]
            ahead, behind = turn(u)
            vb[1 : cz + 1, mid, :] = u
            vbp[1 : cz + 1, mid, :] = ahead
            vbm[1 : cz + 1, mid, :] = behind
            return carry

        def second_tile(t, carry):
            r = rows_of(t)
            mid = rows_of(t + 1)
            u = gather(b_refs, t, base[:, r, :]) * inv[:, r, :]
            ahead, behind = turn(u)
            va[1 : cz + 1, mid, :] = u
            vap[1 : cz + 1, mid, :] = ahead
            vam[1 : cz + 1, mid, :] = behind
            return carry

        def residual_tile(t, carry):
            r = rows_of(t)
            value = va[1 : cz + 1, rows_of(t + 1), :]
            applied = src_ref[:, r, :] - diag[:, r, :] * value
            res_ref[:, r, :] = gather(a_refs, t, applied)
            return carry

        for step in range(ITERS):
            spread_pressure(base, False, step, 2 if step == 0 else 0)
            lax.fori_loop(0, tiles, first_tile, 0, unroll=4)
            lax.fori_loop(0, 2, lambda i, c: second_tile(i * (tiles - 1), c), 0, unroll=2)
            for side, x in ((0, 8), (1, top - 1)):
                stages[step + 1][1][side, 0] = va[1 : cz + 1, x, :]
            start(step + 1, X_FIRST)
            lax.fori_loop(1, tiles - 1, second_tile, 0, unroll=2)
            pack_faces(step + 1, 0, lambda z: va[z + 1, 8:top, :], None)
            start(step + 1, YZ_DIRS)
            if step == ITERS - 1:
                put_out = pltpu.make_async_copy(
                    va.at[1 : cz + 1, 8:top, :], out_hbm, load_sem.at[4]
                )
                put_out.start()
            if step == ITERS - 1:
                lax.fori_loop(0, tiles, residual_tile, 0, unroll=4)
            else:
                lax.fori_loop(0, tiles, inside_tile, 0, unroll=4)
            arrive(step + 1)
        spread_pressure(res_ref, True, ITERS, 0)
        put_res = pltpu.make_async_copy(res_ref, res_hbm, load_sem.at[5])
        put_res.start()
        put_out.wait()
        put_res.wait()

        for stage in range(ITERS + 1):
            for d in DIRS:
                @pl.when(there[d])
                def _(d=d, stage=stage):
                    copy_of(stage, d).wait_send()

    return kernel


def solution(mesh):
    sizes = tuple(mesh.shape[a] for a in AXES)

    def per_device(rock_ids, log_perm, rock_diagonal, rock_shear, rock_storage, source, pressure_start):
        shape = rock_ids.shape
        cz, cx, cy = shape
        classes = rock_storage.shape[0]
        f32 = jnp.float32
        padded = (cz + 2, cx + 16, cy)

        def exchange(nq):
            return [
                pltpu.VMEM((2, nq, cx, cy), f32),
                pltpu.VMEM((2, nq, cz, cy), f32),
                pltpu.VMEM((nq, 2 * cz, cx), f32),
                pltpu.VMEM((len(Z_DIRS), nq, cx, cy), f32),
                pltpu.VMEM((len(X_DIRS), nq, cz, cy), f32),
                pltpu.VMEM((len(Y_DIRS), nq, 2 * cz, cx), f32),
            ]

        hbm = pl.BlockSpec(memory_space=pltpu.HBM)
        smem = pl.BlockSpec(memory_space=pltpu.SMEM)
        return pl.pallas_call(
            make_kernel(sizes, shape, classes),
            out_shape=(jax.ShapeDtypeStruct(shape, f32), jax.ShapeDtypeStruct(shape, f32)),
            in_specs=[hbm, hbm, smem, smem, smem, hbm, hbm],
            out_specs=(hbm, hbm),
            scratch_shapes=[
                pltpu.VMEM((7, classes, 8, cy), f32),
                pltpu.VMEM((6,) + padded, f32),
                pltpu.VMEM((3,) + padded, f32),
                pltpu.VMEM((3,) + padded, f32),
            ]
            + [pltpu.VMEM(padded, f32)] * 6
            + [pltpu.VMEM((len(OFFSETS), cz, cx + 8, cy), f32)]
            + [pltpu.VMEM(shape, f32)] * 5
            + [
                pltpu.VMEM((cx, cy), f32),
                pltpu.VMEM((cx + 16, cy), f32),
                pltpu.VMEM((2, 5, cz, cy), f32),
                pltpu.VMEM((5, 2 * cz, cx), f32),
                pltpu.VMEM((2, 5, cx, cy), f32),
            ]
            + exchange(3)
            + exchange(1)
            + exchange(1)
            + [pltpu.VMEM(shape, jnp.int32)]
            + [pltpu.VMEM(shape, f32)] * 4
            + [
                pltpu.SemaphoreType.DMA((6,)),
                pltpu.SemaphoreType.DMA((ITERS + 1, len(DIRS))),
                pltpu.SemaphoreType.DMA((ITERS + 1, len(DIRS))),
            ],
            compiler_params=pltpu.CompilerParams(
                collective_id=0, has_side_effects=True, vmem_limit_bytes=61440 * 1024
            ),
            name="schwarz",
        )(rock_ids, log_perm, rock_diagonal.T, rock_shear.T, rock_storage, source, pressure_start)

    block = P("gz", "gx", "gy")
    return jax.shard_map(
        per_device,
        mesh=mesh,
        in_specs=(block, block, P(), P(), P(), block, block),
        out_specs=(block, block),
        check_vma=False,
    )
```

```python
import jax
import jax.numpy as jnp
from jax import lax
from jax.experimental import pallas as pl
from jax.experimental.pallas import tpu as pltpu
from jax.sharding import PartitionSpec as P

ITERS = 2
SWEEPS = 2
ROBIN = 0.5
AXES = ("gz", "gx", "gy")
LANES = 128
FACE = 2.0
EDGE = 0.125


def build_offsets():
    found = []
    for axis in range(3):
        for sign in (1, -1):
            vector = [0, 0, 0]
            vector[axis] = sign
            found.append((tuple(vector), axis, 1))
    for first, second, comp in ((0, 1, 3), (0, 2, 4), (1, 2, 5)):
        for sign_a in (1, -1):
            for sign_b in (1, -1):
                vector = [0, 0, 0]
                vector[first] = sign_a
                vector[second] = sign_b
                found.append((tuple(vector), comp, sign_a * sign_b))
    return found


OFFSETS = build_offsets()


def z_kinds(blocks):
    if blocks < 2:
        return ()
    return ("other",) if blocks == 2 else (1, -1)


def directions(kinds):
    found = [(0, dx, dy) for dx in (1, -1) for dy in (1, -1)]
    found += [(k + 1, dx, 0) for k in range(len(kinds)) for dx in (1, -1)]
    found += [(0, dx, 0) for dx in (1, -1)]
    x_dirs = found
    y_dirs = [(k + 1, 0, dy) for k in range(len(kinds)) for dy in (1, -1)]
    y_dirs += [(0, 0, dy) for dy in (1, -1)]
    z_dirs = [(k + 1, 0, 0) for k in range(len(kinds))]
    return x_dirs, y_dirs, z_dirs


def make_kernel(sizes, shape, classes):
    cz, cx, cy = shape
    tiles = cx // 8
    top = cx + 8
    last = cz - 1
    kinds = z_kinds(sizes[0])
    x_dirs, y_dirs, z_dirs = directions(kinds)
    dirs = x_dirs + y_dirs + z_dirs
    slot = {d: i for i, d in enumerate(dirs)}
    x_slot = {d: i for i, d in enumerate(x_dirs)}
    y_slot = {d: i for i, d in enumerate(y_dirs)}

    def opposite(d):
        k = d[0]
        if k and len(kinds) == 2:
            k = 3 - k
        return (k, -d[1], -d[2])

    def kernel(
        ids_hbm, lp_hbm, dia_ref, she_ref, sto_ref, src_hbm, p_hbm,
        va, res_ref,
        tab, ten, vb,
        coef, diag, robin, inv, base, part, mixed, pack, turn, zpad,
        rcx, rcy, rcz,
        zs1, xs1, ys1, zl1, xl1, yl1,
        xs2, ys2, zl2, xl2, yl2,
        xs3, ys3, zl3, xl3, yl3,
        ids_ref, lp_ref, src_ref, load_sem,
        send_sem, recv_sem,
    ):
        whole = pl.ds(8, cx)
        loads = [
            pltpu.make_async_copy(a, b, load_sem.at[i])
            for i, (a, b) in enumerate(
                ((ids_hbm, ids_ref), (lp_hbm, lp_ref), (p_hbm, va.at[:, whole, :]), (src_hbm, src_ref))
            )
        ]
        for load in loads:
            load.start()
        here = [lax.axis_index(a) for a in AXES]
        if len(kinds) == 1:
            steps = [(1 - 2 * here[0], last * (1 - here[0]), last * here[0])]
        else:
            steps = [(k, last if k == 1 else 0, 0 if k == 1 else last) for k in kinds]

        ends_z = [(0, last), [s[2] for s in steps], ()][len(kinds)]

        def exists(d):
            ok = None
            terms = []
            if d[0] and len(kinds) == 2:
                terms.append(here[0] < sizes[0] - 1 if kinds[d[0] - 1] == 1 else here[0] > 0)
            for axis in (1, 2):
                if d[axis] == 1:
                    terms.append(here[axis] < sizes[axis] - 1)
                elif d[axis] == -1:
                    terms.append(here[axis] > 0)
            for term in terms:
                ok = term if ok is None else jnp.logical_and(ok, term)
            return ok

        there = {d: exists(d) for d in dirs}

        def when(ok):
            if ok is None:
                return lambda f: f()
            return pl.when(ok)

        def target(d):
            out = {AXES[i]: here[i] + d[i] for i in (1, 2) if d[i] != 0}
            if d[0]:
                out[AXES[0]] = here[0] + steps[d[0] - 1][0]
            return out

        barrier = pltpu.get_barrier_semaphore()

        for ref in (zl1, xl1, yl1, zl2, xl2, yl2, zl3, xl3, yl3):
            ref[...] = jnp.zeros_like(ref)

        expected = jnp.int32(0)
        for d in dirs:
            @when(there[d])
            def _(d=d):
                pl.semaphore_signal(
                    barrier, inc=1, device_id=target(d),
                    device_id_type=pl.DeviceIdType.MESH,
                )
            expected = expected + (1 if there[d] is None else there[d].astype(jnp.int32))

        stages = (
            (None, xs1, ys1, zl1, xl1, yl1),
            (None, xs2, ys2, zl2, xl2, yl2),
            (None, xs3, ys3, zl3, xl3, yl3),
        )

        lane = lax.broadcasted_iota(jnp.int32, (cx, LANES), 1)
        lane_t = lax.broadcasted_iota(jnp.int32, (8, LANES), 1)

        def copy_of(stage, d):
            zs, xs, ys, zl, xl, yl = stages[stage]
            if d[1] != 0:
                src, dst = xs.at[(d[1] + 1) // 2], xl.at[x_slot[d]]
            elif d[2] != 0:
                src, dst = ys, yl.at[y_slot[d]]
            else:
                k = d[0] - 1
                src = zs1.at[k] if stage == 0 else va.at[pl.ds(steps[k][1], 1), whole, :]
                dst = zl.at[k]
            return pltpu.make_async_remote_copy(
                src_ref=src, dst_ref=dst,
                send_sem=send_sem.at[stage, slot[d]],
                recv_sem=recv_sem.at[stage, slot[d]],
                device_id=target(d), device_id_type=pl.DeviceIdType.MESH,
            )

        def start(stage, some):
            for d in some:
                @when(there[d])
                def _(d=d):
                    copy_of(stage, d).start()

        def arrive(stage, some):
            for d in some:
                @when(there[opposite(d)])
                def _(d=d):
                    copy_of(stage, d).wait_recv()

        def sent(stage):
            for d in dirs:
                @when(there[d])
                def _(d=d):
                    copy_of(stage, d).wait_send()

        def getters(stage, q):
            zl, xl, yl = stages[stage][3:]

            def get_z(k):
                return zl[opposite((k + 1, 0, 0))[0] - 1, q]

            def get_x(sx, sy):
                return xl[x_slot[(0, -sx, -sy)], q]

            def get_y(sy):
                return yl[y_slot[(0, 0, -sy)], q]

            def get_zx(k, sx):
                return xl[x_slot[opposite((k + 1, sx, 0))], q, pl.ds(steps[k][2], 1), :]

            def get_zy(k, sy):
                return yl[y_slot[opposite((k + 1, 0, sy))], q, pl.ds(2 * steps[k][2], 2), :]

            return get_z, get_x, get_y, get_zx, get_zy

        lane_x = lax.broadcasted_iota(jnp.int32, (cz, LANES), 1)
        sub_x = lax.broadcasted_iota(jnp.int32, (cz, LANES), 0)
        lane_y = lax.broadcasted_iota(jnp.int32, (2 * cz, LANES), 1)
        sub_y = lax.broadcasted_iota(jnp.int32, (2 * cz, LANES), 0)
        even = sub_y % 2 == 0
        zero = jnp.float32(0)

        def near_x(get, sx, names):
            get_x = get[1]
            plain = get_x(sx, 0)
            out = [plain]
            if "z" in names:
                out.append(jnp.where(sub_x < last, pltpu.roll(plain, cz - 1, 0), zero))
                out.append(jnp.where(sub_x > 0, pltpu.roll(plain, 1, 0), zero))
            if "y" in names:
                side = jnp.where(lane_x >= LANES // 2, get_x(sx, -1), get_x(sx, 1))
                out.append(pltpu.roll(jnp.where(lane_x == 0, side, plain), LANES - 1, 1))
                out.append(pltpu.roll(jnp.where(lane_x == LANES - 1, side, plain), 1, 1))
            return out

        def near_y(get, names):
            get_y = get[2]
            plain = jnp.where(
                even,
                pltpu.roll(get_y(1), 2 * cz - 1, 0),
                pltpu.roll(get_y(-1), 1, 0),
            )
            out = [plain]
            if "z" in names:
                out.append(jnp.where(sub_y < 2 * last, pltpu.roll(plain, 2 * cz - 2, 0), zero))
                out.append(jnp.where(sub_y >= 2, pltpu.roll(plain, 2, 0), zero))
            if "x" in names:
                ahead, behind = pltpu.roll(plain, LANES - 1, 1), pltpu.roll(plain, 1, 1)
                out.append(jnp.where(lane_y < LANES - 1, ahead, zero))
                out.append(jnp.where(lane_y > 0, behind, zero))
            return out

        even_two = lax.broadcasted_iota(jnp.int32, (2, LANES), 0) == 0

        def pack_sides(get):
            get_zy = get[4]
            for k in range(len(kinds)):
                at = 2 * cz + 2 * k
                pack[at : at + 2, :] = jnp.where(even_two, get_zy(k, -1), get_zy(k, 1))

        def near_z(get, k, names, turned):
            get_z, get_zx = get[0], get[3]
            plain = get_z(k)
            out = [plain]
            if "x" in names:
                zpad[8:top, :] = plain
                zpad[7:8, :] = get_zx(k, -1)
                zpad[top : top + 1, :] = get_zx(k, 1)
                out.append(zpad[9 : top + 1, :])
                out.append(zpad[7 : top - 1, :])
            if "y" in names:
                side = pltpu.roll(turned, LANES - 1 - (2 * cz + 2 * k), 1)
                out.append(pltpu.roll(jnp.where(lane == 0, side, plain), LANES - 1, 1))
                out.append(pltpu.roll(jnp.where(lane == LANES - 1, side, plain), 1, 1))
            return out

        def harmonic(own, near):
            return own * near / (own + near)

        def rows_of(t):
            return pl.ds(pl.multiple_of(t * 8, 8), 8)

        ends = jnp.logical_or(lane_t == 0, lane_t == LANES - 1)

        def at_ends(ref, r, z):
            return jnp.where(ends, pltpu.roll(ref[r, :], LANES - 1 - 2 * z, 1), zero)

        def add_xz(dest, of_x, of_z):
            for k in range(len(kinds)):
                dest[pl.ds(steps[k][1], 1)] += of_z(k)[None]
            for sx, row in ((-1, 0), (1, cx - 1)):
                dest[:, row, :] += of_x(sx)

        def mix(planes):
            out = None
            for z in range(cz):
                moved = pltpu.roll(planes[z], 2 * z + 1, 1)
                out = moved if out is None else jnp.where((lane_t // 2) == z, moved, out)
            return out

        scale_of = (FACE, FACE, FACE, EDGE, EDGE, EDGE)
        for c in range(classes):
            cols = [jnp.full((8, LANES), dia_ref[k, c], jnp.float32) for k in range(3)]
            for k in range(3):
                tab[k, c] = cols[k] * scale_of[k]
            for k, (a, b) in enumerate(((0, 1), (0, 2), (1, 2))):
                tab[3 + k, c] = scale_of[3 + k] * she_ref[k, c] * jnp.sqrt(cols[a] * cols[b])
            tab[6, c] = jnp.full((8, LANES), sto_ref[c], jnp.float32)

        pack[...] = jnp.zeros_like(pack)
        for ref in (va, vb):
            for lo in (0, top):
                ref[:, lo : lo + 8, :] = jnp.zeros((cz, 8, LANES), jnp.float32)
        for lo in (0, top):
            ten[:, :, lo : lo + 8, :] = jnp.zeros((6, cz, 8, LANES), jnp.float32)

        def code_of(ids):
            return (ids + 1).astype(jnp.float32)

        for load in loads[:3]:
            load.wait()

        for k in range(len(kinds)):
            face = pl.ds(steps[k][1], 1)
            zs1[k, 0:1] = code_of(ids_ref[face])
            zs1[k, 1:2] = lp_ref[face]
            zs1[k, 2:3] = va[face, whole, :]
        for side, x in ((0, 0), (1, cx - 1)):
            xs1[side, 0] = code_of(ids_ref[:, x, :])
            xs1[side, 1] = lp_ref[:, x, :]
            xs1[side, 2] = va[:, 8 + x, :]

        def mix_tile(t, carry):
            r = rows_of(t)
            mixed[0, r, :] = mix(code_of(ids_ref[:, r, :]))
            mixed[1, r, :] = mix(lp_ref[:, r, :])
            mixed[2, r, :] = mix(va[:, rows_of(t + 1), :])
            return carry

        lax.fori_loop(0, tiles, mix_tile, 0, unroll=2)
        for q in range(3):
            ys1[q] = mixed[q].T[: 2 * cz]

        pl.semaphore_wait(barrier, expected)
        start(0, dirs)

        def lookup(code, comps):
            found = [jnp.zeros(code.shape, jnp.float32) for _ in comps]
            for c in range(classes):
                hit = code == jnp.float32(c + 1)
                found = [
                    jnp.where(hit, jnp.broadcast_to(tab[k, c, 0:1, :], code.shape), f)
                    for k, f in zip(comps, found)
                ]
            return found

        def tensor_tile(t, carry):
            r = rows_of(t)
            out = rows_of(t + 1)
            gain = jnp.exp(lp_ref[:, r, :])
            found = lookup(code_of(ids_ref[:, r, :]), range(7))
            for k in range(6):
                ten[k, :, out, :] = found[k] * gain
            diag[:, r, :] = found[6]
            return carry

        lax.fori_loop(0, tiles, tensor_tile, 0, unroll=2)

        row_t = lax.broadcasted_iota(jnp.int32, (8, LANES), 0)

        def coef_tile(t, carry):
            r = rows_of(t)
            mid = rows_of(t + 1)
            row = {0: mid, 1: pl.ds(t * 8 + 9, 8), -1: pl.ds(t * 8 + 7, 8)}
            x_out = {1: row_t + t * 8 == cx - 1, -1: row_t + t * 8 == 0}
            y_out = {1: lane_t == 0, -1: lane_t == LANES - 1}
            xy_out = {(dx, dy): jnp.logical_or(x_out[dx], y_out[dy]) for dx in (1, -1) for dy in (1, -1)}
            for z in range(cz):
                own = {}
                for comp in range(6):
                    value = ten[comp, z, mid, :]
                    own[comp, 0] = value
                    if comp in (2, 4, 5):
                        own[comp, 1] = pltpu.roll(value, 1, 1)
                        own[comp, -1] = pltpu.roll(value, LANES - 1, 1)
                total = {0: diag[z, r, :], 1: None, -1: None}
                for e, ((dz, dx, dy), comp, sign) in enumerate(OFFSETS):
                    if not 0 <= z + dz < cz:
                        continue
                    near = ten[comp, z + dz, row[dx], :]
                    if comp < 3:
                        value = harmonic(own[comp, dy], near)
                    else:
                        value = own[comp, dy] + near
                    if dx and dy:
                        value = jnp.where(xy_out[dx, dy], zero, value)
                    elif dx and dz:
                        value = jnp.where(x_out[dx], zero, value)
                    elif dy:
                        value = jnp.where(y_out[dy], zero, value)
                    coef[e, z, r, :] = value
                    size = value if comp < 3 else jnp.abs(value)
                    total[dy] = size if total[dy] is None else total[dy] + size
                diag[z, r, :] = total[0] + pltpu.roll(total[1], LANES - 1, 1) + pltpu.roll(total[-1], 1, 1)
                robin[z, r, :] = jnp.zeros((8, LANES), jnp.float32)
            return carry

        lax.fori_loop(0, tiles, coef_tile, 0, unroll=2)

        def gather(ref, t, first):
            r = rows_of(t)
            row = {0: rows_of(t + 1), 1: pl.ds(t * 8 + 9, 8), -1: pl.ds(t * 8 + 7, 8)}
            near = {dx: ref[:, row[dx], :] for dx in (0, 1, -1)}
            out = []
            for z in range(cz):
                acc = {0: first(z), 1: None, -1: None}
                for e, ((dz, dx, dy), comp, sign) in enumerate(OFFSETS):
                    if not 0 <= z + dz < cz:
                        continue
                    term = coef[e, z, r, :] * near[dx][z + dz]
                    if acc[dy] is None:
                        acc[dy] = term if sign == 1 else -term
                    else:
                        acc[dy] = acc[dy] + term if sign == 1 else acc[dy] - term
                out.append(acc[0] + (pltpu.roll(acc[1], LANES - 1, 1) + pltpu.roll(acc[-1], 1, 1)))
            return out

        for plane in ends_z:
            own = [jnp.abs(ten[c, pl.ds(plane, 1), 8:top, :]) for c in (3, 4)]
            robin[pl.ds(plane, 1)] += 2.0 * (own[0] + own[1])

        loads[3].wait()

        def inside_tile(t, carry):
            r = rows_of(t)
            for z, value in enumerate(gather(va, t, lambda z: None)):
                part[z, r, :] = value
            base[:, r, :] = src_ref[:, r, :]
            return carry

        lax.fori_loop(0, tiles, inside_tile, 0, unroll=4)

        arrive(0, dirs)

        gid = getters(0, 0)
        glp = getters(0, 1)

        def tensor_get(k):
            def of(which):
                def get(*args):
                    code = gid[which](*args)
                    return lookup(code, [k])[0] * jnp.exp(glp[which](*args))
                return get
            return tuple(of(i) for i in range(5))

        gets = {k: tensor_get(k) for k in range(6)}
        rim_x = {}
        for side, sx in ((0, -1), (1, 1)):
            row = 8 if sx == -1 else top - 1
            own = {k: ten[k, :, row, :] for k in (1, 3, 5)}
            values = [harmonic(own[1], near_x(gets[1], sx, "")[0])]
            near = near_x(gets[3], sx, "z")
            for dz, got, ok in ((1, near[1], sub_x < last), (-1, near[2], sub_x > 0)):
                values.append(jnp.where(ok, (dz * sx) * (own[3] + got), zero))
            near = near_x(gets[5], sx, "y")
            for dy, got in ((1, near[1]), (-1, near[2])):
                values.append((sx * dy) * (own[5] + got))
            size = None
            for j, value in enumerate(values):
                rcx[side, j] = value
                size = jnp.abs(value) if size is None else size + jnp.abs(value)
            rim_x[sx] = size

        code = ys1[0]
        gain = jnp.exp(ys1[1])
        own = {k: f * gain for k, f in zip((2, 4, 5), lookup(code, (2, 4, 5)))}
        sy = jnp.where(even, jnp.float32(1), jnp.float32(-1))
        values = [harmonic(own[2], near_y(gets[2], "")[0])]
        near = near_y(gets[4], "z")
        for dz, got, ok in ((1, near[1], sub_y < 2 * last), (-1, near[2], sub_y >= 2)):
            values.append(jnp.where(ok, dz * sy * (own[4] + got), zero))
        near = near_y(gets[5], "x")
        for dx, got, ok in ((1, near[1], lane_y < LANES - 1), (-1, near[2], lane_y > 0)):
            values.append(jnp.where(ok, dx * sy * (own[5] + got), zero))
        size = None
        for j, value in enumerate(values):
            rcy[j] = value
            size = jnp.abs(value) if size is None else size + jnp.abs(value)
        pack[0 : 2 * cz, :] = size
        pack_sides(gets[4])
        turned = pack[...].T
        turn[0] = turned
        rim_z = {}
        for k in range(len(kinds)):
            sz, face = steps[k][:2]
            sign = jnp.float32(sz) if isinstance(sz, int) else sz.astype(jnp.float32)
            own = {c: ten[c, pl.ds(face, 1), 8:top, :][0] for c in (0, 3, 4)}
            values = [harmonic(own[0], near_z(gets[0], k, "", None)[0])]
            near = near_z(gets[3], k, "x", None)
            for dx, got in ((1, near[1]), (-1, near[2])):
                values.append((sign * dx) * (own[3] + got))
            near = near_z(gets[4], k, "y", turned)
            for dy, got in ((1, near[1]), (-1, near[2])):
                values.append((sign * dy) * (own[4] + got))
            size = None
            for j, value in enumerate(values):
                rcz[k, j] = value
                size = jnp.abs(value) if size is None else size + jnp.abs(value)
            rim_z[k] = size
        add_xz(robin, lambda sx: rim_x[sx], lambda k: rim_z[k])

        def weigh(weights, values):
            out = None
            for j, value in enumerate(values):
                term = weights(j) * value
                out = term if out is None else out + term
            return out

        def spread_pressure(dest, stage, q):
            get = getters(stage, q)
            pack[0 : 2 * cz, :] = weigh(lambda j: rcy[j], near_y(get, "zx"))
            pack_sides(get)
            turned = pack[...].T
            turn[1] = turned
            add_xz(
                dest,
                lambda sx: weigh(lambda j: rcx[(sx + 1) // 2, j], near_x(get, sx, "zy")),
                lambda k: weigh(lambda j: rcz[k, j], near_z(get, k, "xy", turned)),
            )

        def first_tile(step, t, carry):
            r = rows_of(t)
            mid = rows_of(t + 1)
            for z in range(cz):
                if step == 0:
                    rim = robin[z, r, :] + at_ends(turn.at[0], r, z)
                    total = diag[z, r, :] + rim
                    rim = ROBIN * rim
                    weight = 1.0 / (total + rim)
                    diag[z, r, :] = total
                    robin[z, r, :] = rim
                    inv[z, r, :] = weight
                else:
                    rim = robin[z, r, :]
                    weight = inv[z, r, :]
                fixed = base[z, r, :] + at_ends(turn.at[1], r, z) + rim * va[z, mid, :]
                base[z, r, :] = fixed
                vb[z, mid, :] = (fixed + part[z, r, :]) * weight
            return carry

        def second_tile(t, carry):
            r = rows_of(t)
            got = gather(vb, t, lambda z: base[z, r, :])
            planes = [value * inv[z, r, :] for z, value in enumerate(got)]
            for z in range(cz):
                va[z, rows_of(t + 1), :] = planes[z]
            mixed[0, r, :] = mix(planes)
            return carry

        def residual_tile(t, carry):
            r = rows_of(t)
            mid = rows_of(t + 1)
            for z, value in enumerate(
                gather(va, t, lambda z: src_ref[z, r, :] - diag[z, r, :] * va[z, mid, :])
            ):
                res_ref[z, r, :] = value
            return carry

        def last_tile(t, carry):
            r = rows_of(t)
            for z in range(cz):
                res_ref[z, r, :] += at_ends(turn.at[1], r, z)
            return carry

        for step in range(ITERS):
            spread_pressure(base, step, 2 if step == 0 else 0)
            lax.fori_loop(0, tiles, lambda t, c: first_tile(step, t, c), 0, unroll=2)
            lax.fori_loop(0, 2, lambda i, c: second_tile(i * (tiles - 1), c), 0)
            xs, ys = stages[step + 1][1:3]
            for side, x in ((0, 8), (1, top - 1)):
                xs[side, 0] = va[:, x, :]
            start(step + 1, x_dirs)
            lax.fori_loop(1, tiles - 1, second_tile, 0, unroll=2)
            ys[0] = mixed[0].T[: 2 * cz]
            start(step + 1, y_dirs + z_dirs)
            lax.fori_loop(0, tiles, residual_tile if step == ITERS - 1 else inside_tile, 0, unroll=4)
            if step == 0:
                sent(step)
            sent(step + 1)
            arrive(step + 1, dirs)
        spread_pressure(res_ref, ITERS, 0)
        lax.fori_loop(0, tiles, last_tile, 0, unroll=4)

    return kernel


def write_out(pressure, residual, out_hbm, res_hbm, sem):
    cz, cx, cy = residual.shape
    copies = [
        pltpu.make_async_copy(pressure.at[:, pl.ds(8, cx), :], out_hbm, sem.at[0]),
        pltpu.make_async_copy(residual, res_hbm, sem.at[1]),
    ]
    for copy in copies:
        copy.start()
    for copy in copies:
        copy.wait()


def solution(mesh):
    sizes = tuple(mesh.shape[a] for a in AXES)

    def per_device(rock_ids, log_perm, rock_diagonal, rock_shear, rock_storage, source, pressure_start):
        shape = rock_ids.shape
        cz, cx, cy = shape
        classes = rock_storage.shape[0]
        f32 = jnp.float32
        padded = (cz, cx + 16, cy)
        x_dirs, y_dirs, z_dirs = directions(z_kinds(sizes[0]))
        faces = max(len(z_dirs), 1)

        def exchange(nq):
            return [
                pltpu.VMEM((2, nq, cz, cy), f32),
                pltpu.VMEM((nq, 2 * cz, cx), f32),
                pltpu.VMEM((faces, nq, cx, cy), f32),
                pltpu.VMEM((len(x_dirs), nq, cz, cy), f32),
                pltpu.VMEM((len(y_dirs), nq, 2 * cz, cx), f32),
            ]

        hbm = pl.BlockSpec(memory_space=pltpu.HBM)
        smem = pl.BlockSpec(memory_space=pltpu.SMEM)
        vmem = pl.BlockSpec(memory_space=pltpu.VMEM)
        count = len(x_dirs) + len(y_dirs) + len(z_dirs)
        kept = pl.pallas_call(
            make_kernel(sizes, shape, classes),
            out_shape=(pltpu.VMEM(padded, f32), pltpu.VMEM(shape, f32)),
            in_specs=[hbm, hbm, smem, smem, smem, hbm, hbm],
            out_specs=(vmem, vmem),
            scratch_shapes=[
                pltpu.VMEM((7, classes, 8, cy), f32),
                pltpu.VMEM((6,) + padded, f32),
                pltpu.VMEM(padded, f32),
                pltpu.VMEM((len(OFFSETS), cz, cx + 8, cy), f32),
            ]
            + [pltpu.VMEM(shape, f32)] * 5
            + [
                pltpu.VMEM((3, cx, cy), f32),
                pltpu.VMEM((cx, cy), f32),
                pltpu.VMEM((2, cx, cy), f32),
                pltpu.VMEM((cx + 16, cy), f32),
                pltpu.VMEM((2, 5, cz, cy), f32),
                pltpu.VMEM((5, 2 * cz, cx), f32),
                pltpu.VMEM((faces, 5, cx, cy), f32),
                pltpu.VMEM((faces, 3, cx, cy), f32),
            ]
            + exchange(3)
            + exchange(1)
            + exchange(1)
            + [pltpu.VMEM(shape, jnp.int32)]
            + [pltpu.VMEM(shape, f32)] * 2
            + [
                pltpu.SemaphoreType.DMA((4,)),
                pltpu.SemaphoreType.DMA((ITERS + 1, count)),
                pltpu.SemaphoreType.DMA((ITERS + 1, count)),
            ],
            compiler_params=pltpu.CompilerParams(
                collective_id=0, has_side_effects=True, vmem_limit_bytes=61440 * 1024
            ),
            name="schwarz",
        )(rock_ids, log_perm, rock_diagonal.T, rock_shear.T, rock_storage, source, pressure_start)
        return pl.pallas_call(
            write_out,
            out_shape=(jax.ShapeDtypeStruct(shape, f32), jax.ShapeDtypeStruct(shape, f32)),
            in_specs=[vmem, vmem],
            out_specs=(hbm, hbm),
            scratch_shapes=[pltpu.SemaphoreType.DMA((2,))],
            name="write_out",
        )(*(pltpu.with_memory_space_constraint(k, pltpu.VMEM) for k in kept))

    block = P("gz", "gx", "gy")
    return jax.shard_map(
        per_device,
        mesh=mesh,
        in_specs=(block, block, P(), P(), P(), block, block),
        out_specs=(block, block),
        check_vma=False,
    )
```

```python
import jax
import jax.numpy as jnp
from jax import lax
from jax.experimental import pallas as pl
from jax.experimental.pallas import tpu as pltpu
from jax.sharding import PartitionSpec as P

ITERS = 2
SWEEPS = 2
ROBIN = 0.5
AXES = ("gz", "gx", "gy")
LANES = 128
FACE = 2.0
EDGE = 0.125


def build_offsets():
    found = []
    for axis in range(3):
        for sign in (1, -1):
            vector = [0, 0, 0]
            vector[axis] = sign
            found.append((tuple(vector), axis, 1))
    for first, second, comp in ((0, 1, 3), (0, 2, 4), (1, 2, 5)):
        for sign_a in (1, -1):
            for sign_b in (1, -1):
                vector = [0, 0, 0]
                vector[first] = sign_a
                vector[second] = sign_b
                found.append((tuple(vector), comp, sign_a * sign_b))
    return found


OFFSETS = build_offsets()


def z_kinds(blocks):
    if blocks < 2:
        return ()
    return ("other",) if blocks == 2 else (1, -1)


def directions(kinds):
    found = [(0, dx, dy) for dx in (1, -1) for dy in (1, -1)]
    found += [(k + 1, dx, 0) for k in range(len(kinds)) for dx in (1, -1)]
    found += [(0, dx, 0) for dx in (1, -1)]
    x_dirs = found
    y_dirs = [(k + 1, 0, dy) for k in range(len(kinds)) for dy in (1, -1)]
    y_dirs += [(0, 0, dy) for dy in (1, -1)]
    z_dirs = [(k + 1, 0, 0) for k in range(len(kinds))]
    return x_dirs, y_dirs, z_dirs


def make_kernel(sizes, shape, classes):
    cz, cx, cy = shape
    tiles = cx // 8
    top = cx + 8
    last = cz - 1
    kinds = z_kinds(sizes[0])
    x_dirs, y_dirs, z_dirs = directions(kinds)
    dirs = x_dirs + y_dirs + z_dirs
    slot = {d: i for i, d in enumerate(dirs)}
    x_slot = {d: i for i, d in enumerate(x_dirs)}
    y_slot = {d: i for i, d in enumerate(y_dirs)}

    def opposite(d):
        k = d[0]
        if k and len(kinds) == 2:
            k = 3 - k
        return (k, -d[1], -d[2])

    def kernel(
        ids_hbm, lp_hbm, dia_ref, she_ref, sto_ref, src_hbm, p_hbm,
        va, res_ref,
        tab, ten, tup, tdn, dup, ddn, vb,
        coef, diag, robin, inv, base, part, mixed, pack, turn, zpad,
        rcx, rcy, rcz,
        zs1, xs1, ys1, zl1, xl1, yl1,
        xs2, ys2, zl2, xl2, yl2,
        xs3, ys3, zl3, xl3, yl3,
        ids_ref, lp_ref, src_ref, load_sem,
        send_sem, recv_sem,
    ):
        whole = pl.ds(8, cx)
        loads = [
            pltpu.make_async_copy(a, b, load_sem.at[i])
            for i, (a, b) in enumerate(
                ((ids_hbm, ids_ref), (lp_hbm, lp_ref), (p_hbm, va.at[:, whole, :]), (src_hbm, src_ref))
            )
        ]
        for load in loads:
            load.start()
        here = [lax.axis_index(a) for a in AXES]
        if len(kinds) == 1:
            steps = [(1 - 2 * here[0], last * (1 - here[0]), last * here[0])]
        else:
            steps = [(k, last if k == 1 else 0, 0 if k == 1 else last) for k in kinds]

        ends_z = [(0, last), [s[2] for s in steps], ()][len(kinds)]

        def exists(d):
            ok = None
            terms = []
            if d[0] and len(kinds) == 2:
                terms.append(here[0] < sizes[0] - 1 if kinds[d[0] - 1] == 1 else here[0] > 0)
            for axis in (1, 2):
                if d[axis] == 1:
                    terms.append(here[axis] < sizes[axis] - 1)
                elif d[axis] == -1:
                    terms.append(here[axis] > 0)
            for term in terms:
                ok = term if ok is None else jnp.logical_and(ok, term)
            return ok

        there = {d: exists(d) for d in dirs}

        def when(ok):
            if ok is None:
                return lambda f: f()
            return pl.when(ok)

        def target(d):
            out = {AXES[i]: here[i] + d[i] for i in (1, 2) if d[i] != 0}
            if d[0]:
                out[AXES[0]] = here[0] + steps[d[0] - 1][0]
            return out

        barrier = pltpu.get_barrier_semaphore()

        for ref in (zl1, xl1, yl1, zl2, xl2, yl2, zl3, xl3, yl3):
            ref[...] = jnp.zeros_like(ref)

        expected = jnp.int32(0)
        for d in dirs:
            @when(there[d])
            def _(d=d):
                pl.semaphore_signal(
                    barrier, inc=1, device_id=target(d),
                    device_id_type=pl.DeviceIdType.MESH,
                )
            expected = expected + (1 if there[d] is None else there[d].astype(jnp.int32))

        stages = (
            (None, xs1, ys1, zl1, xl1, yl1),
            (None, xs2, ys2, zl2, xl2, yl2),
            (None, xs3, ys3, zl3, xl3, yl3),
        )

        lane = lax.broadcasted_iota(jnp.int32, (cx, LANES), 1)
        lane_t = lax.broadcasted_iota(jnp.int32, (8, LANES), 1)

        def copy_of(stage, d):
            zs, xs, ys, zl, xl, yl = stages[stage]
            if d[1] != 0:
                src, dst = xs.at[(d[1] + 1) // 2], xl.at[x_slot[d]]
            elif d[2] != 0:
                src, dst = ys, yl.at[y_slot[d]]
            else:
                k = d[0] - 1
                src = zs1.at[k] if stage == 0 else va.at[pl.ds(steps[k][1], 1), whole, :]
                dst = zl.at[k]
            return pltpu.make_async_remote_copy(
                src_ref=src, dst_ref=dst,
                send_sem=send_sem.at[stage, slot[d]],
                recv_sem=recv_sem.at[stage, slot[d]],
                device_id=target(d), device_id_type=pl.DeviceIdType.MESH,
            )

        def start(stage, some):
            for d in some:
                @when(there[d])
                def _(d=d):
                    copy_of(stage, d).start()

        def arrive(stage, some):
            for d in some:
                @when(there[opposite(d)])
                def _(d=d):
                    copy_of(stage, d).wait_recv()

        def sent(stage):
            for d in dirs:
                @when(there[d])
                def _(d=d):
                    copy_of(stage, d).wait_send()

        def getters(stage, q):
            zl, xl, yl = stages[stage][3:]

            def get_z(k):
                return zl[opposite((k + 1, 0, 0))[0] - 1, q]

            def get_x(sx, sy):
                return xl[x_slot[(0, -sx, -sy)], q]

            def get_y(sy):
                return yl[y_slot[(0, 0, -sy)], q]

            def get_zx(k, sx):
                return xl[x_slot[opposite((k + 1, sx, 0))], q, pl.ds(steps[k][2], 1), :]

            def get_zy(k, sy):
                return yl[y_slot[opposite((k + 1, 0, sy))], q, pl.ds(2 * steps[k][2], 2), :]

            return get_z, get_x, get_y, get_zx, get_zy

        lane_x = lax.broadcasted_iota(jnp.int32, (cz, LANES), 1)
        sub_x = lax.broadcasted_iota(jnp.int32, (cz, LANES), 0)
        lane_y = lax.broadcasted_iota(jnp.int32, (2 * cz, LANES), 1)
        sub_y = lax.broadcasted_iota(jnp.int32, (2 * cz, LANES), 0)
        even = sub_y % 2 == 0
        zero = jnp.float32(0)

        def near_x(get, sx, names):
            get_x = get[1]
            plain = get_x(sx, 0)
            out = [plain]
            if "z" in names:
                out.append(jnp.where(sub_x < last, pltpu.roll(plain, cz - 1, 0), zero))
                out.append(jnp.where(sub_x > 0, pltpu.roll(plain, 1, 0), zero))
            if "y" in names:
                side = jnp.where(lane_x >= LANES // 2, get_x(sx, -1), get_x(sx, 1))
                out.append(pltpu.roll(jnp.where(lane_x == 0, side, plain), LANES - 1, 1))
                out.append(pltpu.roll(jnp.where(lane_x == LANES - 1, side, plain), 1, 1))
            return out

        def near_y(get, names):
            get_y = get[2]
            plain = jnp.where(
                even,
                pltpu.roll(get_y(1), 2 * cz - 1, 0),
                pltpu.roll(get_y(-1), 1, 0),
            )
            out = [plain]
            if "z" in names:
                out.append(jnp.where(sub_y < 2 * last, pltpu.roll(plain, 2 * cz - 2, 0), zero))
                out.append(jnp.where(sub_y >= 2, pltpu.roll(plain, 2, 0), zero))
            if "x" in names:
                ahead, behind = pltpu.roll(plain, LANES - 1, 1), pltpu.roll(plain, 1, 1)
                out.append(jnp.where(lane_y < LANES - 1, ahead, zero))
                out.append(jnp.where(lane_y > 0, behind, zero))
            return out

        even_two = lax.broadcasted_iota(jnp.int32, (2, LANES), 0) == 0

        def pack_sides(get):
            get_zy = get[4]
            for k in range(len(kinds)):
                at = 2 * cz + 2 * k
                pack[at : at + 2, :] = jnp.where(even_two, get_zy(k, -1), get_zy(k, 1))

        def near_z(get, k, names, turned):
            get_z, get_zx = get[0], get[3]
            plain = get_z(k)
            out = [plain]
            if "x" in names:
                zpad[8:top, :] = plain
                zpad[7:8, :] = get_zx(k, -1)
                zpad[top : top + 1, :] = get_zx(k, 1)
                out.append(zpad[9 : top + 1, :])
                out.append(zpad[7 : top - 1, :])
            if "y" in names:
                at = 2 * cz + 2 * k
                ahead, behind = pltpu.roll(plain, LANES - 1, 1), pltpu.roll(plain, 1, 1)
                out.append(jnp.where(lane == LANES - 1, pltpu.roll(turned, LANES - 2 - at, 1), ahead))
                out.append(jnp.where(lane == 0, pltpu.roll(turned, LANES - at, 1), behind))
            return out

        def harmonic(own, near):
            return own * near / (own + near)

        def rows_of(t):
            return pl.ds(pl.multiple_of(t * 8, 8), 8)

        ends = jnp.logical_or(lane_t == 0, lane_t == LANES - 1)

        def at_ends(ref, r, z):
            return jnp.where(ends, pltpu.roll(ref[r, :], LANES - 1 - 2 * z, 1), zero)

        def add_xz(dest, of_x, of_z):
            for k in range(len(kinds)):
                dest[pl.ds(steps[k][1], 1)] += of_z(k)[None]
            for sx, row in ((-1, 0), (1, cx - 1)):
                dest[:, row, :] += of_x(sx)

        def mix(planes):
            out = None
            for z in range(cz):
                moved = pltpu.roll(planes[z], 2 * z + 1, 1)
                out = moved if out is None else jnp.where((lane_t // 2) == z, moved, out)
            return out

        for c in range(classes):
            for k in range(3):
                tab[k, c : c + 1, :] = jnp.full((1, LANES), dia_ref[k, c], jnp.float32)
                tab[3 + k, c : c + 1, :] = jnp.full((1, LANES), she_ref[k, c], jnp.float32)
            tab[6, c : c + 1, :] = jnp.full((1, LANES), sto_ref[c], jnp.float32)
        cols = [tab[k] for k in range(3)]
        for k, (a, b) in enumerate(((0, 1), (0, 2), (1, 2))):
            tab[3 + k] = EDGE * tab[3 + k] * jnp.sqrt(cols[a] * cols[b])
        for k in range(3):
            tab[k] = FACE * cols[k]

        pack[...] = jnp.zeros_like(pack)
        for ref in (va, vb):
            for lo in (0, top):
                ref[:, lo : lo + 8, :] = jnp.zeros((cz, 8, LANES), jnp.float32)
        for lo in (0, top):
            ten[:, :, lo : lo + 8, :] = jnp.zeros((6, cz, 8, LANES), jnp.float32)

        def code_of(ids):
            return (ids + 1).astype(jnp.float32)

        for load in loads[:3]:
            load.wait()

        for k in range(len(kinds)):
            face = pl.ds(steps[k][1], 1)
            zs1[k, 0:1] = code_of(ids_ref[face])
            zs1[k, 1:2] = lp_ref[face]
            zs1[k, 2:3] = va[face, whole, :]
        for side, x in ((0, 0), (1, cx - 1)):
            xs1[side, 0] = code_of(ids_ref[:, x, :])
            xs1[side, 1] = lp_ref[:, x, :]
            xs1[side, 2] = va[:, 8 + x, :]

        def mix_tile(t, carry):
            r = rows_of(t)
            mixed[0, r, :] = mix(code_of(ids_ref[:, r, :]))
            mixed[1, r, :] = mix(lp_ref[:, r, :])
            mixed[2, r, :] = mix(va[:, rows_of(t + 1), :])
            return carry

        lax.fori_loop(0, tiles, mix_tile, 0, unroll=4)
        for q in range(3):
            ys1[q] = mixed[q].T[: 2 * cz]

        pl.semaphore_wait(barrier, expected)
        start(0, dirs)

        def pick(ids, comps):
            count = ids.shape[0]
            if count < 8:
                ids = jnp.concatenate([ids] * (8 // count), axis=0)
            found = []
            for k in comps:
                parts = []
                for at in range(0, ids.shape[0], 8):
                    some = ids[at : at + 8]
                    if classes <= 8:
                        part_ = jnp.take_along_axis(tab[k], some, axis=0, mode="promise_in_bounds")
                    else:
                        part_ = jnp.zeros(some.shape, jnp.float32)
                        for c in range(classes):
                            part_ = jnp.where(some == c, tab[k, c : c + 1, :], part_)
                    parts.append(part_)
                got = parts[0] if len(parts) == 1 else jnp.concatenate(parts, axis=0)
                found.append(got[:count])
            return found

        def tensors(code, perm, comps):
            ids = jnp.maximum(code - 1.0, 0.0).astype(jnp.int32)
            gain = jnp.where(code > 0.5, jnp.exp(perm), zero)
            return [f * gain for f in pick(ids, comps)]

        turned_of = (2, 4, 5)

        def tensor_tile(t, carry):
            r = rows_of(t)
            out = rows_of(t + 1)
            for z in range(cz):
                gain = jnp.exp(lp_ref[z, r, :])
                found = pick(ids_ref[z, r, :], range(7))
                diag[z, r, :] = found[6]
                for k in range(6):
                    value = found[k] * gain
                    ten[k, z, out, :] = value
                    if k in turned_of:
                        at = turned_of.index(k)
                        tup[at, z, r, :] = pltpu.roll(value, 1, 1)
                        tdn[at, z, r, :] = pltpu.roll(value, LANES - 1, 1)
            return carry

        lax.fori_loop(0, tiles, tensor_tile, 0, unroll=2)

        row_t = lax.broadcasted_iota(jnp.int32, (8, LANES), 0)

        def coef_tile(t, carry):
            r = rows_of(t)
            mid = rows_of(t + 1)
            row = {0: mid, 1: pl.ds(t * 8 + 9, 8), -1: pl.ds(t * 8 + 7, 8)}
            x_out = {1: row_t + t * 8 == cx - 1, -1: row_t + t * 8 == 0}
            y_out = {1: lane_t == 0, -1: lane_t == LANES - 1}
            xy_out = {(dx, dy): jnp.logical_or(x_out[dx], y_out[dy]) for dx in (1, -1) for dy in (1, -1)}
            for z in range(cz):
                own = {}
                for comp in range(6):
                    own[comp, 0] = ten[comp, z, mid, :]
                    if comp in turned_of:
                        own[comp, 1] = tup[turned_of.index(comp), z, r, :]
                        own[comp, -1] = tdn[turned_of.index(comp), z, r, :]
                total = {0: diag[z, r, :], 1: None, -1: None}
                for e, ((dz, dx, dy), comp, sign) in enumerate(OFFSETS):
                    if not 0 <= z + dz < cz:
                        continue
                    near = ten[comp, z + dz, row[dx], :]
                    if comp < 3:
                        value = harmonic(own[comp, dy], near)
                    else:
                        value = own[comp, dy] + near
                    if dx and dy:
                        value = jnp.where(xy_out[dx, dy], zero, value)
                    elif dx and dz:
                        value = jnp.where(x_out[dx], zero, value)
                    elif dy:
                        value = jnp.where(y_out[dy], zero, value)
                    coef[e, z, r, :] = value
                    size = value if comp < 3 else jnp.abs(value)
                    total[dy] = size if total[dy] is None else total[dy] + size
                diag[z, r, :] = total[0]
                dup[z, r, :] = total[1]
                ddn[z, r, :] = total[-1]
                robin[z, r, :] = jnp.zeros((8, LANES), jnp.float32)
            return carry

        lax.fori_loop(0, tiles, coef_tile, 0, unroll=2)

        def gather(ref, t, first):
            r = rows_of(t)
            row = {0: rows_of(t + 1), 1: pl.ds(t * 8 + 9, 8), -1: pl.ds(t * 8 + 7, 8)}
            near = {dx: ref[:, row[dx], :] for dx in (0, 1, -1)}
            out = []
            for z in range(cz):
                acc = {0: first(z), 1: None, -1: None}
                for e, ((dz, dx, dy), comp, sign) in enumerate(OFFSETS):
                    if not 0 <= z + dz < cz:
                        continue
                    term = coef[e, z, r, :] * near[dx][z + dz]
                    if acc[dy] is None:
                        acc[dy] = term if sign == 1 else -term
                    else:
                        acc[dy] = acc[dy] + term if sign == 1 else acc[dy] - term
                out.append(acc[0] + (pltpu.roll(acc[1], LANES - 1, 1) + pltpu.roll(acc[-1], 1, 1)))
            return out

        for plane in ends_z:
            own = [jnp.abs(ten[c, pl.ds(plane, 1), 8:top, :]) for c in (3, 4)]
            robin[pl.ds(plane, 1)] += 2.0 * (own[0] + own[1])

        loads[3].wait()

        def inside_tile(step, t, carry):
            r = rows_of(t)
            if step == 0:
                for z in range(cz):
                    diag[z, r, :] += pltpu.roll(dup[z, r, :], LANES - 1, 1) + pltpu.roll(ddn[z, r, :], 1, 1)
            for z, value in enumerate(gather(va, t, lambda z: None)):
                part[z, r, :] = value
            base[:, r, :] = src_ref[:, r, :]
            return carry

        lax.fori_loop(0, tiles, lambda t, c: inside_tile(0, t, c), 0, unroll=4)

        arrive(0, dirs)

        gid = getters(0, 0)
        glp = getters(0, 1)

        def tensor_get(k):
            def of(which):
                def get(*args):
                    return tensors(gid[which](*args), glp[which](*args), [k])[0]
                return get
            return tuple(of(i) for i in range(5))

        gets = {k: tensor_get(k) for k in range(6)}
        rim_x = {}
        for side, sx in ((0, -1), (1, 1)):
            row = 8 if sx == -1 else top - 1
            own = {k: ten[k, :, row, :] for k in (1, 3, 5)}
            values = [harmonic(own[1], near_x(gets[1], sx, "")[0])]
            near = near_x(gets[3], sx, "z")
            for dz, got, ok in ((1, near[1], sub_x < last), (-1, near[2], sub_x > 0)):
                values.append(jnp.where(ok, (dz * sx) * (own[3] + got), zero))
            near = near_x(gets[5], sx, "y")
            for dy, got in ((1, near[1]), (-1, near[2])):
                values.append((sx * dy) * (own[5] + got))
            size = None
            for j, value in enumerate(values):
                rcx[side, j] = value
                size = jnp.abs(value) if size is None else size + jnp.abs(value)
            rim_x[sx] = size

        own = dict(zip((2, 4, 5), tensors(ys1[0], ys1[1], (2, 4, 5))))
        sy = jnp.where(even, jnp.float32(1), jnp.float32(-1))
        values = [harmonic(own[2], near_y(gets[2], "")[0])]
        near = near_y(gets[4], "z")
        for dz, got, ok in ((1, near[1], sub_y < 2 * last), (-1, near[2], sub_y >= 2)):
            values.append(jnp.where(ok, dz * sy * (own[4] + got), zero))
        near = near_y(gets[5], "x")
        for dx, got, ok in ((1, near[1], lane_y < LANES - 1), (-1, near[2], lane_y > 0)):
            values.append(jnp.where(ok, dx * sy * (own[5] + got), zero))
        size = None
        for j, value in enumerate(values):
            rcy[j] = value
            size = jnp.abs(value) if size is None else size + jnp.abs(value)
        pack[0 : 2 * cz, :] = size
        pack_sides(gets[4])
        turned = pack[...].T
        turn[0] = turned
        rim_z = {}
        for k in range(len(kinds)):
            sz, face = steps[k][:2]
            sign = jnp.float32(sz) if isinstance(sz, int) else sz.astype(jnp.float32)
            own = {c: ten[c, pl.ds(face, 1), 8:top, :][0] for c in (0, 3, 4)}
            values = [harmonic(own[0], near_z(gets[0], k, "", None)[0])]
            near = near_z(gets[3], k, "x", None)
            for dx, got in ((1, near[1]), (-1, near[2])):
                values.append((sign * dx) * (own[3] + got))
            near = near_z(gets[4], k, "y", turned)
            for dy, got in ((1, near[1]), (-1, near[2])):
                values.append((sign * dy) * (own[4] + got))
            size = None
            for j, value in enumerate(values):
                rcz[k, j] = value
                size = jnp.abs(value) if size is None else size + jnp.abs(value)
            rim_z[k] = size
        add_xz(robin, lambda sx: rim_x[sx], lambda k: rim_z[k])

        def weigh(weights, values):
            out = None
            for j, value in enumerate(values):
                term = weights(j) * value
                out = term if out is None else out + term
            return out

        def spread_pressure(dest, stage, q):
            get = getters(stage, q)
            pack[0 : 2 * cz, :] = weigh(lambda j: rcy[j], near_y(get, "zx"))
            pack_sides(get)
            turned = pack[...].T
            turn[1] = turned
            add_xz(
                dest,
                lambda sx: weigh(lambda j: rcx[(sx + 1) // 2, j], near_x(get, sx, "zy")),
                lambda k: weigh(lambda j: rcz[k, j], near_z(get, k, "xy", turned)),
            )

        def first_tile(step, t, carry):
            r = rows_of(t)
            mid = rows_of(t + 1)
            for z in range(cz):
                if step == 0:
                    rim = robin[z, r, :] + at_ends(turn.at[0], r, z)
                    total = diag[z, r, :] + rim
                    rim = ROBIN * rim
                    weight = 1.0 / (total + rim)
                    diag[z, r, :] = total
                    robin[z, r, :] = rim
                    inv[z, r, :] = weight
                else:
                    rim = robin[z, r, :]
                    weight = inv[z, r, :]
                fixed = base[z, r, :] + at_ends(turn.at[1], r, z) + rim * va[z, mid, :]
                base[z, r, :] = fixed
                vb[z, mid, :] = (fixed + part[z, r, :]) * weight
            return carry

        def second_tile(t, carry):
            r = rows_of(t)
            got = gather(vb, t, lambda z: base[z, r, :])
            for z, value in enumerate(got):
                va[z, rows_of(t + 1), :] = value * inv[z, r, :]
            return carry

        def mix_sent(t, carry):
            mixed[0, rows_of(t), :] = mix(va[:, rows_of(t + 1), :])
            return carry

        def residual_tile(t, carry):
            r = rows_of(t)
            mid = rows_of(t + 1)
            for z, value in enumerate(
                gather(va, t, lambda z: src_ref[z, r, :] - diag[z, r, :] * va[z, mid, :])
            ):
                res_ref[z, r, :] = value
            return carry

        def last_tile(t, carry):
            r = rows_of(t)
            for z in range(cz):
                res_ref[z, r, :] += at_ends(turn.at[1], r, z)
            return carry

        for step in range(ITERS):
            spread_pressure(base, step, 2 if step == 0 else 0)
            lax.fori_loop(0, tiles, lambda t, c: first_tile(step, t, c), 0, unroll=4)
            lax.fori_loop(0, tiles, second_tile, 0, unroll=4)
            xs, ys = stages[step + 1][1:3]
            for side, x in ((0, 8), (1, top - 1)):
                xs[side, 0] = va[:, x, :]
            start(step + 1, x_dirs)
            lax.fori_loop(0, tiles, mix_sent, 0, unroll=8)
            ys[0] = mixed[0].T[: 2 * cz]
            start(step + 1, y_dirs + z_dirs)
            if step == ITERS - 1:
                lax.fori_loop(0, tiles, residual_tile, 0, unroll=4)
            else:
                lax.fori_loop(0, tiles, lambda t, c: inside_tile(step + 1, t, c), 0, unroll=4)
            if step == 0:
                sent(step)
            sent(step + 1)
            arrive(step + 1, dirs)
        spread_pressure(res_ref, ITERS, 0)
        lax.fori_loop(0, tiles, last_tile, 0, unroll=8)

    return kernel


def write_out(pressure, residual, out_hbm, res_hbm, sem):
    cz, cx, cy = residual.shape
    copies = [
        pltpu.make_async_copy(pressure.at[:, pl.ds(8, cx), :], out_hbm, sem.at[0]),
        pltpu.make_async_copy(residual, res_hbm, sem.at[1]),
    ]
    for copy in copies:
        copy.start()
    for copy in copies:
        copy.wait()


def solution(mesh):
    sizes = tuple(mesh.shape[a] for a in AXES)

    def per_device(rock_ids, log_perm, rock_diagonal, rock_shear, rock_storage, source, pressure_start):
        shape = rock_ids.shape
        cz, cx, cy = shape
        classes = rock_storage.shape[0]
        f32 = jnp.float32
        padded = (cz, cx + 16, cy)
        x_dirs, y_dirs, z_dirs = directions(z_kinds(sizes[0]))
        faces = max(len(z_dirs), 1)

        def exchange(nq):
            return [
                pltpu.VMEM((2, nq, cz, cy), f32),
                pltpu.VMEM((nq, 2 * cz, cx), f32),
                pltpu.VMEM((faces, nq, cx, cy), f32),
                pltpu.VMEM((len(x_dirs), nq, cz, cy), f32),
                pltpu.VMEM((len(y_dirs), nq, 2 * cz, cx), f32),
            ]

        hbm = pl.BlockSpec(memory_space=pltpu.HBM)
        smem = pl.BlockSpec(memory_space=pltpu.SMEM)
        vmem = pl.BlockSpec(memory_space=pltpu.VMEM)
        count = len(x_dirs) + len(y_dirs) + len(z_dirs)
        kept = pl.pallas_call(
            make_kernel(sizes, shape, classes),
            out_shape=(pltpu.VMEM(padded, f32), pltpu.VMEM(shape, f32)),
            in_specs=[hbm, hbm, smem, smem, smem, hbm, hbm],
            out_specs=(vmem, vmem),
            scratch_shapes=[
                pltpu.VMEM((7, -(-classes // 8) * 8, cy), f32),
                pltpu.VMEM((6,) + padded, f32),
                pltpu.VMEM((3, cz, cx + 8, cy), f32),
                pltpu.VMEM((3, cz, cx + 8, cy), f32),
                pltpu.VMEM((cz, cx + 8, cy), f32),
                pltpu.VMEM((cz, cx + 8, cy), f32),
                pltpu.VMEM(padded, f32),
                pltpu.VMEM((len(OFFSETS), cz, cx + 8, cy), f32),
            ]
            + [pltpu.VMEM(shape, f32)] * 5
            + [
                pltpu.VMEM((3, cx, cy), f32),
                pltpu.VMEM((cx, cy), f32),
                pltpu.VMEM((2, cx, cy), f32),
                pltpu.VMEM((cx + 16, cy), f32),
                pltpu.VMEM((2, 5, cz, cy), f32),
                pltpu.VMEM((5, 2 * cz, cx), f32),
                pltpu.VMEM((faces, 5, cx, cy), f32),
                pltpu.VMEM((faces, 3, cx, cy), f32),
            ]
            + exchange(3)
            + exchange(1)
            + exchange(1)
            + [pltpu.VMEM(shape, jnp.int32)]
            + [pltpu.VMEM(shape, f32)] * 2
            + [
                pltpu.SemaphoreType.DMA((4,)),
                pltpu.SemaphoreType.DMA((ITERS + 1, count)),
                pltpu.SemaphoreType.DMA((ITERS + 1, count)),
            ],
            compiler_params=pltpu.CompilerParams(
                collective_id=0, has_side_effects=True, vmem_limit_bytes=61440 * 1024
            ),
            name="schwarz",
        )(rock_ids, log_perm, rock_diagonal.T, rock_shear.T, rock_storage, source, pressure_start)
        return pl.pallas_call(
            write_out,
            out_shape=(jax.ShapeDtypeStruct(shape, f32), jax.ShapeDtypeStruct(shape, f32)),
            in_specs=[vmem, vmem],
            out_specs=(hbm, hbm),
            scratch_shapes=[pltpu.SemaphoreType.DMA((2,))],
            name="write_out",
        )(*(pltpu.with_memory_space_constraint(k, pltpu.VMEM) for k in kept))

    block = P("gz", "gx", "gy")
    return jax.shard_map(
        per_device,
        mesh=mesh,
        in_specs=(block, block, P(), P(), P(), block, block),
        out_specs=(block, block),
        check_vma=False,
    )
```

```python
import jax
import jax.numpy as jnp
from jax import lax
from jax.experimental import pallas as pl
from jax.experimental.pallas import tpu as pltpu
from jax.sharding import PartitionSpec as P

ITERS = 2
SWEEPS = 2
ROBIN = 0.5
AXES = ("gz", "gx", "gy")
LANES = 128
FACE = 2.0
EDGE = 0.125


def build_offsets():
    found = []
    for axis in range(3):
        for sign in (1, -1):
            vector = [0, 0, 0]
            vector[axis] = sign
            found.append((tuple(vector), axis, 1))
    for first, second, comp in ((0, 1, 3), (0, 2, 4), (1, 2, 5)):
        for sign_a in (1, -1):
            for sign_b in (1, -1):
                vector = [0, 0, 0]
                vector[first] = sign_a
                vector[second] = sign_b
                found.append((tuple(vector), comp, sign_a * sign_b))
    return found


OFFSETS = build_offsets()


def z_kinds(blocks):
    if blocks < 2:
        return ()
    return ("other",) if blocks == 2 else (1, -1)


def directions(kinds):
    xy_dirs = [(0, dx, dy) for dx in (1, -1) for dy in (1, -1)]
    x_dirs = [(0, dx, 0) for dx in (1, -1)]
    y_dirs = [(0, 0, dy) for dy in (1, -1)]
    zx_dirs = [(k + 1, dx, 0) for k in range(len(kinds)) for dx in (1, -1)]
    zy_dirs = [(k + 1, 0, dy) for k in range(len(kinds)) for dy in (1, -1)]
    z_dirs = [(k + 1, 0, 0) for k in range(len(kinds))]
    return xy_dirs, y_dirs, x_dirs, zy_dirs, zx_dirs, z_dirs


def make_kernel(sizes, shape, classes):
    cz, cx, cy = shape
    tiles = cx // 8
    top = cx + 8
    last = cz - 1
    kinds = z_kinds(sizes[0])
    groups = directions(kinds)
    xy_dirs, y_dirs, x_dirs, zy_dirs, zx_dirs, z_dirs = groups
    dirs = [d for group in groups for d in group]
    slot = {d: i for i, d in enumerate(dirs)}
    place = {d: i for group in groups for i, d in enumerate(group)}

    def opposite(d):
        k = d[0]
        if k and len(kinds) == 2:
            k = 3 - k
        return (k, -d[1], -d[2])

    def kernel(
        ids_hbm, lp_hbm, dia_ref, she_ref, sto_ref, src_hbm, p_hbm,
        va, res_ref, turn_ref,
        tab, ten, tup, tdn, dup, ddn, vb,
        coef, diag, robin, inv, base, part, mixed, pack, turn, zpad,
        rcx, rcy, rcz,
        zs1, xc1, yfull, tall, woven,
        xs1, ys1, xyl1, yl1, xl1, zyl1, zxl1, zl1,
        xs2, ys2, xyl2, yl2, xl2, zyl2, zxl2, zl2,
        xs3, ys3, xyl3, yl3, xl3, zyl3, zxl3, zl3,
        ids_ref, lp_ref, src_ref, load_sem,
        send_sem, recv_sem,
    ):
        whole = pl.ds(8, cx)
        loads = [
            pltpu.make_async_copy(a, b, load_sem.at[i])
            for i, (a, b) in enumerate(
                ((ids_hbm, ids_ref), (lp_hbm, lp_ref), (p_hbm, va.at[:, whole, :]), (src_hbm, src_ref))
            )
        ]
        for load in loads:
            load.start()
        here = [lax.axis_index(a) for a in AXES]
        if len(kinds) == 1:
            steps = [(1 - 2 * here[0], last * (1 - here[0]), last * here[0])]
        else:
            steps = [(k, last if k == 1 else 0, 0 if k == 1 else last) for k in kinds]

        ends_z = [(0, last), [s[2] for s in steps], ()][len(kinds)]

        def exists(d):
            ok = None
            terms = []
            if d[0] and len(kinds) == 2:
                terms.append(here[0] < sizes[0] - 1 if kinds[d[0] - 1] == 1 else here[0] > 0)
            for axis in (1, 2):
                if d[axis] == 1:
                    terms.append(here[axis] < sizes[axis] - 1)
                elif d[axis] == -1:
                    terms.append(here[axis] > 0)
            for term in terms:
                ok = term if ok is None else jnp.logical_and(ok, term)
            return ok

        there = {d: exists(d) for d in dirs}

        def when(ok):
            if ok is None:
                return lambda f: f()
            return pl.when(ok)

        def target(d):
            out = {AXES[i]: here[i] + d[i] for i in (1, 2) if d[i] != 0}
            if d[0]:
                out[AXES[0]] = here[0] + steps[d[0] - 1][0]
            return out

        barrier = pltpu.get_barrier_semaphore()

        expected = jnp.int32(0)
        for d in dirs:
            @when(there[d])
            def _(d=d):
                pl.semaphore_signal(
                    barrier, inc=1, device_id=target(d),
                    device_id_type=pl.DeviceIdType.MESH,
                )
            expected = expected + (1 if there[d] is None else there[d].astype(jnp.int32))

        stages = (
            (xs1, ys1, xyl1, yl1, xl1, zyl1, zxl1, zl1),
            (xs2, ys2, xyl2, yl2, xl2, zyl2, zxl2, zl2),
            (xs3, ys3, xyl3, yl3, xl3, zyl3, zxl3, zl3),
        )

        def land(stage, d):
            kind = [d in group for group in groups].index(True)
            return stages[stage][2 + kind].at[place[d]]

        for d in dirs:
            if there[opposite(d)] is None:
                continue

            @pl.when(jnp.logical_not(there[opposite(d)]))
            def _(d=d):
                for stage in range(ITERS + 1):
                    ref = land(stage, d)
                    ref[...] = jnp.zeros_like(ref)

        lane = lax.broadcasted_iota(jnp.int32, (cx, LANES), 1)
        lane_t = lax.broadcasted_iota(jnp.int32, (8, LANES), 1)

        def copy_of(stage, d):
            xs, ys = stages[stage][:2]
            x_side, y_side = (d[1] + 1) // 2, (d[2] + 1) // 2
            face = pl.ds(steps[d[0] - 1][1], 1) if d[0] else None
            if d[1] and d[2]:
                src = xc1.at[x_side] if stage == 0 else xs.at[x_side, 0]
            elif d[1]:
                src = xs.at[x_side, :, face, :] if d[0] else xs.at[x_side]
            elif d[2]:
                src = ys.at[y_side, :, face, :] if d[0] else ys.at[y_side]
            else:
                src = zs1.at[d[0] - 1] if stage == 0 else va.at[face, whole, :]
            dst = land(stage, d)
            return pltpu.make_async_remote_copy(
                src_ref=src, dst_ref=dst,
                send_sem=send_sem.at[stage, slot[d]],
                recv_sem=recv_sem.at[stage, slot[d]],
                device_id=target(d), device_id_type=pl.DeviceIdType.MESH,
            )

        def start(stage, some):
            for d in some:
                @when(there[d])
                def _(d=d):
                    copy_of(stage, d).start()

        def arrive(stage, some):
            for d in some:
                @when(there[opposite(d)])
                def _(d=d):
                    copy_of(stage, d).wait_recv()

        def sent(stage):
            for d in dirs:
                @when(there[d])
                def _(d=d):
                    copy_of(stage, d).wait_send()

        def getters(stage, q):
            def got(d):
                return land(stage, opposite(d))

            def get_z(k):
                return got((k + 1, 0, 0))[q]

            def get_x(sx):
                return got((0, sx, 0))[q]

            def get_y(sy):
                return got((0, 0, sy))[q]

            def get_zx(k, sx):
                return got((k + 1, sx, 0))[q]

            def get_zy(k, sy):
                return got((k + 1, 0, sy))[q]

            def get_xy(sx, sy):
                if sy == 1:
                    shift = LANES - 2 - 2 * q if stage == 0 else LANES - 1
                else:
                    shift = (LANES - 2 * q) % LANES if stage == 0 else 1
                held = got((0, sx, sy))[...]
                return pltpu.roll(held, shift, 1) if shift else held

            return get_z, get_x, get_y, get_zx, get_zy, get_xy

        lane_x = lax.broadcasted_iota(jnp.int32, (cz, LANES), 1)
        sub_x = lax.broadcasted_iota(jnp.int32, (cz, LANES), 0)
        lane_y = lax.broadcasted_iota(jnp.int32, (2 * cz, LANES), 1)
        sub_y = lax.broadcasted_iota(jnp.int32, (2 * cz, LANES), 0)
        even = sub_y % 2 == 0
        zero = jnp.float32(0)

        def near_x(get, sx, names, corners=True):
            plain = get[1](sx)
            out = [plain]
            if "z" in names:
                out.append(jnp.where(sub_x < last, pltpu.roll(plain, cz - 1, 0), zero))
                out.append(jnp.where(sub_x > 0, pltpu.roll(plain, 1, 0), zero))
            if "y" in names:
                ahead, behind = pltpu.roll(plain, LANES - 1, 1), pltpu.roll(plain, 1, 1)
                out.append(jnp.where(lane_x == LANES - 1, get[5](sx, 1) if corners else zero, ahead))
                out.append(jnp.where(lane_x == 0, get[5](sx, -1) if corners else zero, behind))
            return out

        def near_y(get, names, at):
            get_y = get[2]
            woven[at, pl.ds(0, cz, 2), :] = get_y(1)
            woven[at, pl.ds(1, cz, 2), :] = get_y(-1)
            plain = woven[at]
            out = [plain]
            if "z" in names:
                out.append(jnp.where(sub_y < 2 * last, pltpu.roll(plain, 2 * cz - 2, 0), zero))
                out.append(jnp.where(sub_y >= 2, pltpu.roll(plain, 2, 0), zero))
            if "x" in names:
                ahead, behind = pltpu.roll(plain, LANES - 1, 1), pltpu.roll(plain, 1, 1)
                out.append(jnp.where(lane_y < LANES - 1, ahead, zero))
                out.append(jnp.where(lane_y > 0, behind, zero))
            return out

        def pack_sides(get):
            get_zy = get[4]
            for k in range(len(kinds)):
                at = 2 * cz + 2 * k
                pack[at : at + 1, :] = get_zy(k, -1)
                pack[at + 1 : at + 2, :] = get_zy(k, 1)

        def near_z(get, k, names, turned):
            get_z, get_zx = get[0], get[3]
            plain = get_z(k)
            out = [plain]
            if "x" in names:
                zpad[8:top, :] = plain
                zpad[7:8, :] = get_zx(k, -1)
                zpad[top : top + 1, :] = get_zx(k, 1)
                out.append(zpad[9 : top + 1, :])
                out.append(zpad[7 : top - 1, :])
            if "y" in names:
                at = 2 * cz + 2 * k
                ahead, behind = pltpu.roll(plain, LANES - 1, 1), pltpu.roll(plain, 1, 1)
                out.append(jnp.where(lane == LANES - 1, pltpu.roll(turned, LANES - 2 - at, 1), ahead))
                out.append(jnp.where(lane == 0, pltpu.roll(turned, LANES - at, 1), behind))
            return out

        def harmonic(own, near):
            return own * near / (own + near)

        def rows_of(t):
            return pl.ds(pl.multiple_of(t * 8, 8), 8)

        ends = jnp.logical_or(lane_t == 0, lane_t == LANES - 1)

        def at_ends(ref, r, z):
            return jnp.where(ends, pltpu.roll(ref[r, :], LANES - 1 - 2 * z, 1), zero)

        def add_xz(dest, of_x, of_z):
            for k in range(len(kinds)):
                dest[pl.ds(steps[k][1], 1)] += of_z(k)[None]
            for sx, row in ((-1, 0), (1, cx - 1)):
                dest[:, row, :] += of_x(sx)

        def mix(planes):
            out = None
            for z in range(cz):
                moved = pltpu.roll(planes[z], 2 * z + 1, 1)
                out = moved if out is None else jnp.where((lane_t // 2) == z, moved, out)
            return out

        for c in range(classes):
            for k in range(3):
                tab[k, c : c + 1, :] = jnp.full((1, LANES), dia_ref[k, c], jnp.float32)
                tab[3 + k, c : c + 1, :] = jnp.full((1, LANES), she_ref[k, c], jnp.float32)
            tab[6, c : c + 1, :] = jnp.full((1, LANES), sto_ref[c], jnp.float32)
        cols = [tab[k] for k in range(3)]
        for k, (a, b) in enumerate(((0, 1), (0, 2), (1, 2))):
            tab[3 + k] = EDGE * tab[3 + k] * jnp.sqrt(cols[a] * cols[b])
        for k in range(3):
            tab[k] = FACE * cols[k]

        pack[...] = jnp.zeros_like(pack)
        for ref in (va, vb):
            for lo in (0, top):
                ref[:, lo : lo + 8, :] = jnp.zeros((cz, 8, LANES), jnp.float32)
        for lo in (0, top):
            ten[:, :, lo : lo + 8, :] = jnp.zeros((6, cz, 8, LANES), jnp.float32)

        def code_of(ids):
            return (ids + 1).astype(jnp.float32)

        for load in loads[:3]:
            load.wait()

        for k in range(len(kinds)):
            face = pl.ds(steps[k][1], 1)
            zs1[k, 0:1] = code_of(ids_ref[face])
            zs1[k, 1:2] = lp_ref[face]
            zs1[k, 2:3] = va[face, whole, :]
        for side, x in ((0, 0), (1, cx - 1)):
            xs1[side, 0] = code_of(ids_ref[:, x, :])
            xs1[side, 1] = lp_ref[:, x, :]
            xs1[side, 2] = va[:, 8 + x, :]

        def mix_tile(t, carry):
            r = rows_of(t)
            mixed[0, r, :] = mix(code_of(ids_ref[:, r, :]))
            mixed[1, r, :] = mix(lp_ref[:, r, :])
            mixed[2, r, :] = mix(va[:, rows_of(t + 1), :])
            return carry

        def unweave(q, ys):
            tall[q] = mixed[q].T[: 2 * cz]
            ys[1, q] = tall[q, pl.ds(0, cz, 2), :]
            ys[0, q] = tall[q, pl.ds(1, cz, 2), :]

        lax.fori_loop(0, tiles, mix_tile, 0, unroll=4)
        for q in range(3):
            unweave(q, ys1)
        for q in range(2):
            yfull[q] = tall[q]
        for side in range(2):
            held = None
            for q in range(3):
                moved = pltpu.roll(xs1[side, q], 2 * q + 1, 1)
                held = moved if held is None else jnp.where((lane_x // 2) == q, moved, held)
            xc1[side] = held

        pl.semaphore_wait(barrier, expected)
        start(0, dirs)

        def pick(ids, comps):
            count = ids.shape[0]
            if count < 8:
                ids = jnp.concatenate([ids] * (8 // count), axis=0)
            found = []
            for k in comps:
                parts = []
                for at in range(0, ids.shape[0], 8):
                    some = ids[at : at + 8]
                    if classes <= 8:
                        part_ = jnp.take_along_axis(tab[k], some, axis=0, mode="promise_in_bounds")
                    else:
                        part_ = jnp.zeros(some.shape, jnp.float32)
                        for c in range(classes):
                            part_ = jnp.where(some == c, tab[k, c : c + 1, :], part_)
                    parts.append(part_)
                got = parts[0] if len(parts) == 1 else jnp.concatenate(parts, axis=0)
                found.append(got[:count])
            return found

        def tensors(code, perm, comps):
            ids = jnp.maximum(code - 1.0, 0.0).astype(jnp.int32)
            gain = jnp.where(code > 0.5, jnp.exp(perm), zero)
            return [f * gain for f in pick(ids, comps)]

        turned_of = (2, 4, 5)

        def tensor_tile(t, carry):
            r = rows_of(t)
            out = rows_of(t + 1)
            for z in range(cz):
                gain = jnp.exp(lp_ref[z, r, :])
                found = pick(ids_ref[z, r, :], range(7))
                diag[z, r, :] = found[6]
                for k in range(6):
                    value = found[k] * gain
                    ten[k, z, out, :] = value
                    if k in turned_of:
                        at = turned_of.index(k)
                        tup[at, z, r, :] = pltpu.roll(value, 1, 1)
                        tdn[at, z, r, :] = pltpu.roll(value, LANES - 1, 1)
            return carry

        lax.fori_loop(0, tiles, tensor_tile, 0, unroll=2)

        row_t = lax.broadcasted_iota(jnp.int32, (8, LANES), 0)

        def coef_tile(t, carry):
            r = rows_of(t)
            mid = rows_of(t + 1)
            row = {0: mid, 1: pl.ds(t * 8 + 9, 8), -1: pl.ds(t * 8 + 7, 8)}
            x_out = {1: row_t + t * 8 == cx - 1, -1: row_t + t * 8 == 0}
            y_out = {1: lane_t == 0, -1: lane_t == LANES - 1}
            xy_out = {(dx, dy): jnp.logical_or(x_out[dx], y_out[dy]) for dx in (1, -1) for dy in (1, -1)}
            for z in range(cz):
                own = {}
                for comp in range(6):
                    own[comp, 0] = ten[comp, z, mid, :]
                    if comp in turned_of:
                        own[comp, 1] = tup[turned_of.index(comp), z, r, :]
                        own[comp, -1] = tdn[turned_of.index(comp), z, r, :]
                total = {0: diag[z, r, :], 1: None, -1: None}
                for e, ((dz, dx, dy), comp, sign) in enumerate(OFFSETS):
                    if not 0 <= z + dz < cz:
                        continue
                    near = ten[comp, z + dz, row[dx], :]
                    if comp < 3:
                        value = harmonic(own[comp, dy], near)
                    else:
                        value = own[comp, dy] + near
                    if dx and dy:
                        value = jnp.where(xy_out[dx, dy], zero, value)
                    elif dx and dz:
                        value = jnp.where(x_out[dx], zero, value)
                    elif dy:
                        value = jnp.where(y_out[dy], zero, value)
                    coef[e, z, r, :] = value
                    size = value if comp < 3 else jnp.abs(value)
                    total[dy] = size if total[dy] is None else total[dy] + size
                diag[z, r, :] = total[0]
                dup[z, r, :] = total[1]
                ddn[z, r, :] = total[-1]
                robin[z, r, :] = jnp.zeros((8, LANES), jnp.float32)
            return carry

        lax.fori_loop(0, tiles, coef_tile, 0, unroll=2)

        def gather(ref, t, first):
            r = rows_of(t)
            row = {0: rows_of(t + 1), 1: pl.ds(t * 8 + 9, 8), -1: pl.ds(t * 8 + 7, 8)}
            near = {dx: ref[:, row[dx], :] for dx in (0, 1, -1)}
            out = []
            for z in range(cz):
                acc = {0: first(z), 1: None, -1: None}
                for e, ((dz, dx, dy), comp, sign) in enumerate(OFFSETS):
                    if not 0 <= z + dz < cz:
                        continue
                    term = coef[e, z, r, :] * near[dx][z + dz]
                    if acc[dy] is None:
                        acc[dy] = term if sign == 1 else -term
                    else:
                        acc[dy] = acc[dy] + term if sign == 1 else acc[dy] - term
                out.append(acc[0] + (pltpu.roll(acc[1], LANES - 1, 1) + pltpu.roll(acc[-1], 1, 1)))
            return out

        for plane in ends_z:
            own = [jnp.abs(ten[c, pl.ds(plane, 1), 8:top, :]) for c in (3, 4)]
            robin[pl.ds(plane, 1)] += 2.0 * (own[0] + own[1])

        loads[3].wait()

        def inside_tile(step, t, carry):
            r = rows_of(t)
            if step == 0:
                for z in range(cz):
                    diag[z, r, :] += pltpu.roll(dup[z, r, :], LANES - 1, 1) + pltpu.roll(ddn[z, r, :], 1, 1)
            for z, value in enumerate(gather(va, t, lambda z: None)):
                part[z, r, :] = value
            base[:, r, :] = src_ref[:, r, :]
            return carry

        lax.fori_loop(0, tiles, lambda t, c: inside_tile(0, t, c), 0, unroll=4)

        arrive(0, dirs)

        gid = getters(0, 0)
        glp = getters(0, 1)

        def tensor_get(k):
            def of(which):
                def get(*args):
                    return tensors(gid[which](*args), glp[which](*args), [k])[0]
                return get
            return tuple(of(i) for i in range(6))

        gets = {k: tensor_get(k) for k in range(6)}
        rim_x = {}
        for side, sx in ((0, -1), (1, 1)):
            row = 8 if sx == -1 else top - 1
            own = {k: ten[k, :, row, :] for k in (1, 3, 5)}
            values = [harmonic(own[1], near_x(gets[1], sx, "")[0])]
            near = near_x(gets[3], sx, "z")
            for dz, got, ok in ((1, near[1], sub_x < last), (-1, near[2], sub_x > 0)):
                values.append(jnp.where(ok, (dz * sx) * (own[3] + got), zero))
            near = near_x(gets[5], sx, "y")
            for dy, got in ((1, near[1]), (-1, near[2])):
                values.append((sx * dy) * (own[5] + got))
            size = None
            for j, value in enumerate(values):
                rcx[side, j] = value
                size = jnp.abs(value) if size is None else size + jnp.abs(value)
            rim_x[sx] = size

        own = dict(zip((2, 4, 5), tensors(yfull[0], yfull[1], (2, 4, 5))))
        sy = jnp.where(even, jnp.float32(1), jnp.float32(-1))
        values = [harmonic(own[2], near_y(gets[2], "", 0)[0])]
        near = near_y(gets[4], "z", 1)
        for dz, got, ok in ((1, near[1], sub_y < 2 * last), (-1, near[2], sub_y >= 2)):
            values.append(jnp.where(ok, dz * sy * (own[4] + got), zero))
        near = near_y(gets[5], "x", 2)
        for dx, got, ok in ((1, near[1], lane_y < LANES - 1), (-1, near[2], lane_y > 0)):
            values.append(jnp.where(ok, dx * sy * (own[5] + got), zero))
        size = None
        for j, value in enumerate(values):
            rcy[j] = value
            size = jnp.abs(value) if size is None else size + jnp.abs(value)
        pack[0 : 2 * cz, :] = size
        pack_sides(gets[4])
        turned = pack[...].T
        turn[0] = turned
        rim_z = {}
        for k in range(len(kinds)):
            sz, face = steps[k][:2]
            sign = jnp.float32(sz) if isinstance(sz, int) else sz.astype(jnp.float32)
            own = {c: ten[c, pl.ds(face, 1), 8:top, :][0] for c in (0, 3, 4)}
            values = [harmonic(own[0], near_z(gets[0], k, "", None)[0])]
            near = near_z(gets[3], k, "x", None)
            for dx, got in ((1, near[1]), (-1, near[2])):
                values.append((sign * dx) * (own[3] + got))
            near = near_z(gets[4], k, "y", turned)
            for dy, got in ((1, near[1]), (-1, near[2])):
                values.append((sign * dy) * (own[4] + got))
            size = None
            for j, value in enumerate(values):
                rcz[k, j] = value
                size = jnp.abs(value) if size is None else size + jnp.abs(value)
            rim_z[k] = size
        add_xz(robin, lambda sx: rim_x[sx], lambda k: rim_z[k])

        def weigh(weights, values):
            out = None
            for j, value in enumerate(values):
                term = weights(j) * value
                out = term if out is None else out + term
            return out

        def corner(stage, q, sx):
            get, side = getters(stage, q), (sx + 1) // 2
            return rcx[side, 3] * jnp.where(lane_x == LANES - 1, get[5](sx, 1), zero) + rcx[
                side, 4
            ] * jnp.where(lane_x == 0, get[5](sx, -1), zero)

        def spread_pressure(dest, stage, q):
            get = getters(stage, q)
            pack[0 : 2 * cz, :] = weigh(lambda j: rcy[j], near_y(get, "zx", 3))
            pack_sides(get)
            turned = pack[...].T
            turn[1] = turned
            add_xz(
                dest,
                lambda sx: weigh(lambda j: rcx[(sx + 1) // 2, j], near_x(get, sx, "zy", stage == 0)),
                lambda k: weigh(lambda j: rcz[k, j], near_z(get, k, "xy", turned)),
            )

        def sides_of(step, t):
            r = rows_of(t)
            rims = [at_ends(turn.at[0], r, z) for z in range(cz)] if step == 0 else None
            return rims, [at_ends(turn.at[1], r, z) for z in range(cz)]

        def first_tile(step, t, sides):
            r = rows_of(t)
            mid = rows_of(t + 1)
            rims, flows = sides
            for z in range(cz):
                if step == 0:
                    rim = robin[z, r, :] + rims[z]
                    total = diag[z, r, :] + rim
                    rim = ROBIN * rim
                    weight = 1.0 / (total + rim)
                    diag[z, r, :] = total
                    robin[z, r, :] = rim
                    inv[z, r, :] = weight
                else:
                    rim = robin[z, r, :]
                    weight = inv[z, r, :]
                fixed = base[z, r, :] + flows[z] + rim * va[z, mid, :]
                base[z, r, :] = fixed
                vb[z, mid, :] = (fixed + part[z, r, :]) * weight

        def second_tile(t):
            r = rows_of(t)
            got = gather(vb, t, lambda z: base[z, r, :])
            for z, value in enumerate(got):
                va[z, rows_of(t + 1), :] = value * inv[z, r, :]

        def mix_sent(t):
            mixed[0, rows_of(t), :] = mix(va[:, rows_of(t + 1), :])

        group = 2
        count = tiles // group

        def work(step, mix_at, second_at, first_at):
            of = lambda g: [] if g is None else [g * group + i for i in range(group)]
            for t in of(mix_at):
                mix_sent(t)
            sides = [(t, sides_of(step, t)) for t in of(first_at)]
            for t in of(second_at):
                second_tile(t)
            for t, got in sides:
                first_tile(step, t, got)

        def sweeps(step, before_ends):
            for g in range(3):
                work(step, None, None, g)
            work(step, None, 1, 3)

            def body(g, carry):
                work(step, g - 1, g, g + 2)
                return carry

            lax.fori_loop(2, count - 2, body, 0)
            work(step, count - 3, count - 2, None)
            before_ends()
            work(step, count - 2, count - 1, None)
            work(step, count - 1, 0, None)
            work(step, 0, None, None)

        def residual_tile(t, carry):
            r = rows_of(t)
            mid = rows_of(t + 1)
            for z, value in enumerate(
                gather(va, t, lambda z: src_ref[z, r, :] - diag[z, r, :] * va[z, mid, :])
            ):
                res_ref[z, r, :] = value
            return carry

        for step in range(ITERS):
            spread_pressure(base, step, 2 if step == 0 else 0)

            def before_ends(step=step):
                if step == 0:
                    return
                arrive(step, xy_dirs)
                for sx, row in ((-1, 0), (1, cx - 1)):
                    more = corner(step, 0, sx)
                    base[:, row, :] += more
                    vb[:, 8 + row, :] += more * inv[:, row, :]

            sweeps(step, before_ends)
            xs, ys = stages[step + 1][:2]
            for side, x in ((0, 8), (1, top - 1)):
                xs[side, 0] = va[:, x, :]
            unweave(0, ys)
            start(step + 1, dirs)
            if step == ITERS - 1:
                lax.fori_loop(0, tiles, residual_tile, 0, unroll=4)
            else:
                lax.fori_loop(0, tiles, lambda t, c: inside_tile(step + 1, t, c), 0, unroll=4)
            if step == 0:
                sent(step)
            sent(step + 1)
            arrive(step + 1, [d for d in dirs if d not in xy_dirs])
        spread_pressure(res_ref, ITERS, 0)
        arrive(ITERS, xy_dirs)
        for sx, row in ((-1, 0), (1, cx - 1)):
            res_ref[:, row, :] += corner(ITERS, 0, sx)
        turn_ref[...] = turn[1]

    return kernel


def write_out(pressure, residual, turned, out_hbm, res_hbm, sem):
    cz, cx, cy = residual.shape
    put_out = pltpu.make_async_copy(pressure.at[:, pl.ds(8, cx), :], out_hbm, sem.at[0])
    put_out.start()
    lane = lax.broadcasted_iota(jnp.int32, (8, LANES), 1)
    ends = jnp.logical_or(lane == 0, lane == LANES - 1)

    def tile(t, carry):
        r = pl.ds(pl.multiple_of(t * 8, 8), 8)
        side = turned[r, :]
        for z in range(cz):
            residual[z, r, :] += jnp.where(ends, pltpu.roll(side, LANES - 1 - 2 * z, 1), 0.0)
        return carry

    lax.fori_loop(0, cx // 8, tile, 0, unroll=8)
    put_res = pltpu.make_async_copy(residual, res_hbm, sem.at[1])
    put_res.start()
    put_out.wait()
    put_res.wait()


def solution(mesh):
    sizes = tuple(mesh.shape[a] for a in AXES)

    def per_device(rock_ids, log_perm, rock_diagonal, rock_shear, rock_storage, source, pressure_start):
        shape = rock_ids.shape
        cz, cx, cy = shape
        classes = rock_storage.shape[0]
        f32 = jnp.float32
        padded = (cz, cx + 16, cy)
        groups = directions(z_kinds(sizes[0]))
        many = [max(len(group), 1) for group in groups]
        faces = many[5]

        def exchange(nq):
            return [
                pltpu.VMEM((2, nq, cz, cy), f32),
                pltpu.VMEM((2, nq, cz, cx), f32),
                pltpu.VMEM((many[0], cz, cy), f32),
                pltpu.VMEM((many[1], nq, cz, cx), f32),
                pltpu.VMEM((many[2], nq, cz, cy), f32),
                pltpu.VMEM((many[3], nq, 1, cx), f32),
                pltpu.VMEM((many[4], nq, 1, cy), f32),
                pltpu.VMEM((faces, nq, cx, cy), f32),
            ]

        hbm = pl.BlockSpec(memory_space=pltpu.HBM)
        smem = pl.BlockSpec(memory_space=pltpu.SMEM)
        vmem = pl.BlockSpec(memory_space=pltpu.VMEM)
        count = sum(len(group) for group in groups)
        kept = pl.pallas_call(
            make_kernel(sizes, shape, classes),
            out_shape=(pltpu.VMEM(padded, f32), pltpu.VMEM(shape, f32), pltpu.VMEM((cx, cy), f32)),
            in_specs=[hbm, hbm, smem, smem, smem, hbm, hbm],
            out_specs=(vmem, vmem, vmem),
            scratch_shapes=[
                pltpu.VMEM((7, -(-classes // 8) * 8, cy), f32),
                pltpu.VMEM((6,) + padded, f32),
                pltpu.VMEM((3, cz, cx + 8, cy), f32),
                pltpu.VMEM((3, cz, cx + 8, cy), f32),
                pltpu.VMEM((cz, cx + 8, cy), f32),
                pltpu.VMEM((cz, cx + 8, cy), f32),
                pltpu.VMEM(padded, f32),
                pltpu.VMEM((len(OFFSETS), cz, cx + 8, cy), f32),
            ]
            + [pltpu.VMEM(shape, f32)] * 5
            + [
                pltpu.VMEM((3, cx, cy), f32),
                pltpu.VMEM((cx, cy), f32),
                pltpu.VMEM((2, cx, cy), f32),
                pltpu.VMEM((cx + 16, cy), f32),
                pltpu.VMEM((2, 5, cz, cy), f32),
                pltpu.VMEM((5, 2 * cz, cx), f32),
                pltpu.VMEM((faces, 5, cx, cy), f32),
                pltpu.VMEM((faces, 3, cx, cy), f32),
                pltpu.VMEM((2, cz, cy), f32),
                pltpu.VMEM((2, 2 * cz, cx), f32),
                pltpu.VMEM((3, 2 * cz, cx), f32),
                pltpu.VMEM((4, 2 * cz, cx), f32),
            ]
            + exchange(3)
            + exchange(1)
            + exchange(1)
            + [pltpu.VMEM(shape, jnp.int32)]
            + [pltpu.VMEM(shape, f32)] * 2
            + [
                pltpu.SemaphoreType.DMA((4,)),
                pltpu.SemaphoreType.DMA((ITERS + 1, count)),
                pltpu.SemaphoreType.DMA((ITERS + 1, count)),
            ],
            compiler_params=pltpu.CompilerParams(
                collective_id=0, has_side_effects=True, vmem_limit_bytes=61440 * 1024
            ),
            name="schwarz",
        )(rock_ids, log_perm, rock_diagonal.T, rock_shear.T, rock_storage, source, pressure_start)
        return pl.pallas_call(
            write_out,
            out_shape=(jax.ShapeDtypeStruct(shape, f32), jax.ShapeDtypeStruct(shape, f32)),
            in_specs=[vmem, vmem, vmem],
            out_specs=(hbm, hbm),
            scratch_shapes=[pltpu.SemaphoreType.DMA((2,))],
            name="write_out",
        )(*(pltpu.with_memory_space_constraint(k, pltpu.VMEM) for k in kept))

    block = P("gz", "gx", "gy")
    return jax.shard_map(
        per_device,
        mesh=mesh,
        in_specs=(block, block, P(), P(), P(), block, block),
        out_specs=(block, block),
        check_vma=False,
    )
```

```python
import jax
import jax.numpy as jnp
from jax import lax
from jax.experimental import pallas as pl
from jax.experimental.pallas import tpu as pltpu
from jax.sharding import PartitionSpec as P

ITERS = 2
SWEEPS = 2
ROBIN = 0.5
AXES = ("gz", "gx", "gy")
LANES = 128
FACE = 2.0
EDGE = 0.125


def build_offsets():
    found = []
    for axis in range(3):
        for sign in (1, -1):
            vector = [0, 0, 0]
            vector[axis] = sign
            found.append((tuple(vector), axis, 1))
    for first, second, comp in ((0, 1, 3), (0, 2, 4), (1, 2, 5)):
        for sign_a in (1, -1):
            for sign_b in (1, -1):
                vector = [0, 0, 0]
                vector[first] = sign_a
                vector[second] = sign_b
                found.append((tuple(vector), comp, sign_a * sign_b))
    return found


OFFSETS = build_offsets()


def z_kinds(blocks):
    if blocks < 2:
        return ()
    return ("other",) if blocks == 2 else (1, -1)


def directions(kinds):
    xy_dirs = [(0, dx, dy) for dx in (1, -1) for dy in (1, -1)]
    x_dirs = [(0, dx, 0) for dx in (1, -1)]
    y_dirs = [(0, 0, dy) for dy in (1, -1)]
    zx_dirs = [(k + 1, dx, 0) for k in range(len(kinds)) for dx in (1, -1)]
    zy_dirs = [(k + 1, 0, dy) for k in range(len(kinds)) for dy in (1, -1)]
    z_dirs = [(k + 1, 0, 0) for k in range(len(kinds))]
    return xy_dirs, y_dirs, x_dirs, zy_dirs, zx_dirs, z_dirs


def make_kernel(sizes, shape, classes):
    cz, cx, cy = shape
    tiles = cx // 8
    top = cx + 8
    last = cz - 1
    kinds = z_kinds(sizes[0])
    groups = directions(kinds)
    xy_dirs, y_dirs, x_dirs, zy_dirs, zx_dirs, z_dirs = groups
    dirs = [d for group in groups for d in group]
    slot = {d: i for i, d in enumerate(dirs)}
    place = {d: i for group in groups for i, d in enumerate(group)}

    def opposite(d):
        k = d[0]
        if k and len(kinds) == 2:
            k = 3 - k
        return (k, -d[1], -d[2])

    def kernel(
        ids_hbm, lp_hbm, dia_hbm, she_hbm, sto_hbm, src_hbm, p_hbm,
        va, res_ref, turn_ref,
        tab, ten, tup, tdn, dup, ddn, vb,
        coef, diag, robin, inv, base, part, mixed, pack, turn, zpad,
        rcx, rcy, rcz, rzx, rzy,
        zs1, xc1, yfull, tall, woven,
        xs1, ys1, xyl1, yl1, xl1, zyl1, zxl1, zl1,
        xs2, ys2, xyl2, yl2, xl2, zyl2, zxl2, zl2,
        xs3, ys3, xyl3, yl3, xl3, zyl3, zxl3, zl3,
        dia_ref, she_ref, sto_ref, ids_ref, lp_ref, src_ref, load_sem,
        send_sem, recv_sem,
    ):
        whole = pl.ds(8, cx)
        loads = [
            pltpu.make_async_copy(a, b, load_sem.at[i])
            for i, (a, b) in enumerate(
                (
                    (ids_hbm, ids_ref), (lp_hbm, lp_ref), (p_hbm, va.at[:, whole, :]), (src_hbm, src_ref),
                    (dia_hbm, dia_ref), (she_hbm, she_ref), (sto_hbm, sto_ref),
                )
            )
        ]
        here = [lax.axis_index(a) for a in AXES]
        if len(kinds) == 1:
            steps = [(1 - 2 * here[0], last * (1 - here[0]), last * here[0])]
        else:
            steps = [(k, last if k == 1 else 0, 0 if k == 1 else last) for k in kinds]

        ends_z = [(0, last), [s[2] for s in steps], ()][len(kinds)]

        def exists(d):
            ok = None
            terms = []
            if d[0] and len(kinds) == 2:
                terms.append(here[0] < sizes[0] - 1 if kinds[d[0] - 1] == 1 else here[0] > 0)
            for axis in (1, 2):
                if d[axis] == 1:
                    terms.append(here[axis] < sizes[axis] - 1)
                elif d[axis] == -1:
                    terms.append(here[axis] > 0)
            for term in terms:
                ok = term if ok is None else jnp.logical_and(ok, term)
            return ok

        there = {d: exists(d) for d in dirs}

        def when(ok):
            if ok is None:
                return lambda f: f()
            return pl.when(ok)

        def target(d):
            out = {AXES[i]: here[i] + d[i] for i in (1, 2) if d[i] != 0}
            if d[0]:
                out[AXES[0]] = here[0] + steps[d[0] - 1][0]
            return out

        barrier = pltpu.get_barrier_semaphore()

        expected = jnp.int32(0)
        for d in dirs:
            @when(there[d])
            def _(d=d):
                pl.semaphore_signal(
                    barrier, inc=1, device_id=target(d),
                    device_id_type=pl.DeviceIdType.MESH,
                )
            expected = expected + (1 if there[d] is None else there[d].astype(jnp.int32))

        for load in loads[4:] + loads[:4]:
            load.start()

        stages = (
            (xs1, ys1, xyl1, yl1, xl1, zyl1, zxl1, zl1),
            (xs2, ys2, xyl2, yl2, xl2, zyl2, zxl2, zl2),
            (xs3, ys3, xyl3, yl3, xl3, zyl3, zxl3, zl3),
        )

        def land(stage, d):
            kind = [d in group for group in groups].index(True)
            return stages[stage][2 + kind].at[place[d]]

        for d in dirs:
            if there[opposite(d)] is None:
                continue

            @pl.when(jnp.logical_not(there[opposite(d)]))
            def _(d=d):
                for stage in range(ITERS + 1):
                    ref = land(stage, d)
                    ref[...] = jnp.zeros_like(ref)

        lane = lax.broadcasted_iota(jnp.int32, (cx, LANES), 1)
        lane_t = lax.broadcasted_iota(jnp.int32, (8, LANES), 1)

        def copy_of(stage, d):
            xs, ys = stages[stage][:2]
            x_side, y_side = (d[1] + 1) // 2, (d[2] + 1) // 2
            face = pl.ds(steps[d[0] - 1][1], 1) if d[0] else None
            if d[1] and d[2]:
                src = xc1.at[x_side] if stage == 0 else xs.at[x_side, 0]
            elif d[1]:
                src = xs.at[x_side, :, face, :] if d[0] else xs.at[x_side]
            elif d[2]:
                src = ys.at[y_side, :, face, :] if d[0] else ys.at[y_side]
            else:
                src = zs1.at[d[0] - 1] if stage == 0 else va.at[face, whole, :]
            dst = land(stage, d)
            return pltpu.make_async_remote_copy(
                src_ref=src, dst_ref=dst,
                send_sem=send_sem.at[stage, slot[d]],
                recv_sem=recv_sem.at[stage, slot[d]],
                device_id=target(d), device_id_type=pl.DeviceIdType.MESH,
            )

        def start(stage, some):
            for d in some:
                @when(there[d])
                def _(d=d):
                    copy_of(stage, d).start()

        def arrive(stage, some):
            for d in some:
                @when(there[opposite(d)])
                def _(d=d):
                    copy_of(stage, d).wait_recv()

        def sent(stage):
            for d in dirs:
                @when(there[d])
                def _(d=d):
                    copy_of(stage, d).wait_send()

        def getters(stage, q):
            def got(d):
                return land(stage, opposite(d))

            def get_z(k):
                return got((k + 1, 0, 0))[q]

            def get_x(sx):
                return got((0, sx, 0))[q]

            def get_y(sy):
                return got((0, 0, sy))[q]

            def get_zx(k, sx):
                return got((k + 1, sx, 0))[q]

            def get_zy(k, sy):
                return got((k + 1, 0, sy))[q]

            def get_xy(sx, sy):
                if sy == 1:
                    shift = LANES - 2 - 2 * q if stage == 0 else LANES - 1
                else:
                    shift = (LANES - 2 * q) % LANES if stage == 0 else 1
                held = got((0, sx, sy))[...]
                return pltpu.roll(held, shift, 1) if shift else held

            return get_z, get_x, get_y, get_zx, get_zy, get_xy

        lane_x = lax.broadcasted_iota(jnp.int32, (cz, LANES), 1)
        sub_x = lax.broadcasted_iota(jnp.int32, (cz, LANES), 0)
        lane_y = lax.broadcasted_iota(jnp.int32, (2 * cz, LANES), 1)
        sub_y = lax.broadcasted_iota(jnp.int32, (2 * cz, LANES), 0)
        even = sub_y % 2 == 0
        zero = jnp.float32(0)

        def near_x(get, sx, names, corners=True):
            plain = get[1](sx)
            out = [plain]
            if "z" in names:
                out.append(jnp.where(sub_x < last, pltpu.roll(plain, cz - 1, 0), zero))
                out.append(jnp.where(sub_x > 0, pltpu.roll(plain, 1, 0), zero))
            if "y" in names:
                ahead, behind = pltpu.roll(plain, LANES - 1, 1), pltpu.roll(plain, 1, 1)
                out.append(jnp.where(lane_x == LANES - 1, get[5](sx, 1) if corners else zero, ahead))
                out.append(jnp.where(lane_x == 0, get[5](sx, -1) if corners else zero, behind))
            return out

        def near_y(get, names, at):
            get_y = get[2]
            woven[at, pl.ds(0, cz, 2), :] = get_y(1)
            woven[at, pl.ds(1, cz, 2), :] = get_y(-1)
            plain = woven[at]
            out = [plain]
            if "z" in names:
                out.append(jnp.where(sub_y < 2 * last, pltpu.roll(plain, 2 * cz - 2, 0), zero))
                out.append(jnp.where(sub_y >= 2, pltpu.roll(plain, 2, 0), zero))
            if "x" in names:
                ahead, behind = pltpu.roll(plain, LANES - 1, 1), pltpu.roll(plain, 1, 1)
                out.append(jnp.where(lane_y < LANES - 1, ahead, zero))
                out.append(jnp.where(lane_y > 0, behind, zero))
            return out

        row = lax.broadcasted_iota(jnp.int32, (cx, LANES), 0)

        def near_z(plain, names):
            out = [plain]
            if "x" in names:
                zpad[8:top, :] = plain
                out.append(zpad[9 : top + 1, :])
                out.append(zpad[7 : top - 1, :])
            if "y" in names:
                out.append(pltpu.roll(plain, LANES - 1, 1))
                out.append(pltpu.roll(plain, 1, 1))
            return out

        def harmonic(own, near):
            return own * near / (own + near)

        def rows_of(t):
            return pl.ds(pl.multiple_of(t * 8, 8), 8)

        ends = jnp.logical_or(lane_t == 0, lane_t == LANES - 1)

        def at_ends(ref, r, z):
            return jnp.where(ends, pltpu.roll(ref[r, :], LANES - 1 - 2 * z, 1), zero)

        def add_x(dest, of_x):
            for sx, at in ((-1, 0), (1, cx - 1)):
                dest[:, at, :] += of_x(sx)

        def add_plane(dest, k, value):
            dest[pl.ds(steps[k][1], 1), 0:cx, :] += value[None]

        def add_row(dest, k, at, value):
            dest[pl.ds(steps[k][1], 1), at : at + 1, :] += value[None]

        def mix(planes):
            out = None
            for z in range(cz):
                moved = pltpu.roll(planes[z], 2 * z + 1, 1)
                out = moved if out is None else jnp.where((lane_t // 2) == z, moved, out)
            return out

        pack[...] = jnp.zeros_like(pack)
        zpad[0:8, :] = jnp.zeros((8, LANES), jnp.float32)
        zpad[top : top + 8, :] = jnp.zeros((8, LANES), jnp.float32)
        for ref in (va, vb):
            for lo in (0, top):
                ref[:, lo : lo + 8, :] = jnp.zeros((cz, 8, LANES), jnp.float32)
        for lo in (0, top):
            ten[:, :, lo : lo + 8, :] = jnp.zeros((6, cz, 8, LANES), jnp.float32)

        def code_of(ids):
            return (ids + 1).astype(jnp.float32)

        for load in loads[:3]:
            load.wait()

        for k in range(len(kinds)):
            face = pl.ds(steps[k][1], 1)
            zs1[k, 0:1] = code_of(ids_ref[face])
            zs1[k, 1:2] = lp_ref[face]
            zs1[k, 2:3] = va[face, whole, :]
        for side, x in ((0, 0), (1, cx - 1)):
            xs1[side, 0] = code_of(ids_ref[:, x, :])
            xs1[side, 1] = lp_ref[:, x, :]
            xs1[side, 2] = va[:, 8 + x, :]

        def mix_tile(t, carry):
            r = rows_of(t)
            mixed[0, r, :] = mix(code_of(ids_ref[:, r, :]))
            mixed[1, r, :] = mix(lp_ref[:, r, :])
            mixed[2, r, :] = mix(va[:, rows_of(t + 1), :])
            return carry

        def unweave(q, ys):
            tall[q] = mixed[q].T[: 2 * cz]
            ys[1, q] = tall[q, pl.ds(0, cz, 2), :]
            ys[0, q] = tall[q, pl.ds(1, cz, 2), :]

        lax.fori_loop(0, tiles, mix_tile, 0, unroll=4)
        for q in range(3):
            unweave(q, ys1)
        for q in range(2):
            yfull[q] = tall[q]
        for side in range(2):
            held = None
            for q in range(3):
                moved = pltpu.roll(xs1[side, q], 2 * q + 1, 1)
                held = moved if held is None else jnp.where((lane_x // 2) == q, moved, held)
            xc1[side] = held

        pl.semaphore_wait(barrier, expected)
        start(0, dirs)

        for load in loads[4:]:
            load.wait()
        high = tab.shape[1]
        on_class = lax.broadcasted_iota(jnp.int32, (high, classes), 0) == lax.broadcasted_iota(
            jnp.int32, (high, classes), 1
        )

        def down(values):
            spread = jnp.where(on_class, jnp.broadcast_to(values, (high, classes)), zero)
            return jnp.broadcast_to(jnp.sum(spread, axis=1, keepdims=True), (high, LANES))

        cols = [down(dia_ref[k : k + 1, :]) for k in range(3)]
        for k, (a, b) in enumerate(((0, 1), (0, 2), (1, 2))):
            tab[3 + k] = EDGE * down(she_ref[k : k + 1, :]) * jnp.sqrt(cols[a] * cols[b])
        for k in range(3):
            tab[k] = FACE * cols[k]
        tab[6] = down(sto_ref[...])


        def pick(ids, comps):
            count = ids.shape[0]
            if count < 8:
                ids = jnp.concatenate([ids] * (8 // count), axis=0)
            found = []
            for k in comps:
                parts = []
                for at in range(0, ids.shape[0], 8):
                    some = ids[at : at + 8]
                    if classes <= 8:
                        part_ = jnp.take_along_axis(tab[k], some, axis=0, mode="promise_in_bounds")
                    else:
                        part_ = jnp.zeros(some.shape, jnp.float32)
                        for c in range(classes):
                            part_ = jnp.where(some == c, tab[k, c : c + 1, :], part_)
                    parts.append(part_)
                got = parts[0] if len(parts) == 1 else jnp.concatenate(parts, axis=0)
                found.append(got[:count])
            return found

        def tensors(code, perm, comps):
            ids = jnp.maximum(code - 1.0, 0.0).astype(jnp.int32)
            gain = jnp.where(code > 0.5, jnp.exp(perm), zero)
            return [f * gain for f in pick(ids, comps)]

        turned_of = (2, 4, 5)

        def tensor_tile(t, carry):
            r = rows_of(t)
            out = rows_of(t + 1)
            for z in range(cz):
                gain = jnp.exp(lp_ref[z, r, :])
                found = pick(ids_ref[z, r, :], range(7))
                diag[z, r, :] = found[6]
                for k in range(6):
                    value = found[k] * gain
                    ten[k, z, out, :] = value
                    if k in turned_of:
                        at = turned_of.index(k)
                        tup[at, z, r, :] = pltpu.roll(value, 1, 1)
                        tdn[at, z, r, :] = pltpu.roll(value, LANES - 1, 1)
            return carry

        lax.fori_loop(0, tiles, tensor_tile, 0, unroll=2)

        row_t = lax.broadcasted_iota(jnp.int32, (8, LANES), 0)

        def coef_tile(t, carry):
            r = rows_of(t)
            mid = rows_of(t + 1)
            row = {0: mid, 1: pl.ds(t * 8 + 9, 8), -1: pl.ds(t * 8 + 7, 8)}
            x_out = {1: row_t + t * 8 == cx - 1, -1: row_t + t * 8 == 0}
            y_out = {1: lane_t == 0, -1: lane_t == LANES - 1}
            xy_out = {(dx, dy): jnp.logical_or(x_out[dx], y_out[dy]) for dx in (1, -1) for dy in (1, -1)}
            for z in range(cz):
                own = {}
                for comp in range(6):
                    own[comp, 0] = ten[comp, z, mid, :]
                    if comp in turned_of:
                        own[comp, 1] = tup[turned_of.index(comp), z, r, :]
                        own[comp, -1] = tdn[turned_of.index(comp), z, r, :]
                total = {0: diag[z, r, :], 1: None, -1: None}
                for e, ((dz, dx, dy), comp, sign) in enumerate(OFFSETS):
                    if not 0 <= z + dz < cz:
                        continue
                    near = ten[comp, z + dz, row[dx], :]
                    if comp < 3:
                        value = harmonic(own[comp, dy], near)
                    else:
                        value = own[comp, dy] + near
                    if dx and dy:
                        value = jnp.where(xy_out[dx, dy], zero, value)
                    elif dx and dz:
                        value = jnp.where(x_out[dx], zero, value)
                    elif dy:
                        value = jnp.where(y_out[dy], zero, value)
                    coef[e, z, r, :] = value
                    size = value if comp < 3 else jnp.abs(value)
                    total[dy] = size if total[dy] is None else total[dy] + size
                diag[z, r, :] = total[0]
                dup[z, r, :] = total[1]
                ddn[z, r, :] = total[-1]
                robin[z, r, :] = jnp.zeros((8, LANES), jnp.float32)
            return carry

        lax.fori_loop(0, tiles, coef_tile, 0, unroll=2)

        def gather(ref, t, first):
            r = rows_of(t)
            row = {0: rows_of(t + 1), 1: pl.ds(t * 8 + 9, 8), -1: pl.ds(t * 8 + 7, 8)}
            near = {dx: ref[:, row[dx], :] for dx in (0, 1, -1)}
            out = []
            for z in range(cz):
                acc = {0: first(z), 1: None, -1: None}
                for e, ((dz, dx, dy), comp, sign) in enumerate(OFFSETS):
                    if not 0 <= z + dz < cz:
                        continue
                    term = coef[e, z, r, :] * near[dx][z + dz]
                    if acc[dy] is None:
                        acc[dy] = term if sign == 1 else -term
                    else:
                        acc[dy] = acc[dy] + term if sign == 1 else acc[dy] - term
                out.append(acc[0] + (pltpu.roll(acc[1], LANES - 1, 1) + pltpu.roll(acc[-1], 1, 1)))
            return out

        for plane in ends_z:
            own = [jnp.abs(ten[c, pl.ds(plane, 1), 8:top, :]) for c in (3, 4)]
            robin[pl.ds(plane, 1), 0:cx, :] += 2.0 * (own[0] + own[1])

        loads[3].wait()

        def inside_tile(step, t, carry):
            r = rows_of(t)
            if step == 0:
                for z in range(cz):
                    diag[z, r, :] += pltpu.roll(dup[z, r, :], LANES - 1, 1) + pltpu.roll(ddn[z, r, :], 1, 1)
            for z, value in enumerate(gather(va, t, lambda z: None)):
                part[z, r, :] = value
            base[:, r, :] = src_ref[:, r, :]
            return carry

        lax.fori_loop(0, tiles, lambda t, c: inside_tile(0, t, c), 0, unroll=4)

        rest = [d for d in dirs if d not in z_dirs]
        late = [d for d in rest if d not in xy_dirs]
        signs = [jnp.float32(p[0]) if isinstance(p[0], int) else p[0].astype(jnp.float32) for p in steps]

        def weigh(weights, values):
            out = None
            for j, value in enumerate(values):
                term = weights(j) * value
                out = term if out is None else out + term
            return out

        def early_pressure(dest, stage, q):
            get_z = getters(stage, q)[0]
            for k in range(len(kinds)):
                add_plane(dest, k, weigh(lambda j: rcz[k, j], near_z(get_z(k), "xy")))

        arrive(0, z_dirs)
        for k in range(len(kinds)):
            face = steps[k][1]
            own = {c: ten[c, pl.ds(face, 1), 8:top, :][0] for c in (0, 3, 4)}
            there_z = dict(zip((0, 3, 4), tensors(getters(0, 0)[0](k), getters(0, 1)[0](k), (0, 3, 4))))
            values = [harmonic(own[0], there_z[0])]
            near = near_z(there_z[3], "x")
            for dx, got, out in ((1, near[1], row == cx - 1), (-1, near[2], row == 0)):
                values.append(jnp.where(out, zero, (signs[k] * dx) * (own[3] + got)))
            near = near_z(there_z[4], "y")
            for dy, got, out in ((1, near[1], lane == LANES - 1), (-1, near[2], lane == 0)):
                values.append(jnp.where(out, zero, (signs[k] * dy) * (own[4] + got)))
            size = None
            for j, value in enumerate(values):
                rcz[k, j] = value
                size = jnp.abs(value) if size is None else size + jnp.abs(value)
            add_plane(robin, k, size)
        early_pressure(base, 0, 2)
        arrive(0, rest)

        gid = getters(0, 0)
        glp = getters(0, 1)

        def tensor_get(k):
            def of(which):
                def get(*args):
                    return tensors(gid[which](*args), glp[which](*args), [k])[0]
                return get
            return tuple(of(i) for i in range(6))

        gets = {k: tensor_get(k) for k in range(6)}
        rim_x = {}
        for side, sx in ((0, -1), (1, 1)):
            row = 8 if sx == -1 else top - 1
            own = {k: ten[k, :, row, :] for k in (1, 3, 5)}
            values = [harmonic(own[1], near_x(gets[1], sx, "")[0])]
            near = near_x(gets[3], sx, "z")
            for dz, got, ok in ((1, near[1], sub_x < last), (-1, near[2], sub_x > 0)):
                values.append(jnp.where(ok, (dz * sx) * (own[3] + got), zero))
            near = near_x(gets[5], sx, "y")
            for dy, got in ((1, near[1]), (-1, near[2])):
                values.append((sx * dy) * (own[5] + got))
            size = None
            for j, value in enumerate(values):
                rcx[side, j] = value
                size = jnp.abs(value) if size is None else size + jnp.abs(value)
            rim_x[sx] = size

        own = dict(zip((2, 4, 5), tensors(yfull[0], yfull[1], (2, 4, 5))))
        sy = jnp.where(even, jnp.float32(1), jnp.float32(-1))
        values = [harmonic(own[2], near_y(gets[2], "", 0)[0])]
        near = near_y(gets[4], "z", 1)
        for dz, got, ok in ((1, near[1], sub_y < 2 * last), (-1, near[2], sub_y >= 2)):
            values.append(jnp.where(ok, dz * sy * (own[4] + got), zero))
        near = near_y(gets[5], "x", 2)
        for dx, got, ok in ((1, near[1], lane_y < LANES - 1), (-1, near[2], lane_y > 0)):
            values.append(jnp.where(ok, dx * sy * (own[5] + got), zero))
        size = None
        for j, value in enumerate(values):
            rcy[j] = value
            size = jnp.abs(value) if size is None else size + jnp.abs(value)
        pack[0 : 2 * cz, :] = size
        woven[4] = own[4]
        for k in range(len(kinds)):
            face = pl.ds(2 * steps[k][1], 2)
            for at, sy_, code_row in ((0, 1, gets[4][4](k, 1)), (1, -1, gets[4][4](k, -1))):
                value = (signs[k] * sy_) * (woven[4, pl.ds(2 * steps[k][1] + at, 1), :] + code_row)
                rzy[k, at : at + 1, :] = value
                pack[pl.ds(2 * steps[k][1] + at, 1), :] += jnp.abs(value)
            for side, sx, at in ((0, -1, 0), (1, 1, cx - 1)):
                mine = ten[3, pl.ds(steps[k][1], 1), 8 + at : 9 + at, :][0]
                value = (signs[k] * sx) * (mine + gets[3][3](k, sx))
                rzx[k, side : side + 1, :] = value
                add_row(robin, k, at, jnp.abs(value))
        turn[0] = pack[...].T
        add_x(robin, lambda sx: rim_x[sx])

        def corner(stage, q, sx):
            get, side = getters(stage, q), (sx + 1) // 2
            return rcx[side, 3] * jnp.where(lane_x == LANES - 1, get[5](sx, 1), zero) + rcx[
                side, 4
            ] * jnp.where(lane_x == 0, get[5](sx, -1), zero)

        def spread_pressure(dest, stage, q):
            get = getters(stage, q)
            pack[0 : 2 * cz, :] = weigh(lambda j: rcy[j], near_y(get, "zx", 3))
            for k in range(len(kinds)):
                for at, sy_ in ((0, 1), (1, -1)):
                    pack[pl.ds(2 * steps[k][1] + at, 1), :] += rzy[k, at : at + 1, :] * get[4](k, sy_)
            turn[1] = pack[...].T
            for k in range(len(kinds)):
                for side, sx, at in ((0, -1, 0), (1, 1, cx - 1)):
                    add_row(dest, k, at, rzx[k, side : side + 1, :] * get[3](k, sx))
            add_x(dest, lambda sx: weigh(lambda j: rcx[(sx + 1) // 2, j], near_x(get, sx, "zy", stage == 0)))

        def sides_of(step, t):
            r = rows_of(t)
            rims = [at_ends(turn.at[0], r, z) for z in range(cz)] if step == 0 else None
            return rims, [at_ends(turn.at[1], r, z) for z in range(cz)]

        def first_tile(step, t, sides):
            r = rows_of(t)
            mid = rows_of(t + 1)
            rims, flows = sides
            for z in range(cz):
                if step == 0:
                    rim = robin[z, r, :] + rims[z]
                    total = diag[z, r, :] + rim
                    rim = ROBIN * rim
                    weight = 1.0 / (total + rim)
                    diag[z, r, :] = total
                    robin[z, r, :] = rim
                    inv[z, r, :] = weight
                else:
                    rim = robin[z, r, :]
                    weight = inv[z, r, :]
                fixed = base[z, r, :] + flows[z] + rim * va[z, mid, :]
                base[z, r, :] = fixed
                vb[z, mid, :] = (fixed + part[z, r, :]) * weight

        def second_tile(t):
            r = rows_of(t)
            got = gather(vb, t, lambda z: base[z, r, :])
            for z, value in enumerate(got):
                va[z, rows_of(t + 1), :] = value * inv[z, r, :]

        def mix_sent(t):
            mixed[0, rows_of(t), :] = mix(va[:, rows_of(t + 1), :])

        group = 2
        count = tiles // group

        def work(step, mix_at, second_at, first_at):
            of = lambda g: [] if g is None else [g * group + i for i in range(group)]
            for t in of(mix_at):
                mix_sent(t)
            sides = [(t, sides_of(step, t)) for t in of(first_at)]
            for t in of(second_at):
                second_tile(t)
            for t, got in sides:
                first_tile(step, t, got)

        def sweeps(step, before_ends):
            for g in range(3):
                work(step, None, None, g)
            work(step, None, 1, 3)

            def body(g, carry):
                work(step, g - 1, g, g + 2)
                return carry

            lax.fori_loop(2, count - 2, body, 0)
            work(step, count - 3, count - 2, None)
            before_ends()
            work(step, count - 2, count - 1, None)
            work(step, count - 1, 0, None)

        def residual_tile(t, carry):
            r = rows_of(t)
            mid = rows_of(t + 1)
            for z, value in enumerate(
                gather(va, t, lambda z: src_ref[z, r, :] - diag[z, r, :] * va[z, mid, :])
            ):
                res_ref[z, r, :] = value
            return carry

        for step in range(ITERS):
            spread_pressure(base, step, 2 if step == 0 else 0)

            def before_ends(step=step):
                if step == 0:
                    return
                arrive(step, xy_dirs)
                for sx, row in ((-1, 0), (1, cx - 1)):
                    more = corner(step, 0, sx)
                    base[:, row, :] += more
                    vb[:, 8 + row, :] += more * inv[:, row, :]

            sweeps(step, before_ends)
            xs, ys = stages[step + 1][:2]
            for side, x in ((0, 8), (1, top - 1)):
                xs[side, 0] = va[:, x, :]
            start(step + 1, xy_dirs + x_dirs + zx_dirs)
            work(step, 0, None, None)
            unweave(0, ys)
            start(step + 1, y_dirs + zy_dirs + z_dirs)
            if step == ITERS - 1:
                lax.fori_loop(0, tiles, residual_tile, 0, unroll=4)
            else:
                lax.fori_loop(0, tiles, lambda t, c: inside_tile(step + 1, t, c), 0, unroll=4)
            if step == 0:
                sent(step)
            sent(step + 1)
            arrive(step + 1, z_dirs)
            early_pressure(res_ref if step == ITERS - 1 else base, step + 1, 0)
            arrive(step + 1, late)
        spread_pressure(res_ref, ITERS, 0)
        arrive(ITERS, xy_dirs)
        for sx, row in ((-1, 0), (1, cx - 1)):
            res_ref[:, row, :] += corner(ITERS, 0, sx)
        turn_ref[...] = turn[1]

    return kernel


def write_out(pressure, residual, turned, out_hbm, res_hbm, sem):
    cz, cx, cy = residual.shape
    put_out = pltpu.make_async_copy(pressure.at[:, pl.ds(8, cx), :], out_hbm, sem.at[0])
    put_out.start()
    lane = lax.broadcasted_iota(jnp.int32, (8, LANES), 1)
    ends = jnp.logical_or(lane == 0, lane == LANES - 1)

    def tile(t, carry):
        r = pl.ds(pl.multiple_of(t * 8, 8), 8)
        side = turned[r, :]
        for z in range(cz):
            residual[z, r, :] += jnp.where(ends, pltpu.roll(side, LANES - 1 - 2 * z, 1), 0.0)
        return carry

    lax.fori_loop(0, cx // 8, tile, 0, unroll=8)
    put_res = pltpu.make_async_copy(residual, res_hbm, sem.at[1])
    put_res.start()
    put_out.wait()
    put_res.wait()


def solution(mesh):
    sizes = tuple(mesh.shape[a] for a in AXES)

    def per_device(rock_ids, log_perm, rock_diagonal, rock_shear, rock_storage, source, pressure_start):
        shape = rock_ids.shape
        cz, cx, cy = shape
        classes = rock_storage.shape[0]
        f32 = jnp.float32
        padded = (cz, cx + 24, cy)
        groups = directions(z_kinds(sizes[0]))
        many = [max(len(group), 1) for group in groups]
        faces = many[5]

        def exchange(nq):
            return [
                pltpu.VMEM((2, nq, cz, cy), f32),
                pltpu.VMEM((2, nq, cz, cx), f32),
                pltpu.VMEM((many[0], cz, cy), f32),
                pltpu.VMEM((many[1], nq, cz, cx), f32),
                pltpu.VMEM((many[2], nq, cz, cy), f32),
                pltpu.VMEM((many[3], nq, 1, cx), f32),
                pltpu.VMEM((many[4], nq, 1, cy), f32),
                pltpu.VMEM((faces, nq, cx, cy), f32),
            ]

        hbm = pl.BlockSpec(memory_space=pltpu.HBM)
        vmem = pl.BlockSpec(memory_space=pltpu.VMEM)
        count = sum(len(group) for group in groups)
        kept = pl.pallas_call(
            make_kernel(sizes, shape, classes),
            out_shape=(pltpu.VMEM(padded, f32), pltpu.VMEM(shape, f32), pltpu.VMEM((cx, cy), f32)),
            in_specs=[hbm] * 7,
            out_specs=(vmem, vmem, vmem),
            scratch_shapes=[
                pltpu.VMEM((7, -(-classes // 8) * 8, cy), f32),
                pltpu.VMEM((6,) + padded, f32),
                pltpu.VMEM((3, cz, cx + 8, cy), f32),
                pltpu.VMEM((3, cz, cx + 8, cy), f32),
                pltpu.VMEM((cz, cx + 8, cy), f32),
                pltpu.VMEM((cz, cx + 8, cy), f32),
                pltpu.VMEM(padded, f32),
                pltpu.VMEM((len(OFFSETS), cz, cx + 8, cy), f32),
            ]
            + [pltpu.VMEM((cz, cx + 8, cy), f32)] * 5
            + [
                pltpu.VMEM((3, cx, cy), f32),
                pltpu.VMEM((cx, cy), f32),
                pltpu.VMEM((2, cx, cy), f32),
                pltpu.VMEM((cx + 16, cy), f32),
                pltpu.VMEM((2, 5, cz, cy), f32),
                pltpu.VMEM((5, 2 * cz, cx), f32),
                pltpu.VMEM((faces, 5, cx, cy), f32),
                pltpu.VMEM((faces, 2, cy), f32),
                pltpu.VMEM((faces, 2, cx), f32),
                pltpu.VMEM((faces, 3, cx, cy), f32),
                pltpu.VMEM((2, cz, cy), f32),
                pltpu.VMEM((2, 2 * cz, cx), f32),
                pltpu.VMEM((3, 2 * cz, cx), f32),
                pltpu.VMEM((5, 2 * cz, cx), f32),
            ]
            + exchange(3)
            + exchange(1)
            + exchange(1)
            + [pltpu.VMEM((3, classes), f32)] * 2
            + [pltpu.VMEM((1, classes), f32)]
            + [pltpu.VMEM(shape, jnp.int32)]
            + [pltpu.VMEM(shape, f32)] * 2
            + [
                pltpu.SemaphoreType.DMA((7,)),
                pltpu.SemaphoreType.DMA((ITERS + 1, count)),
                pltpu.SemaphoreType.DMA((ITERS + 1, count)),
            ],
            compiler_params=pltpu.CompilerParams(
                collective_id=0, has_side_effects=True, vmem_limit_bytes=61440 * 1024
            ),
            name="schwarz",
        )(rock_ids, log_perm, rock_diagonal.T, rock_shear.T, rock_storage.reshape(1, classes), source, pressure_start)
        return pl.pallas_call(
            write_out,
            out_shape=(jax.ShapeDtypeStruct(shape, f32), jax.ShapeDtypeStruct(shape, f32)),
            in_specs=[vmem, vmem, vmem],
            out_specs=(hbm, hbm),
            scratch_shapes=[pltpu.SemaphoreType.DMA((2,))],
            name="write_out",
        )(*(pltpu.with_memory_space_constraint(k, pltpu.VMEM) for k in kept))

    block = P("gz", "gx", "gy")
    return jax.shard_map(
        per_device,
        mesh=mesh,
        in_specs=(block, block, P(), P(), P(), block, block),
        out_specs=(block, block),
        check_vma=False,
    )
```

```python
import jax
import jax.numpy as jnp
from jax import lax
from jax.experimental import pallas as pl
from jax.experimental.pallas import tpu as pltpu
from jax.sharding import PartitionSpec as P

ITERS = 2
SWEEPS = 2
ROBIN = 0.5
AXES = ("gz", "gx", "gy")
LANES = 128
FACE = 2.0
EDGE = 0.125


def build_offsets():
    found = []
    for axis in range(3):
        for sign in (1, -1):
            vector = [0, 0, 0]
            vector[axis] = sign
            found.append((tuple(vector), axis, 1))
    for first, second, comp in ((0, 1, 3), (0, 2, 4), (1, 2, 5)):
        for sign_a in (1, -1):
            for sign_b in (1, -1):
                vector = [0, 0, 0]
                vector[first] = sign_a
                vector[second] = sign_b
                found.append((tuple(vector), comp, sign_a * sign_b))
    return found


OFFSETS = build_offsets()


def z_kinds(blocks):
    if blocks < 2:
        return ()
    return ("other",) if blocks == 2 else (1, -1)


def directions(kinds):
    xy_dirs = [(0, dx, dy) for dx in (1, -1) for dy in (1, -1)]
    x_dirs = [(0, dx, 0) for dx in (1, -1)]
    y_dirs = [(0, 0, dy) for dy in (1, -1)]
    zx_dirs = [(k + 1, dx, 0) for k in range(len(kinds)) for dx in (1, -1)]
    zy_dirs = [(k + 1, 0, dy) for k in range(len(kinds)) for dy in (1, -1)]
    z_dirs = [(k + 1, 0, 0) for k in range(len(kinds))]
    return xy_dirs, y_dirs, x_dirs, zy_dirs, zx_dirs, z_dirs


def make_kernel(sizes, shape, classes):
    cz, cx, cy = shape
    tiles = cx // 8
    top = cx + 8
    last = cz - 1
    kinds = z_kinds(sizes[0])
    groups = directions(kinds)
    xy_dirs, y_dirs, x_dirs, zy_dirs, zx_dirs, z_dirs = groups
    dirs = [d for group in groups for d in group]
    slot = {d: i for i, d in enumerate(dirs)}
    place = {d: i for group in groups for i, d in enumerate(group)}

    def opposite(d):
        k = d[0]
        if k and len(kinds) == 2:
            k = 3 - k
        return (k, -d[1], -d[2])

    def kernel(
        ids_hbm, lp_hbm, dia_hbm, she_hbm, sto_hbm, src_hbm, p_hbm,
        va, res_ref, turn_ref,
        tab, ten, tup, tdn, dup, ddn, vb,
        coef, diag, robin, inv, base, part, mixed, pack, turn, zpad,
        rcx, rcy, rcz, rzx, rzy,
        zs1, xc1, yfull, tall, woven,
        xs1, ys1, xyl1, yl1, xl1, zyl1, zxl1, zl1,
        xs2, ys2, xyl2, yl2, xl2, zyl2, zxl2, zl2,
        xs3, ys3, xyl3, yl3, xl3, zyl3, zxl3, zl3,
        dia_ref, she_ref, sto_ref, ids_ref, lp_ref, src_ref, load_sem,
        send_sem, recv_sem,
    ):
        whole = pl.ds(8, cx)
        loads = [
            pltpu.make_async_copy(a, b, load_sem.at[i])
            for i, (a, b) in enumerate(
                (
                    (ids_hbm, ids_ref), (lp_hbm, lp_ref), (p_hbm, va.at[:, whole, :]), (src_hbm, src_ref),
                    (dia_hbm, dia_ref), (she_hbm, she_ref), (sto_hbm, sto_ref),
                )
            )
        ]
        here = [lax.axis_index(a) for a in AXES]
        if len(kinds) == 1:
            steps = [(1 - 2 * here[0], last * (1 - here[0]), last * here[0])]
        else:
            steps = [(k, last if k == 1 else 0, 0 if k == 1 else last) for k in kinds]

        ends_z = [(0, last), [s[2] for s in steps], ()][len(kinds)]

        def exists(d):
            ok = None
            terms = []
            if d[0] and len(kinds) == 2:
                terms.append(here[0] < sizes[0] - 1 if kinds[d[0] - 1] == 1 else here[0] > 0)
            for axis in (1, 2):
                if d[axis] == 1:
                    terms.append(here[axis] < sizes[axis] - 1)
                elif d[axis] == -1:
                    terms.append(here[axis] > 0)
            for term in terms:
                ok = term if ok is None else jnp.logical_and(ok, term)
            return ok

        there = {d: exists(d) for d in dirs}

        def when(ok):
            if ok is None:
                return lambda f: f()
            return pl.when(ok)

        def target(d):
            out = {AXES[i]: here[i] + d[i] for i in (1, 2) if d[i] != 0}
            if d[0]:
                out[AXES[0]] = here[0] + steps[d[0] - 1][0]
            return out

        barrier = pltpu.get_barrier_semaphore()

        expected = jnp.int32(0)
        for d in dirs:
            @when(there[d])
            def _(d=d):
                pl.semaphore_signal(
                    barrier, inc=1, device_id=target(d),
                    device_id_type=pl.DeviceIdType.MESH,
                )
            expected = expected + (1 if there[d] is None else there[d].astype(jnp.int32))

        for load in loads[4:] + loads[:4]:
            load.start()

        stages = (
            (xs1, ys1, xyl1, yl1, xl1, zyl1, zxl1, zl1),
            (xs2, ys2, xyl2, yl2, xl2, zyl2, zxl2, zl2),
            (xs3, ys3, xyl3, yl3, xl3, zyl3, zxl3, zl3),
        )

        def land(stage, d):
            kind = [d in group for group in groups].index(True)
            return stages[stage][2 + kind].at[place[d]]

        for d in dirs:
            if there[opposite(d)] is None:
                continue

            @pl.when(jnp.logical_not(there[opposite(d)]))
            def _(d=d):
                for stage in range(ITERS + 1):
                    ref = land(stage, d)
                    ref[...] = jnp.zeros_like(ref)

        lane = lax.broadcasted_iota(jnp.int32, (cx, LANES), 1)
        lane_t = lax.broadcasted_iota(jnp.int32, (8, LANES), 1)

        def copy_of(stage, d):
            xs, ys = stages[stage][:2]
            x_side, y_side = (d[1] + 1) // 2, (d[2] + 1) // 2
            face = pl.ds(steps[d[0] - 1][1], 1) if d[0] else None
            if d[1] and d[2]:
                src = xc1.at[x_side] if stage == 0 else xs.at[x_side, 0]
            elif d[1]:
                src = xs.at[x_side, :, face, :] if d[0] else xs.at[x_side]
            elif d[2]:
                src = ys.at[y_side, :, face, :] if d[0] else ys.at[y_side]
            else:
                src = zs1.at[d[0] - 1] if stage == 0 else va.at[face, whole, :]
            dst = land(stage, d)
            return pltpu.make_async_remote_copy(
                src_ref=src, dst_ref=dst,
                send_sem=send_sem.at[stage, slot[d]],
                recv_sem=recv_sem.at[stage, slot[d]],
                device_id=target(d), device_id_type=pl.DeviceIdType.MESH,
            )

        def start(stage, some):
            for d in some:
                @when(there[d])
                def _(d=d):
                    copy_of(stage, d).start()

        def arrive(stage, some):
            for d in some:
                @when(there[opposite(d)])
                def _(d=d):
                    copy_of(stage, d).wait_recv()

        def sent(stage):
            for d in dirs:
                @when(there[d])
                def _(d=d):
                    copy_of(stage, d).wait_send()

        def getters(stage, q):
            def got(d):
                return land(stage, opposite(d))

            def get_z(k):
                return got((k + 1, 0, 0))[q]

            def get_x(sx):
                return got((0, sx, 0))[q]

            def get_y(sy):
                return got((0, 0, sy))[q]

            def get_zx(k, sx):
                return got((k + 1, sx, 0))[q]

            def get_zy(k, sy):
                return got((k + 1, 0, sy))[q]

            def get_xy(sx, sy):
                if sy == 1:
                    shift = LANES - 2 - 2 * q if stage == 0 else LANES - 1
                else:
                    shift = (LANES - 2 * q) % LANES if stage == 0 else 1
                held = got((0, sx, sy))[...]
                return pltpu.roll(held, shift, 1) if shift else held

            return get_z, get_x, get_y, get_zx, get_zy, get_xy

        lane_x = lax.broadcasted_iota(jnp.int32, (cz, LANES), 1)
        sub_x = lax.broadcasted_iota(jnp.int32, (cz, LANES), 0)
        lane_y = lax.broadcasted_iota(jnp.int32, (2 * cz, LANES), 1)
        sub_y = lax.broadcasted_iota(jnp.int32, (2 * cz, LANES), 0)
        even = sub_y % 2 == 0
        zero = jnp.float32(0)

        def near_x(get, sx, names, corners=True):
            plain = get[1](sx)
            out = [plain]
            if "z" in names:
                out.append(jnp.where(sub_x < last, pltpu.roll(plain, cz - 1, 0), zero))
                out.append(jnp.where(sub_x > 0, pltpu.roll(plain, 1, 0), zero))
            if "y" in names:
                ahead, behind = pltpu.roll(plain, LANES - 1, 1), pltpu.roll(plain, 1, 1)
                out.append(jnp.where(lane_x == LANES - 1, get[5](sx, 1) if corners else zero, ahead))
                out.append(jnp.where(lane_x == 0, get[5](sx, -1) if corners else zero, behind))
            return out

        def near_y(get, names, at):
            get_y = get[2]
            woven[at, pl.ds(0, cz, 2), :] = get_y(1)
            woven[at, pl.ds(1, cz, 2), :] = get_y(-1)
            plain = woven[at]
            out = [plain]
            if "z" in names:
                out.append(jnp.where(sub_y < 2 * last, pltpu.roll(plain, 2 * cz - 2, 0), zero))
                out.append(jnp.where(sub_y >= 2, pltpu.roll(plain, 2, 0), zero))
            if "x" in names:
                ahead, behind = pltpu.roll(plain, LANES - 1, 1), pltpu.roll(plain, 1, 1)
                out.append(jnp.where(lane_y < LANES - 1, ahead, zero))
                out.append(jnp.where(lane_y > 0, behind, zero))
            return out

        row = lax.broadcasted_iota(jnp.int32, (cx, LANES), 0)

        def near_z(plain, names):
            out = [plain]
            if "x" in names:
                zpad[8:top, :] = plain
                out.append(zpad[9 : top + 1, :])
                out.append(zpad[7 : top - 1, :])
            if "y" in names:
                out.append(pltpu.roll(plain, LANES - 1, 1))
                out.append(pltpu.roll(plain, 1, 1))
            return out

        def harmonic(own, near):
            return own * near / (own + near)

        def rows_of(t):
            return pl.ds(pl.multiple_of(t * 8, 8), 8)

        ends = jnp.logical_or(lane_t == 0, lane_t == LANES - 1)

        def at_ends(ref, r, z):
            return jnp.where(ends, pltpu.roll(ref[r, :], LANES - 1 - 2 * z, 1), zero)

        def add_x(dest, of_x):
            for sx, at in ((-1, 0), (1, cx - 1)):
                dest[:, at, :] += of_x(sx)

        def add_plane(dest, k, value):
            dest[pl.ds(steps[k][1], 1), 0:cx, :] += value[None]

        def add_row(dest, k, at, value):
            dest[pl.ds(steps[k][1], 1), at : at + 1, :] += value[None]

        def mix(planes):
            out = None
            for z in range(cz):
                moved = pltpu.roll(planes[z], 2 * z + 1, 1)
                out = moved if out is None else jnp.where((lane_t // 2) == z, moved, out)
            return out

        pack[...] = jnp.zeros_like(pack)
        zpad[0:8, :] = jnp.zeros((8, LANES), jnp.float32)
        zpad[top : top + 8, :] = jnp.zeros((8, LANES), jnp.float32)
        for ref in (va, vb):
            for lo in (0, top):
                ref[:, lo : lo + 8, :] = jnp.zeros((cz, 8, LANES), jnp.float32)
        for lo in (0, top):
            ten[:, :, lo : lo + 8, :] = jnp.zeros((6, cz, 8, LANES), jnp.float32)

        def code_of(ids):
            return (ids + 1).astype(jnp.float32)

        for load in loads[:3]:
            load.wait()

        for k in range(len(kinds)):
            face = pl.ds(steps[k][1], 1)
            zs1[k, 0:1] = code_of(ids_ref[face])
            zs1[k, 1:2] = lp_ref[face]
            zs1[k, 2:3] = va[face, whole, :]
        for side, x in ((0, 0), (1, cx - 1)):
            xs1[side, 0] = code_of(ids_ref[:, x, :])
            xs1[side, 1] = lp_ref[:, x, :]
            xs1[side, 2] = va[:, 8 + x, :]

        def mix_tile(t, carry):
            r = rows_of(t)
            mixed[0, r, :] = mix(code_of(ids_ref[:, r, :]))
            mixed[1, r, :] = mix(lp_ref[:, r, :])
            mixed[2, r, :] = mix(va[:, rows_of(t + 1), :])
            return carry

        def unweave(q, ys):
            tall[q] = mixed[q].T[: 2 * cz]
            ys[1, q] = tall[q, pl.ds(0, cz, 2), :]
            ys[0, q] = tall[q, pl.ds(1, cz, 2), :]

        lax.fori_loop(0, tiles, mix_tile, 0, unroll=4)
        for q in range(3):
            unweave(q, ys1)
        for q in range(2):
            yfull[q] = tall[q]
        for side in range(2):
            held = None
            for q in range(3):
                moved = pltpu.roll(xs1[side, q], 2 * q + 1, 1)
                held = moved if held is None else jnp.where((lane_x // 2) == q, moved, held)
            xc1[side] = held

        pl.semaphore_wait(barrier, expected)
        start(0, dirs)

        for load in loads[4:]:
            load.wait()
        high = tab.shape[1]
        on_class = lax.broadcasted_iota(jnp.int32, (high, classes), 0) == lax.broadcasted_iota(
            jnp.int32, (high, classes), 1
        )

        def down(values):
            spread = jnp.where(on_class, jnp.broadcast_to(values, (high, classes)), zero)
            return jnp.broadcast_to(jnp.sum(spread, axis=1, keepdims=True), (high, LANES))

        cols = [down(dia_ref[k : k + 1, :]) for k in range(3)]
        for k, (a, b) in enumerate(((0, 1), (0, 2), (1, 2))):
            tab[3 + k] = EDGE * down(she_ref[k : k + 1, :]) * jnp.sqrt(cols[a] * cols[b])
        for k in range(3):
            tab[k] = FACE * cols[k]
        tab[6] = down(sto_ref[...])


        def pick(ids, comps):
            count = ids.shape[0]
            if count < 8:
                ids = jnp.concatenate([ids] * (8 // count), axis=0)
            found = []
            for k in comps:
                parts = []
                for at in range(0, ids.shape[0], 8):
                    some = ids[at : at + 8]
                    if classes <= 8:
                        part_ = jnp.take_along_axis(tab[k], some, axis=0, mode="promise_in_bounds")
                    else:
                        part_ = jnp.zeros(some.shape, jnp.float32)
                        for c in range(classes):
                            part_ = jnp.where(some == c, tab[k, c : c + 1, :], part_)
                    parts.append(part_)
                got = parts[0] if len(parts) == 1 else jnp.concatenate(parts, axis=0)
                found.append(got[:count])
            return found

        def tensors(code, perm, comps):
            ids = jnp.clip(code - 1.0, 0.0, classes - 1.0).astype(jnp.int32)
            gain = jnp.where(code > 0.5, jnp.exp(perm), zero)
            return [f * gain for f in pick(ids, comps)]

        turned_of = (2, 4, 5)

        def tensor_tile(t, carry):
            r = rows_of(t)
            out = rows_of(t + 1)
            for z in range(cz):
                gain = jnp.exp(lp_ref[z, r, :])
                found = pick(ids_ref[z, r, :], range(7))
                diag[z, r, :] = found[6]
                for k in range(6):
                    value = found[k] * gain
                    ten[k, z, out, :] = value
                    if k in turned_of:
                        at = turned_of.index(k)
                        tup[at, z, r, :] = pltpu.roll(value, 1, 1)
                        tdn[at, z, r, :] = pltpu.roll(value, LANES - 1, 1)
            return carry

        lax.fori_loop(0, tiles, tensor_tile, 0, unroll=2)

        row_t = lax.broadcasted_iota(jnp.int32, (8, LANES), 0)

        def coef_tile(t, carry):
            r = rows_of(t)
            mid = rows_of(t + 1)
            row = {0: mid, 1: pl.ds(t * 8 + 9, 8), -1: pl.ds(t * 8 + 7, 8)}
            x_out = {1: row_t + t * 8 == cx - 1, -1: row_t + t * 8 == 0}
            y_out = {1: lane_t == 0, -1: lane_t == LANES - 1}
            xy_out = {(dx, dy): jnp.logical_or(x_out[dx], y_out[dy]) for dx in (1, -1) for dy in (1, -1)}
            for z in range(cz):
                own = {}
                for comp in range(6):
                    own[comp, 0] = ten[comp, z, mid, :]
                    if comp in turned_of:
                        own[comp, 1] = tup[turned_of.index(comp), z, r, :]
                        own[comp, -1] = tdn[turned_of.index(comp), z, r, :]
                total = {0: diag[z, r, :], 1: None, -1: None}
                for e, ((dz, dx, dy), comp, sign) in enumerate(OFFSETS):
                    if not 0 <= z + dz < cz:
                        continue
                    near = ten[comp, z + dz, row[dx], :]
                    if comp < 3:
                        value = harmonic(own[comp, dy], near)
                    else:
                        value = own[comp, dy] + near
                    if dx and dy:
                        value = jnp.where(xy_out[dx, dy], zero, value)
                    elif dx and dz:
                        value = jnp.where(x_out[dx], zero, value)
                    elif dy:
                        value = jnp.where(y_out[dy], zero, value)
                    coef[e, z, r, :] = value
                    size = value if comp < 3 else jnp.abs(value)
                    total[dy] = size if total[dy] is None else total[dy] + size
                diag[z, r, :] = total[0]
                dup[z, r, :] = total[1]
                ddn[z, r, :] = total[-1]
                robin[z, r, :] = jnp.zeros((8, LANES), jnp.float32)
            return carry

        lax.fori_loop(0, tiles, coef_tile, 0, unroll=2)

        def gather(ref, t, first):
            r = rows_of(t)
            row = {0: rows_of(t + 1), 1: pl.ds(t * 8 + 9, 8), -1: pl.ds(t * 8 + 7, 8)}
            near = {dx: ref[:, row[dx], :] for dx in (0, 1, -1)}
            out = []
            for z in range(cz):
                acc = {0: first(z), 1: None, -1: None}
                for e, ((dz, dx, dy), comp, sign) in enumerate(OFFSETS):
                    if not 0 <= z + dz < cz:
                        continue
                    term = coef[e, z, r, :] * near[dx][z + dz]
                    if acc[dy] is None:
                        acc[dy] = term if sign == 1 else -term
                    else:
                        acc[dy] = acc[dy] + term if sign == 1 else acc[dy] - term
                out.append(acc[0] + (pltpu.roll(acc[1], LANES - 1, 1) + pltpu.roll(acc[-1], 1, 1)))
            return out

        for plane in ends_z:
            own = [jnp.abs(ten[c, pl.ds(plane, 1), 8:top, :]) for c in (3, 4)]
            robin[pl.ds(plane, 1), 0:cx, :] += 2.0 * (own[0] + own[1])

        loads[3].wait()

        def inside_tile(step, t, carry):
            r = rows_of(t)
            if step == 0:
                for z in range(cz):
                    diag[z, r, :] += pltpu.roll(dup[z, r, :], LANES - 1, 1) + pltpu.roll(ddn[z, r, :], 1, 1)
            for z, value in enumerate(gather(va, t, lambda z: None)):
                part[z, r, :] = value
            base[:, r, :] = src_ref[:, r, :]
            return carry

        lax.fori_loop(0, tiles, lambda t, c: inside_tile(0, t, c), 0, unroll=4)

        rest = [d for d in dirs if d not in z_dirs]
        late = [d for d in rest if d not in xy_dirs]
        signs = [jnp.float32(p[0]) if isinstance(p[0], int) else p[0].astype(jnp.float32) for p in steps]

        def weigh(weights, values):
            out = None
            for j, value in enumerate(values):
                term = weights(j) * value
                out = term if out is None else out + term
            return out

        def early_pressure(dest, stage, q):
            get_z = getters(stage, q)[0]
            for k in range(len(kinds)):
                add_plane(dest, k, weigh(lambda j: rcz[k, j], near_z(get_z(k), "xy")))

        arrive(0, z_dirs)
        for k in range(len(kinds)):
            face = steps[k][1]
            own = {c: ten[c, pl.ds(face, 1), 8:top, :][0] for c in (0, 3, 4)}
            there_z = dict(zip((0, 3, 4), tensors(getters(0, 0)[0](k), getters(0, 1)[0](k), (0, 3, 4))))
            values = [harmonic(own[0], there_z[0])]
            near = near_z(there_z[3], "x")
            for dx, got, out in ((1, near[1], row == cx - 1), (-1, near[2], row == 0)):
                values.append(jnp.where(out, zero, (signs[k] * dx) * (own[3] + got)))
            near = near_z(there_z[4], "y")
            for dy, got, out in ((1, near[1], lane == LANES - 1), (-1, near[2], lane == 0)):
                values.append(jnp.where(out, zero, (signs[k] * dy) * (own[4] + got)))
            size = None
            for j, value in enumerate(values):
                rcz[k, j] = value
                size = jnp.abs(value) if size is None else size + jnp.abs(value)
            add_plane(robin, k, size)
        early_pressure(base, 0, 2)
        arrive(0, rest)

        gid = getters(0, 0)
        glp = getters(0, 1)

        def tensor_get(k):
            def of(which):
                def get(*args):
                    return tensors(gid[which](*args), glp[which](*args), [k])[0]
                return get
            return tuple(of(i) for i in range(6))

        gets = {k: tensor_get(k) for k in range(6)}
        rim_x = {}
        for side, sx in ((0, -1), (1, 1)):
            row = 8 if sx == -1 else top - 1
            own = {k: ten[k, :, row, :] for k in (1, 3, 5)}
            values = [harmonic(own[1], near_x(gets[1], sx, "")[0])]
            near = near_x(gets[3], sx, "z")
            for dz, got, ok in ((1, near[1], sub_x < last), (-1, near[2], sub_x > 0)):
                values.append(jnp.where(ok, (dz * sx) * (own[3] + got), zero))
            near = near_x(gets[5], sx, "y")
            for dy, got in ((1, near[1]), (-1, near[2])):
                values.append((sx * dy) * (own[5] + got))
            size = None
            for j, value in enumerate(values):
                rcx[side, j] = value
                size = jnp.abs(value) if size is None else size + jnp.abs(value)
            rim_x[sx] = size

        own = dict(zip((2, 4, 5), tensors(yfull[0], yfull[1], (2, 4, 5))))
        sy = jnp.where(even, jnp.float32(1), jnp.float32(-1))
        values = [harmonic(own[2], near_y(gets[2], "", 0)[0])]
        near = near_y(gets[4], "z", 1)
        for dz, got, ok in ((1, near[1], sub_y < 2 * last), (-1, near[2], sub_y >= 2)):
            values.append(jnp.where(ok, dz * sy * (own[4] + got), zero))
        near = near_y(gets[5], "x", 2)
        for dx, got, ok in ((1, near[1], lane_y < LANES - 1), (-1, near[2], lane_y > 0)):
            values.append(jnp.where(ok, dx * sy * (own[5] + got), zero))
        size = None
        for j, value in enumerate(values):
            rcy[j] = value
            size = jnp.abs(value) if size is None else size + jnp.abs(value)
        pack[0 : 2 * cz, :] = size
        woven[4] = own[4]
        for k in range(len(kinds)):
            face = pl.ds(2 * steps[k][1], 2)
            for at, sy_, code_row in ((0, 1, gets[4][4](k, 1)), (1, -1, gets[4][4](k, -1))):
                value = (signs[k] * sy_) * (woven[4, pl.ds(2 * steps[k][1] + at, 1), :] + code_row)
                rzy[k, at : at + 1, :] = value
                pack[pl.ds(2 * steps[k][1] + at, 1), :] += jnp.abs(value)
            for side, sx, at in ((0, -1, 0), (1, 1, cx - 1)):
                mine = ten[3, pl.ds(steps[k][1], 1), 8 + at : 9 + at, :][0]
                value = (signs[k] * sx) * (mine + gets[3][3](k, sx))
                rzx[k, side : side + 1, :] = value
                add_row(robin, k, at, jnp.abs(value))
        turn[0] = pack[...].T
        add_x(robin, lambda sx: rim_x[sx])

        def corner(stage, q, sx):
            get, side = getters(stage, q), (sx + 1) // 2
            return rcx[side, 3] * jnp.where(lane_x == LANES - 1, get[5](sx, 1), zero) + rcx[
                side, 4
            ] * jnp.where(lane_x == 0, get[5](sx, -1), zero)

        def spread_pressure(dest, stage, q):
            get = getters(stage, q)
            pack[0 : 2 * cz, :] = weigh(lambda j: rcy[j], near_y(get, "zx", 3))
            for k in range(len(kinds)):
                for at, sy_ in ((0, 1), (1, -1)):
                    pack[pl.ds(2 * steps[k][1] + at, 1), :] += rzy[k, at : at + 1, :] * get[4](k, sy_)
            turn[1] = pack[...].T
            for k in range(len(kinds)):
                for side, sx, at in ((0, -1, 0), (1, 1, cx - 1)):
                    add_row(dest, k, at, rzx[k, side : side + 1, :] * get[3](k, sx))
            add_x(dest, lambda sx: weigh(lambda j: rcx[(sx + 1) // 2, j], near_x(get, sx, "zy", stage == 0)))

        def sides_of(step, t):
            r = rows_of(t)
            rims = [at_ends(turn.at[0], r, z) for z in range(cz)] if step == 0 else None
            return rims, [at_ends(turn.at[1], r, z) for z in range(cz)]

        def first_tile(step, t, sides):
            r = rows_of(t)
            mid = rows_of(t + 1)
            rims, flows = sides
            for z in range(cz):
                if step == 0:
                    rim = robin[z, r, :] + rims[z]
                    total = diag[z, r, :] + rim
                    rim = ROBIN * rim
                    weight = 1.0 / (total + rim)
                    diag[z, r, :] = total
                    robin[z, r, :] = rim
                    inv[z, r, :] = weight
                else:
                    rim = robin[z, r, :]
                    weight = inv[z, r, :]
                fixed = base[z, r, :] + flows[z] + rim * va[z, mid, :]
                base[z, r, :] = fixed
                vb[z, mid, :] = (fixed + part[z, r, :]) * weight

        def second_tile(t):
            r = rows_of(t)
            got = gather(vb, t, lambda z: base[z, r, :])
            for z, value in enumerate(got):
                va[z, rows_of(t + 1), :] = value * inv[z, r, :]

        def mix_sent(t):
            mixed[0, rows_of(t), :] = mix(va[:, rows_of(t + 1), :])

        group = 2
        count = tiles // group

        def work(step, mix_at, second_at, first_at):
            of = lambda g: [] if g is None else [g * group + i for i in range(group)]
            for t in of(mix_at):
                mix_sent(t)
            sides = [(t, sides_of(step, t)) for t in of(first_at)]
            for t in of(second_at):
                second_tile(t)
            for t, got in sides:
                first_tile(step, t, got)

        def sweeps(step, before_ends):
            for g in range(3):
                work(step, None, None, g)
            work(step, None, 1, 3)

            def body(g, carry):
                work(step, g - 1, g, g + 2)
                return carry

            lax.fori_loop(2, count - 2, body, 0, unroll=4)
            work(step, count - 3, count - 2, None)
            before_ends()
            work(step, count - 2, count - 1, None)
            work(step, count - 1, 0, None)

        def residual_tile(t, carry):
            r = rows_of(t)
            mid = rows_of(t + 1)
            for z, value in enumerate(
                gather(va, t, lambda z: src_ref[z, r, :] - diag[z, r, :] * va[z, mid, :])
            ):
                res_ref[z, r, :] = value
            return carry

        for step in range(ITERS):
            spread_pressure(base, step, 2 if step == 0 else 0)

            def before_ends(step=step):
                if step == 0:
                    return
                arrive(step, xy_dirs)
                for sx, row in ((-1, 0), (1, cx - 1)):
                    more = corner(step, 0, sx)
                    base[:, row, :] += more
                    vb[:, 8 + row, :] += more * inv[:, row, :]

            sweeps(step, before_ends)
            xs, ys = stages[step + 1][:2]
            for side, x in ((0, 8), (1, top - 1)):
                xs[side, 0] = va[:, x, :]
            start(step + 1, xy_dirs + x_dirs + zx_dirs)
            work(step, 0, None, None)
            unweave(0, ys)
            start(step + 1, y_dirs + zy_dirs + z_dirs)
            if step == ITERS - 1:
                lax.fori_loop(0, tiles, residual_tile, 0, unroll=4)
            else:
                lax.fori_loop(0, tiles, lambda t, c: inside_tile(step + 1, t, c), 0, unroll=4)
            if step == 0:
                sent(step)
            sent(step + 1)
            arrive(step + 1, z_dirs)
            early_pressure(res_ref if step == ITERS - 1 else base, step + 1, 0)
            arrive(step + 1, late)
        spread_pressure(res_ref, ITERS, 0)
        arrive(ITERS, xy_dirs)
        for sx, row in ((-1, 0), (1, cx - 1)):
            res_ref[:, row, :] += corner(ITERS, 0, sx)
        turn_ref[...] = turn[1]

    return kernel


def write_out(pressure, residual, turned, out_hbm, res_hbm, sem):
    cz, cx, cy = residual.shape
    put_out = pltpu.make_async_copy(pressure.at[:, pl.ds(8, cx), :], out_hbm, sem.at[0])
    put_out.start()
    lane = lax.broadcasted_iota(jnp.int32, (8, LANES), 1)
    ends = jnp.logical_or(lane == 0, lane == LANES - 1)

    def tile(t, carry):
        r = pl.ds(pl.multiple_of(t * 8, 8), 8)
        side = turned[r, :]
        for z in range(cz):
            residual[z, r, :] += jnp.where(ends, pltpu.roll(side, LANES - 1 - 2 * z, 1), 0.0)
        return carry

    lax.fori_loop(0, cx // 8, tile, 0, unroll=8)
    put_res = pltpu.make_async_copy(residual, res_hbm, sem.at[1])
    put_res.start()
    put_out.wait()
    put_res.wait()


def solution(mesh):
    sizes = tuple(mesh.shape[a] for a in AXES)

    def per_device(rock_ids, log_perm, rock_diagonal, rock_shear, rock_storage, source, pressure_start):
        shape = rock_ids.shape
        cz, cx, cy = shape
        classes = rock_storage.shape[0]
        f32 = jnp.float32
        padded = (cz, cx + 24, cy)
        groups = directions(z_kinds(sizes[0]))
        many = [max(len(group), 1) for group in groups]
        faces = many[5]

        def exchange(nq):
            return [
                pltpu.VMEM((2, nq, cz, cy), f32),
                pltpu.VMEM((2, nq, cz, cx), f32),
                pltpu.VMEM((many[0], cz, cy), f32),
                pltpu.VMEM((many[1], nq, cz, cx), f32),
                pltpu.VMEM((many[2], nq, cz, cy), f32),
                pltpu.VMEM((many[3], nq, 1, cx), f32),
                pltpu.VMEM((many[4], nq, 1, cy), f32),
                pltpu.VMEM((faces, nq, cx, cy), f32),
            ]

        hbm = pl.BlockSpec(memory_space=pltpu.HBM)
        vmem = pl.BlockSpec(memory_space=pltpu.VMEM)
        count = sum(len(group) for group in groups)
        kept = pl.pallas_call(
            make_kernel(sizes, shape, classes),
            out_shape=(pltpu.VMEM(padded, f32), pltpu.VMEM(shape, f32), pltpu.VMEM((cx, cy), f32)),
            in_specs=[hbm] * 7,
            out_specs=(vmem, vmem, vmem),
            scratch_shapes=[
                pltpu.VMEM((7, -(-classes // 8) * 8, cy), f32),
                pltpu.VMEM((6,) + padded, f32),
                pltpu.VMEM((3, cz, cx + 8, cy), f32),
                pltpu.VMEM((3, cz, cx + 8, cy), f32),
                pltpu.VMEM((cz, cx + 8, cy), f32),
                pltpu.VMEM((cz, cx + 8, cy), f32),
                pltpu.VMEM(padded, f32),
                pltpu.VMEM((len(OFFSETS), cz, cx + 8, cy), f32),
            ]
            + [pltpu.VMEM((cz, cx + 8, cy), f32)] * 5
            + [
                pltpu.VMEM((3, cx, cy), f32),
                pltpu.VMEM((cx, cy), f32),
                pltpu.VMEM((2, cx, cy), f32),
                pltpu.VMEM((cx + 16, cy), f32),
                pltpu.VMEM((2, 5, cz, cy), f32),
                pltpu.VMEM((5, 2 * cz, cx), f32),
                pltpu.VMEM((faces, 5, cx, cy), f32),
                pltpu.VMEM((faces, 2, cy), f32),
                pltpu.VMEM((faces, 2, cx), f32),
                pltpu.VMEM((faces, 3, cx, cy), f32),
                pltpu.VMEM((2, cz, cy), f32),
                pltpu.VMEM((2, 2 * cz, cx), f32),
                pltpu.VMEM((3, 2 * cz, cx), f32),
                pltpu.VMEM((5, 2 * cz, cx), f32),
            ]
            + exchange(3)
            + exchange(1)
            + exchange(1)
            + [pltpu.VMEM((3, classes), f32)] * 2
            + [pltpu.VMEM((1, classes), f32)]
            + [pltpu.VMEM(shape, jnp.int32)]
            + [pltpu.VMEM(shape, f32)] * 2
            + [
                pltpu.SemaphoreType.DMA((7,)),
                pltpu.SemaphoreType.DMA((ITERS + 1, count)),
                pltpu.SemaphoreType.DMA((ITERS + 1, count)),
            ],
            compiler_params=pltpu.CompilerParams(
                collective_id=0, has_side_effects=True, vmem_limit_bytes=61440 * 1024
            ),
            name="schwarz",
        )(rock_ids, log_perm, rock_diagonal.T, rock_shear.T, rock_storage.reshape(1, classes), source, pressure_start)
        return pl.pallas_call(
            write_out,
            out_shape=(jax.ShapeDtypeStruct(shape, f32), jax.ShapeDtypeStruct(shape, f32)),
            in_specs=[vmem, vmem, vmem],
            out_specs=(hbm, hbm),
            scratch_shapes=[pltpu.SemaphoreType.DMA((2,))],
            name="write_out",
        )(*(pltpu.with_memory_space_constraint(k, pltpu.VMEM) for k in kept))

    block = P("gz", "gx", "gy")
    return jax.shard_map(
        per_device,
        mesh=mesh,
        in_specs=(block, block, P(), P(), P(), block, block),
        out_specs=(block, block),
        check_vma=False,
    )
```

```python
import jax
import jax.numpy as jnp
from jax import lax
from jax.experimental import pallas as pl
from jax.experimental.pallas import tpu as pltpu
from jax.sharding import PartitionSpec as P

ITERS = 2
SWEEPS = 2
ROBIN = 0.5
AXES = ("gz", "gx", "gy")
LANES = 128
FACE = 2.0
EDGE = 0.125


def build_offsets():
    found = []
    for axis in range(3):
        for sign in (1, -1):
            vector = [0, 0, 0]
            vector[axis] = sign
            found.append((tuple(vector), axis, 1))
    for first, second, comp in ((0, 1, 3), (0, 2, 4), (1, 2, 5)):
        for sign_a in (1, -1):
            for sign_b in (1, -1):
                vector = [0, 0, 0]
                vector[first] = sign_a
                vector[second] = sign_b
                found.append((tuple(vector), comp, sign_a * sign_b))
    return found


OFFSETS = build_offsets()


def z_kinds(blocks):
    if blocks < 2:
        return ()
    return ("other",) if blocks == 2 else (1, -1)


def directions(kinds):
    xy_dirs = [(0, dx, dy) for dx in (1, -1) for dy in (1, -1)]
    x_dirs = [(0, dx, 0) for dx in (1, -1)]
    y_dirs = [(0, 0, dy) for dy in (1, -1)]
    zx_dirs = [(k + 1, dx, 0) for k in range(len(kinds)) for dx in (1, -1)]
    zy_dirs = [(k + 1, 0, dy) for k in range(len(kinds)) for dy in (1, -1)]
    z_dirs = [(k + 1, 0, 0) for k in range(len(kinds))]
    return xy_dirs, y_dirs, x_dirs, zy_dirs, zx_dirs, z_dirs


def make_kernel(sizes, shape, classes):
    cz, cx, cy = shape
    tiles = cx // 8
    top = cx + 8
    last = cz - 1
    kinds = z_kinds(sizes[0])
    groups = directions(kinds)
    xy_dirs, y_dirs, x_dirs, zy_dirs, zx_dirs, z_dirs = groups
    dirs = [d for group in groups for d in group]
    slot = {d: i for i, d in enumerate(dirs)}
    place = {d: i for group in groups for i, d in enumerate(group)}

    def opposite(d):
        k = d[0]
        if k and len(kinds) == 2:
            k = 3 - k
        return (k, -d[1], -d[2])

    def kernel(
        ids_hbm, lp_hbm, dia_hbm, she_hbm, sto_hbm, src_hbm, p_hbm,
        va, res_ref, turn_ref,
        tab, ten, tup, tdn, dup, ddn, vb,
        coef, diag, robin, inv, base, part, mixed, pack, turn, zpad,
        rcx, rcy, rcz, rzx, rzy,
        zs1, xc1, yfull, tall, woven,
        xs1, ys1, xyl1, yl1, xl1, zyl1, zxl1, zl1,
        xs2, ys2, xyl2, yl2, xl2, zyl2, zxl2, zl2,
        xs3, ys3, xyl3, yl3, xl3, zyl3, zxl3, zl3,
        dia_ref, she_ref, sto_ref, ids_ref, lp_ref, src_ref, load_sem,
        send_sem, recv_sem,
    ):
        whole = pl.ds(8, cx)
        loads = [
            pltpu.make_async_copy(a, b, load_sem.at[i])
            for i, (a, b) in enumerate(
                (
                    (ids_hbm, ids_ref), (lp_hbm, lp_ref), (p_hbm, va.at[:, whole, :]), (src_hbm, src_ref),
                    (dia_hbm, dia_ref), (she_hbm, she_ref), (sto_hbm, sto_ref),
                )
            )
        ]
        here = [lax.axis_index(a) for a in AXES]
        if len(kinds) == 1:
            steps = [(1 - 2 * here[0], last * (1 - here[0]), last * here[0])]
        else:
            steps = [(k, last if k == 1 else 0, 0 if k == 1 else last) for k in kinds]

        ends_z = [(0, last), [s[2] for s in steps], ()][len(kinds)]

        def exists(d):
            ok = None
            terms = []
            if d[0] and len(kinds) == 2:
                terms.append(here[0] < sizes[0] - 1 if kinds[d[0] - 1] == 1 else here[0] > 0)
            for axis in (1, 2):
                if d[axis] == 1:
                    terms.append(here[axis] < sizes[axis] - 1)
                elif d[axis] == -1:
                    terms.append(here[axis] > 0)
            for term in terms:
                ok = term if ok is None else jnp.logical_and(ok, term)
            return ok

        there = {d: exists(d) for d in dirs}

        def when(ok):
            if ok is None:
                return lambda f: f()
            return pl.when(ok)

        def target(d):
            out = {AXES[i]: here[i] + d[i] for i in (1, 2) if d[i] != 0}
            if d[0]:
                out[AXES[0]] = here[0] + steps[d[0] - 1][0]
            return out

        barrier = pltpu.get_barrier_semaphore()

        expected = jnp.int32(0)
        for d in dirs:
            @when(there[d])
            def _(d=d):
                pl.semaphore_signal(
                    barrier, inc=1, device_id=target(d),
                    device_id_type=pl.DeviceIdType.MESH,
                )
            expected = expected + (1 if there[d] is None else there[d].astype(jnp.int32))

        for load in loads[4:] + loads[:4]:
            load.start()

        stages = (
            (xs1, ys1, xyl1, yl1, xl1, zyl1, zxl1, zl1),
            (xs2, ys2, xyl2, yl2, xl2, zyl2, zxl2, zl2),
            (xs3, ys3, xyl3, yl3, xl3, zyl3, zxl3, zl3),
        )

        def land(stage, d):
            kind = [d in group for group in groups].index(True)
            return stages[stage][2 + kind].at[place[d]]

        for d in dirs:
            if there[opposite(d)] is None:
                continue

            @pl.when(jnp.logical_not(there[opposite(d)]))
            def _(d=d):
                for stage in range(ITERS + 1):
                    ref = land(stage, d)
                    ref[...] = jnp.zeros_like(ref)

        lane = lax.broadcasted_iota(jnp.int32, (cx, LANES), 1)
        lane_t = lax.broadcasted_iota(jnp.int32, (8, LANES), 1)

        def copy_of(stage, d):
            xs, ys = stages[stage][:2]
            x_side, y_side = (d[1] + 1) // 2, (d[2] + 1) // 2
            face = pl.ds(steps[d[0] - 1][1], 1) if d[0] else None
            if d[1] and d[2]:
                src = xc1.at[x_side] if stage == 0 else xs.at[x_side, 0]
            elif d[1]:
                src = xs.at[x_side, :, face, :] if d[0] else xs.at[x_side]
            elif d[2]:
                src = ys.at[y_side, :, face, :] if d[0] else ys.at[y_side]
            else:
                src = zs1.at[d[0] - 1] if stage == 0 else va.at[face, whole, :]
            dst = land(stage, d)
            return pltpu.make_async_remote_copy(
                src_ref=src, dst_ref=dst,
                send_sem=send_sem.at[stage, slot[d]],
                recv_sem=recv_sem.at[stage, slot[d]],
                device_id=target(d), device_id_type=pl.DeviceIdType.MESH,
            )

        def start(stage, some):
            for d in some:
                @when(there[d])
                def _(d=d):
                    copy_of(stage, d).start()

        def arrive(stage, some):
            for d in some:
                @when(there[opposite(d)])
                def _(d=d):
                    copy_of(stage, d).wait_recv()

        def sent(stage):
            for d in dirs:
                @when(there[d])
                def _(d=d):
                    copy_of(stage, d).wait_send()

        def getters(stage, q):
            def got(d):
                return land(stage, opposite(d))

            def get_z(k):
                return got((k + 1, 0, 0))[q]

            def get_x(sx):
                return got((0, sx, 0))[q]

            def get_y(sy):
                return got((0, 0, sy))[q]

            def get_zx(k, sx):
                return got((k + 1, sx, 0))[q]

            def get_zy(k, sy):
                return got((k + 1, 0, sy))[q]

            def get_xy(sx, sy):
                if sy == 1:
                    shift = LANES - 2 - 2 * q if stage == 0 else LANES - 1
                else:
                    shift = (LANES - 2 * q) % LANES if stage == 0 else 1
                held = got((0, sx, sy))[...]
                return pltpu.roll(held, shift, 1) if shift else held

            return get_z, get_x, get_y, get_zx, get_zy, get_xy

        lane_x = lax.broadcasted_iota(jnp.int32, (cz, LANES), 1)
        sub_x = lax.broadcasted_iota(jnp.int32, (cz, LANES), 0)
        lane_y = lax.broadcasted_iota(jnp.int32, (2 * cz, LANES), 1)
        sub_y = lax.broadcasted_iota(jnp.int32, (2 * cz, LANES), 0)
        even = sub_y % 2 == 0
        zero = jnp.float32(0)

        def near_x(get, sx, names, corners=True):
            plain = get[1](sx)
            out = [plain]
            if "z" in names:
                out.append(jnp.where(sub_x < last, pltpu.roll(plain, cz - 1, 0), zero))
                out.append(jnp.where(sub_x > 0, pltpu.roll(plain, 1, 0), zero))
            if "y" in names:
                ahead, behind = pltpu.roll(plain, LANES - 1, 1), pltpu.roll(plain, 1, 1)
                out.append(jnp.where(lane_x == LANES - 1, get[5](sx, 1) if corners else zero, ahead))
                out.append(jnp.where(lane_x == 0, get[5](sx, -1) if corners else zero, behind))
            return out

        def near_y(get, names, at):
            get_y = get[2]
            woven[at, pl.ds(0, cz, 2), :] = get_y(1)
            woven[at, pl.ds(1, cz, 2), :] = get_y(-1)
            plain = woven[at]
            out = [plain]
            if "z" in names:
                out.append(jnp.where(sub_y < 2 * last, pltpu.roll(plain, 2 * cz - 2, 0), zero))
                out.append(jnp.where(sub_y >= 2, pltpu.roll(plain, 2, 0), zero))
            if "x" in names:
                ahead, behind = pltpu.roll(plain, LANES - 1, 1), pltpu.roll(plain, 1, 1)
                out.append(jnp.where(lane_y < LANES - 1, ahead, zero))
                out.append(jnp.where(lane_y > 0, behind, zero))
            return out

        row = lax.broadcasted_iota(jnp.int32, (cx, LANES), 0)

        def near_z(plain, names):
            out = [plain]
            if "x" in names:
                zpad[8:top, :] = plain
                out.append(zpad[9 : top + 1, :])
                out.append(zpad[7 : top - 1, :])
            if "y" in names:
                out.append(pltpu.roll(plain, LANES - 1, 1))
                out.append(pltpu.roll(plain, 1, 1))
            return out

        def harmonic(own, near):
            return own * near / (own + near)

        def rows_of(t):
            return pl.ds(pl.multiple_of(t * 8, 8), 8)

        ends = jnp.logical_or(lane_t == 0, lane_t == LANES - 1)

        def at_ends(ref, r, z):
            return jnp.where(ends, pltpu.roll(ref[r, :], LANES - 1 - 2 * z, 1), zero)

        def add_x(dest, of_x):
            for sx, at in ((-1, 0), (1, cx - 1)):
                dest[:, at, :] += of_x(sx)

        def add_plane(dest, k, value):
            dest[pl.ds(steps[k][1], 1), 0:cx, :] += value[None]

        def add_row(dest, k, at, value):
            dest[pl.ds(steps[k][1], 1), at : at + 1, :] += value[None]

        def mix(planes):
            out = None
            for z in range(cz):
                moved = pltpu.roll(planes[z], 2 * z + 1, 1)
                out = moved if out is None else jnp.where((lane_t // 2) == z, moved, out)
            return out

        pack[...] = jnp.zeros_like(pack)
        zpad[0:8, :] = jnp.zeros((8, LANES), jnp.float32)
        zpad[top : top + 8, :] = jnp.zeros((8, LANES), jnp.float32)
        for ref in (va, vb):
            for lo in (0, top):
                ref[:, lo : lo + 8, :] = jnp.zeros((cz, 8, LANES), jnp.float32)
        for lo in (0, top):
            ten[:, :, lo : lo + 8, :] = jnp.zeros((6, cz, 8, LANES), jnp.float32)

        def code_of(ids):
            return (ids + 1).astype(jnp.float32)

        for load in loads[:3]:
            load.wait()

        for k in range(len(kinds)):
            face = pl.ds(steps[k][1], 1)
            zs1[k, 0:1] = code_of(ids_ref[face])
            zs1[k, 1:2] = lp_ref[face]
            zs1[k, 2:3] = va[face, whole, :]
        for side, x in ((0, 0), (1, cx - 1)):
            xs1[side, 0] = code_of(ids_ref[:, x, :])
            xs1[side, 1] = lp_ref[:, x, :]
            xs1[side, 2] = va[:, 8 + x, :]

        def mix_tile(t, carry):
            r = rows_of(t)
            mixed[0, r, :] = mix(code_of(ids_ref[:, r, :]))
            mixed[1, r, :] = mix(lp_ref[:, r, :])
            mixed[2, r, :] = mix(va[:, rows_of(t + 1), :])
            return carry

        def unweave(q, ys):
            tall[q] = mixed[q].T[: 2 * cz]
            ys[1, q] = tall[q, pl.ds(0, cz, 2), :]
            ys[0, q] = tall[q, pl.ds(1, cz, 2), :]

        lax.fori_loop(0, tiles, mix_tile, 0, unroll=4)
        for q in range(3):
            unweave(q, ys1)
        for q in range(2):
            yfull[q] = tall[q]
        for side in range(2):
            held = None
            for q in range(3):
                moved = pltpu.roll(xs1[side, q], 2 * q + 1, 1)
                held = moved if held is None else jnp.where((lane_x // 2) == q, moved, held)
            xc1[side] = held

        pl.semaphore_wait(barrier, expected)
        start(0, dirs)

        for load in loads[4:]:
            load.wait()
        high = tab.shape[1]
        on_class = lax.broadcasted_iota(jnp.int32, (high, classes), 0) == lax.broadcasted_iota(
            jnp.int32, (high, classes), 1
        )

        def down(values):
            spread = jnp.where(on_class, jnp.broadcast_to(values, (high, classes)), zero)
            return jnp.broadcast_to(jnp.sum(spread, axis=1, keepdims=True), (high, LANES))

        cols = [down(dia_ref[k : k + 1, :]) for k in range(3)]
        for k, (a, b) in enumerate(((0, 1), (0, 2), (1, 2))):
            tab[3 + k] = EDGE * down(she_ref[k : k + 1, :]) * jnp.sqrt(cols[a] * cols[b])
        for k in range(3):
            tab[k] = FACE * cols[k]
        tab[6] = down(sto_ref[...])


        def pick(ids, comps):
            count = ids.shape[0]
            if count < 8:
                ids = jnp.concatenate([ids] * (8 // count), axis=0)
            found = []
            for k in comps:
                parts = []
                for at in range(0, ids.shape[0], 8):
                    some = ids[at : at + 8]
                    if classes <= 8:
                        part_ = jnp.take_along_axis(tab[k], some, axis=0, mode="promise_in_bounds")
                    else:
                        part_ = jnp.zeros(some.shape, jnp.float32)
                        for c in range(classes):
                            part_ = jnp.where(some == c, tab[k, c : c + 1, :], part_)
                    parts.append(part_)
                got = parts[0] if len(parts) == 1 else jnp.concatenate(parts, axis=0)
                found.append(got[:count])
            return found

        def tensors(code, perm, comps):
            ids = jnp.clip(code - 1.0, 0.0, classes - 1.0).astype(jnp.int32)
            gain = jnp.where(code > 0.5, jnp.exp(perm), zero)
            return [f * gain for f in pick(ids, comps)]

        turned_of = (2, 4, 5)

        def tensor_tile(t, carry):
            r = rows_of(t)
            out = rows_of(t + 1)
            for z in range(cz):
                gain = jnp.exp(lp_ref[z, r, :])
                found = pick(ids_ref[z, r, :], range(7))
                diag[z, r, :] = found[6]
                for k in range(6):
                    value = found[k] * gain
                    ten[k, z, out, :] = value
                    if k in turned_of:
                        at = turned_of.index(k)
                        tup[at, z, r, :] = pltpu.roll(value, 1, 1)
                        tdn[at, z, r, :] = pltpu.roll(value, LANES - 1, 1)
            return carry

        lax.fori_loop(0, tiles, tensor_tile, 0, unroll=2)

        row_t = lax.broadcasted_iota(jnp.int32, (8, LANES), 0)

        def coef_tile(t, carry):
            r = rows_of(t)
            mid = rows_of(t + 1)
            row = {0: mid, 1: pl.ds(t * 8 + 9, 8), -1: pl.ds(t * 8 + 7, 8)}
            x_out = {1: row_t + t * 8 == cx - 1, -1: row_t + t * 8 == 0}
            y_out = {1: lane_t == 0, -1: lane_t == LANES - 1}
            xy_out = {(dx, dy): jnp.logical_or(x_out[dx], y_out[dy]) for dx in (1, -1) for dy in (1, -1)}
            for z in range(cz):
                own = {}
                for comp in range(6):
                    own[comp, 0] = ten[comp, z, mid, :]
                    if comp in turned_of:
                        own[comp, 1] = tup[turned_of.index(comp), z, r, :]
                        own[comp, -1] = tdn[turned_of.index(comp), z, r, :]
                total = {0: diag[z, r, :], 1: None, -1: None}
                for e, ((dz, dx, dy), comp, sign) in enumerate(OFFSETS):
                    if not 0 <= z + dz < cz:
                        continue
                    near = ten[comp, z + dz, row[dx], :]
                    if comp < 3:
                        value = harmonic(own[comp, dy], near)
                    else:
                        value = own[comp, dy] + near
                    if dx and dy:
                        value = jnp.where(xy_out[dx, dy], zero, value)
                    elif dx and dz:
                        value = jnp.where(x_out[dx], zero, value)
                    elif dy:
                        value = jnp.where(y_out[dy], zero, value)
                    coef[e, z, r, :] = value
                    size = value if comp < 3 else jnp.abs(value)
                    total[dy] = size if total[dy] is None else total[dy] + size
                diag[z, r, :] = total[0]
                dup[z, r, :] = total[1]
                ddn[z, r, :] = total[-1]
                robin[z, r, :] = jnp.zeros((8, LANES), jnp.float32)
            return carry

        lax.fori_loop(0, tiles, coef_tile, 0, unroll=2)

        def gather(ref, t, first):
            r = rows_of(t)
            row = {0: rows_of(t + 1), 1: pl.ds(t * 8 + 9, 8), -1: pl.ds(t * 8 + 7, 8)}
            near = {dx: ref[:, row[dx], :] for dx in (0, 1, -1)}
            out = []
            for z in range(cz):
                acc = {0: first(z), 1: None, -1: None}
                for e, ((dz, dx, dy), comp, sign) in enumerate(OFFSETS):
                    if not 0 <= z + dz < cz:
                        continue
                    term = coef[e, z, r, :] * near[dx][z + dz]
                    if acc[dy] is None:
                        acc[dy] = term if sign == 1 else -term
                    else:
                        acc[dy] = acc[dy] + term if sign == 1 else acc[dy] - term
                out.append(acc[0] + (pltpu.roll(acc[1], LANES - 1, 1) + pltpu.roll(acc[-1], 1, 1)))
            return out

        for plane in ends_z:
            own = [jnp.abs(ten[c, pl.ds(plane, 1), 8:top, :]) for c in (3, 4)]
            robin[pl.ds(plane, 1), 0:cx, :] += 2.0 * (own[0] + own[1])

        loads[3].wait()

        def inside_tile(step, t, carry):
            r = rows_of(t)
            if step == 0:
                for z in range(cz):
                    diag[z, r, :] += pltpu.roll(dup[z, r, :], LANES - 1, 1) + pltpu.roll(ddn[z, r, :], 1, 1)
            for z, value in enumerate(gather(va, t, lambda z: None)):
                part[z, r, :] = value
            base[:, r, :] = src_ref[:, r, :]
            return carry

        lax.fori_loop(0, tiles, lambda t, c: inside_tile(0, t, c), 0, unroll=4)

        rest = [d for d in dirs if d not in z_dirs]
        late = [d for d in rest if d not in xy_dirs]
        signs = [jnp.float32(p[0]) if isinstance(p[0], int) else p[0].astype(jnp.float32) for p in steps]

        def weigh(weights, values):
            out = None
            for j, value in enumerate(values):
                term = weights(j) * value
                out = term if out is None else out + term
            return out

        def early_pressure(dest, stage, q):
            get_z = getters(stage, q)[0]
            for k in range(len(kinds)):
                add_plane(dest, k, weigh(lambda j: rcz[k, j], near_z(get_z(k), "xy")))

        arrive(0, z_dirs)
        for k in range(len(kinds)):
            face = steps[k][1]
            own = {c: ten[c, pl.ds(face, 1), 8:top, :][0] for c in (0, 3, 4)}
            there_z = dict(zip((0, 3, 4), tensors(getters(0, 0)[0](k), getters(0, 1)[0](k), (0, 3, 4))))
            values = [harmonic(own[0], there_z[0])]
            near = near_z(there_z[3], "x")
            for dx, got, out in ((1, near[1], row == cx - 1), (-1, near[2], row == 0)):
                values.append(jnp.where(out, zero, (signs[k] * dx) * (own[3] + got)))
            near = near_z(there_z[4], "y")
            for dy, got, out in ((1, near[1], lane == LANES - 1), (-1, near[2], lane == 0)):
                values.append(jnp.where(out, zero, (signs[k] * dy) * (own[4] + got)))
            size = None
            for j, value in enumerate(values):
                rcz[k, j] = value
                size = jnp.abs(value) if size is None else size + jnp.abs(value)
            add_plane(robin, k, size)
        early_pressure(base, 0, 2)
        arrive(0, rest)

        gid = getters(0, 0)
        glp = getters(0, 1)

        def tensor_get(k):
            def of(which):
                def get(*args):
                    return tensors(gid[which](*args), glp[which](*args), [k])[0]
                return get
            return tuple(of(i) for i in range(6))

        gets = {k: tensor_get(k) for k in range(6)}
        rim_x = {}
        for side, sx in ((0, -1), (1, 1)):
            row = 8 if sx == -1 else top - 1
            own = {k: ten[k, :, row, :] for k in (1, 3, 5)}
            values = [harmonic(own[1], near_x(gets[1], sx, "")[0])]
            near = near_x(gets[3], sx, "z")
            for dz, got, ok in ((1, near[1], sub_x < last), (-1, near[2], sub_x > 0)):
                values.append(jnp.where(ok, (dz * sx) * (own[3] + got), zero))
            near = near_x(gets[5], sx, "y")
            for dy, got in ((1, near[1]), (-1, near[2])):
                values.append((sx * dy) * (own[5] + got))
            size = None
            for j, value in enumerate(values):
                rcx[side, j] = value
                size = jnp.abs(value) if size is None else size + jnp.abs(value)
            rim_x[sx] = size

        own = dict(zip((2, 4, 5), tensors(yfull[0], yfull[1], (2, 4, 5))))
        sy = jnp.where(even, jnp.float32(1), jnp.float32(-1))
        values = [harmonic(own[2], near_y(gets[2], "", 0)[0])]
        near = near_y(gets[4], "z", 1)
        for dz, got, ok in ((1, near[1], sub_y < 2 * last), (-1, near[2], sub_y >= 2)):
            values.append(jnp.where(ok, dz * sy * (own[4] + got), zero))
        near = near_y(gets[5], "x", 2)
        for dx, got, ok in ((1, near[1], lane_y < LANES - 1), (-1, near[2], lane_y > 0)):
            values.append(jnp.where(ok, dx * sy * (own[5] + got), zero))
        size = None
        for j, value in enumerate(values):
            rcy[j] = value
            size = jnp.abs(value) if size is None else size + jnp.abs(value)
        pack[0 : 2 * cz, :] = size
        woven[4] = own[4]
        for k in range(len(kinds)):
            face = pl.ds(2 * steps[k][1], 2)
            for at, sy_, code_row in ((0, 1, gets[4][4](k, 1)), (1, -1, gets[4][4](k, -1))):
                value = (signs[k] * sy_) * (woven[4, pl.ds(2 * steps[k][1] + at, 1), :] + code_row)
                rzy[k, at : at + 1, :] = value
                pack[pl.ds(2 * steps[k][1] + at, 1), :] += jnp.abs(value)
            for side, sx, at in ((0, -1, 0), (1, 1, cx - 1)):
                mine = ten[3, pl.ds(steps[k][1], 1), 8 + at : 9 + at, :][0]
                value = (signs[k] * sx) * (mine + gets[3][3](k, sx))
                rzx[k, side : side + 1, :] = value
                add_row(robin, k, at, jnp.abs(value))
        turn[0] = pack[...].T
        add_x(robin, lambda sx: rim_x[sx])

        def corner(stage, q, sx):
            get, side = getters(stage, q), (sx + 1) // 2
            return rcx[side, 3] * jnp.where(lane_x == LANES - 1, get[5](sx, 1), zero) + rcx[
                side, 4
            ] * jnp.where(lane_x == 0, get[5](sx, -1), zero)

        def spread_pressure(dest, stage, q):
            get = getters(stage, q)
            pack[0 : 2 * cz, :] = weigh(lambda j: rcy[j], near_y(get, "zx", 3))
            for k in range(len(kinds)):
                for at, sy_ in ((0, 1), (1, -1)):
                    pack[pl.ds(2 * steps[k][1] + at, 1), :] += rzy[k, at : at + 1, :] * get[4](k, sy_)
            turn[1] = pack[...].T
            for k in range(len(kinds)):
                for side, sx, at in ((0, -1, 0), (1, 1, cx - 1)):
                    add_row(dest, k, at, rzx[k, side : side + 1, :] * get[3](k, sx))
            add_x(dest, lambda sx: weigh(lambda j: rcx[(sx + 1) // 2, j], near_x(get, sx, "zy", stage == 0)))

        def sides_of(step, t):
            r = rows_of(t)
            rims = [at_ends(turn.at[0], r, z) for z in range(cz)] if step == 0 else None
            return rims, [at_ends(turn.at[1], r, z) for z in range(cz)]

        def first_tile(step, t, sides):
            r = rows_of(t)
            mid = rows_of(t + 1)
            rims, flows = sides
            for z in range(cz):
                if step == 0:
                    rim = robin[z, r, :] + rims[z]
                    total = diag[z, r, :] + rim
                    rim = ROBIN * rim
                    weight = 1.0 / (total + rim)
                    diag[z, r, :] = total
                    robin[z, r, :] = rim
                    inv[z, r, :] = weight
                else:
                    rim = robin[z, r, :]
                    weight = inv[z, r, :]
                fixed = base[z, r, :] + flows[z] + rim * va[z, mid, :]
                base[z, r, :] = fixed
                vb[z, mid, :] = (fixed + part[z, r, :]) * weight

        def second_tile(t):
            r = rows_of(t)
            got = gather(vb, t, lambda z: base[z, r, :])
            for z, value in enumerate(got):
                va[z, rows_of(t + 1), :] = value * inv[z, r, :]

        def mix_sent(t):
            mixed[0, rows_of(t), :] = mix(va[:, rows_of(t + 1), :])

        group = 4
        count = tiles // group

        def work(step, mix_at, second_at, first_at):
            of = lambda g: [] if g is None else [g * group + i for i in range(group)]
            for t in of(mix_at):
                mix_sent(t)
            sides = [(t, sides_of(step, t)) for t in of(first_at)]
            for t in of(second_at):
                second_tile(t)
            for t, got in sides:
                first_tile(step, t, got)

        def sweeps(step, before_ends):
            for g in range(3):
                work(step, None, None, g)
            work(step, None, 1, 3)

            def body(g, carry):
                work(step, g - 1, g, g + 2)
                return carry

            if count > 4:
                lax.fori_loop(2, count - 2, body, 0)
            work(step, count - 3, count - 2, None)
            before_ends()
            work(step, count - 2, count - 1, None)
            work(step, count - 1, 0, None)

        def residual_tile(t, carry):
            r = rows_of(t)
            mid = rows_of(t + 1)
            for z, value in enumerate(
                gather(va, t, lambda z: src_ref[z, r, :] - diag[z, r, :] * va[z, mid, :])
            ):
                res_ref[z, r, :] = value
            return carry

        for step in range(ITERS):
            spread_pressure(base, step, 2 if step == 0 else 0)

            def before_ends(step=step):
                if step == 0:
                    return
                arrive(step, xy_dirs)
                for sx, row in ((-1, 0), (1, cx - 1)):
                    more = corner(step, 0, sx)
                    base[:, row, :] += more
                    vb[:, 8 + row, :] += more * inv[:, row, :]

            sweeps(step, before_ends)
            xs, ys = stages[step + 1][:2]
            for side, x in ((0, 8), (1, top - 1)):
                xs[side, 0] = va[:, x, :]
            start(step + 1, xy_dirs + x_dirs + zx_dirs)
            work(step, 0, None, None)
            unweave(0, ys)
            start(step + 1, y_dirs + zy_dirs + z_dirs)
            if step == ITERS - 1:
                lax.fori_loop(0, tiles, residual_tile, 0, unroll=4)
            else:
                lax.fori_loop(0, tiles, lambda t, c: inside_tile(step + 1, t, c), 0, unroll=4)
            if step == 0:
                sent(step)
            sent(step + 1)
            arrive(step + 1, z_dirs)
            early_pressure(res_ref if step == ITERS - 1 else base, step + 1, 0)
            arrive(step + 1, late)
        spread_pressure(res_ref, ITERS, 0)
        arrive(ITERS, xy_dirs)
        for sx, row in ((-1, 0), (1, cx - 1)):
            res_ref[:, row, :] += corner(ITERS, 0, sx)
        turn_ref[...] = turn[1]

    return kernel


def write_out(pressure, residual, turned, out_hbm, res_hbm, sem):
    cz, cx, cy = residual.shape
    put_out = pltpu.make_async_copy(pressure.at[:, pl.ds(8, cx), :], out_hbm, sem.at[0])
    put_out.start()
    lane = lax.broadcasted_iota(jnp.int32, (8, LANES), 1)
    ends = jnp.logical_or(lane == 0, lane == LANES - 1)

    def tile(t, carry):
        r = pl.ds(pl.multiple_of(t * 8, 8), 8)
        side = turned[r, :]
        for z in range(cz):
            residual[z, r, :] += jnp.where(ends, pltpu.roll(side, LANES - 1 - 2 * z, 1), 0.0)
        return carry

    lax.fori_loop(0, cx // 8, tile, 0, unroll=8)
    put_res = pltpu.make_async_copy(residual, res_hbm, sem.at[1])
    put_res.start()
    put_out.wait()
    put_res.wait()


def solution(mesh):
    sizes = tuple(mesh.shape[a] for a in AXES)

    def per_device(rock_ids, log_perm, rock_diagonal, rock_shear, rock_storage, source, pressure_start):
        shape = rock_ids.shape
        cz, cx, cy = shape
        classes = rock_storage.shape[0]
        f32 = jnp.float32
        padded = (cz, cx + 24, cy)
        groups = directions(z_kinds(sizes[0]))
        many = [max(len(group), 1) for group in groups]
        faces = many[5]

        def exchange(nq):
            return [
                pltpu.VMEM((2, nq, cz, cy), f32),
                pltpu.VMEM((2, nq, cz, cx), f32),
                pltpu.VMEM((many[0], cz, cy), f32),
                pltpu.VMEM((many[1], nq, cz, cx), f32),
                pltpu.VMEM((many[2], nq, cz, cy), f32),
                pltpu.VMEM((many[3], nq, 1, cx), f32),
                pltpu.VMEM((many[4], nq, 1, cy), f32),
                pltpu.VMEM((faces, nq, cx, cy), f32),
            ]

        hbm = pl.BlockSpec(memory_space=pltpu.HBM)
        vmem = pl.BlockSpec(memory_space=pltpu.VMEM)
        count = sum(len(group) for group in groups)
        kept = pl.pallas_call(
            make_kernel(sizes, shape, classes),
            out_shape=(pltpu.VMEM(padded, f32), pltpu.VMEM(shape, f32), pltpu.VMEM((cx, cy), f32)),
            in_specs=[hbm] * 7,
            out_specs=(vmem, vmem, vmem),
            scratch_shapes=[
                pltpu.VMEM((7, -(-classes // 8) * 8, cy), f32),
                pltpu.VMEM((6,) + padded, f32),
                pltpu.VMEM((3, cz, cx + 8, cy), f32),
                pltpu.VMEM((3, cz, cx + 8, cy), f32),
                pltpu.VMEM((cz, cx + 8, cy), f32),
                pltpu.VMEM((cz, cx + 8, cy), f32),
                pltpu.VMEM(padded, f32),
                pltpu.VMEM((len(OFFSETS), cz, cx + 8, cy), f32),
            ]
            + [pltpu.VMEM((cz, cx + 8, cy), f32)] * 5
            + [
                pltpu.VMEM((3, cx, cy), f32),
                pltpu.VMEM((cx, cy), f32),
                pltpu.VMEM((2, cx, cy), f32),
                pltpu.VMEM((cx + 16, cy), f32),
                pltpu.VMEM((2, 5, cz, cy), f32),
                pltpu.VMEM((5, 2 * cz, cx), f32),
                pltpu.VMEM((faces, 5, cx, cy), f32),
                pltpu.VMEM((faces, 2, cy), f32),
                pltpu.VMEM((faces, 2, cx), f32),
                pltpu.VMEM((faces, 3, cx, cy), f32),
                pltpu.VMEM((2, cz, cy), f32),
                pltpu.VMEM((2, 2 * cz, cx), f32),
                pltpu.VMEM((3, 2 * cz, cx), f32),
                pltpu.VMEM((5, 2 * cz, cx), f32),
            ]
            + exchange(3)
            + exchange(1)
            + exchange(1)
            + [pltpu.VMEM((3, classes), f32)] * 2
            + [pltpu.VMEM((1, classes), f32)]
            + [pltpu.VMEM(shape, jnp.int32)]
            + [pltpu.VMEM(shape, f32)] * 2
            + [
                pltpu.SemaphoreType.DMA((7,)),
                pltpu.SemaphoreType.DMA((ITERS + 1, count)),
                pltpu.SemaphoreType.DMA((ITERS + 1, count)),
            ],
            compiler_params=pltpu.CompilerParams(
                collective_id=0, has_side_effects=True, vmem_limit_bytes=61440 * 1024
            ),
            name="schwarz",
        )(rock_ids, log_perm, rock_diagonal.T, rock_shear.T, rock_storage.reshape(1, classes), source, pressure_start)
        return pl.pallas_call(
            write_out,
            out_shape=(jax.ShapeDtypeStruct(shape, f32), jax.ShapeDtypeStruct(shape, f32)),
            in_specs=[vmem, vmem, vmem],
            out_specs=(hbm, hbm),
            scratch_shapes=[pltpu.SemaphoreType.DMA((2,))],
            name="write_out",
        )(*(pltpu.with_memory_space_constraint(k, pltpu.VMEM) for k in kept))

    block = P("gz", "gx", "gy")
    return jax.shard_map(
        per_device,
        mesh=mesh,
        in_specs=(block, block, P(), P(), P(), block, block),
        out_specs=(block, block),
        check_vma=False,
    )
```
